32 devices in a mesh: groups: 2 (over y), ctx: 16 (over z, x, core).
Axes of the slice: x: 2, y: 2, z: 4, core: 2. Of those that a mesh axis runs over, the one named last changes fastest.
Arguments:
- tokens_in: bfloat16 [4096, 1024], P(('groups', 'ctx')), parts along dimension 0, may hold values from -6 to 6
- grad_out: bfloat16 [4096, 1024], P(('groups', 'ctx')), parts along dimension 0, may hold values from -6 to 6
- decay_rate: float32 [1024], replicated, as said below
- w_in: float32 [64], replicated, may hold values from -16 to 16
- b_in: float32 [64], replicated, may hold values from -6 to 6
- w_mid: float32 [64, 64], replicated, may hold values from -0.75 to 0.75
- w_out: float32 [64, 1024], replicated, may hold values from -0.75 to 0.75
Outputs:
- grad_tokens: bfloat16 [4096, 1024], P(('groups', 'ctx')), parts along dimension 0
- grad_w_in: float32 [128], P('groups'), parts along dimension 0
- grad_b_in: float32 [128], P('groups'), parts along dimension 0
- grad_w_mid: float32 [128, 64], P('groups'), parts along dimension 0
- grad_w_out: float32 [128, 1024], P('groups'), parts along dimension 0
The draws below stay inside these ranges and needn't reach their ends.
There are 2 independent parts, one for each index of `groups`. The reference program is written for one: setup_inputs(seed, part) draws one part's arguments, and reference() takes and returns one part's arrays. A program takes and returns all parts, laid end to end along the dimension named above; an argument that names none is the same for every part. Nothing has to cross between parts.
Inputs may be any that keep to these rules, and one draw needn't show every extreme that they name: `decay_rate`: every channel's rate is positive.
All inputs are finite; a program needn't handle non-finite values.
Results may differ from the reference program's by a relative error of at most 0.0051.
Values may be sent and summed in bfloat16 or wider, within the bound.
No kernel may reach another device: no remote copies, remote signals or barrier semaphores. Data moves between devices by JAX's collectives and lax.ppermute only.
A program may use at most 64 MiB of HBM per device.

```python
import math
import jax
import jax.numpy as jnp
from jax import lax

C = 1024
MLP_DIM = 64
LENGTH = 2048


def draw_decay_rate(key, part):
    lowest = math.log(0.25 / LENGTH)
    highest = math.log(1.0 / 32.0)
    return jnp.exp(jax.random.uniform(key, (C,), jnp.float32, lowest, highest))


def steps_of(rng, extent, cuts, low, largest):
    def one(dim, parts):
        draws = jax.random.uniform(jax.random.fold_in(jax.random.fold_in(rng, 6), dim), (parts,), jnp.float32, low / len(cuts), largest / len(cuts))
        return jnp.repeat(jnp.exp(draws), extent[dim] // parts).reshape((-1,) + (1,) * (len(extent) - dim - 1))

    level = one(*cuts[0])
    for cut in cuts[1:]:
        level = level * one(*cut)
    return level


def bell_draw(rng, shape, width, most, cuts=(), kind=jnp.bfloat16):
    drawn = jax.random.normal(rng, shape, jnp.float32) * width
    if len(cuts) > 0:
        drawn = steps_of(rng, shape, cuts, -0.22, 0.18) * drawn
    return jnp.clip(drawn, min=-most, max=most).astype(kind)


def setup_inputs(seed: int = 0, part: int = 0) -> dict:
    key_of = jax.random.split(jax.random.key(seed), 8)
    part_keys = jax.random.split(jax.random.fold_in(key_of[7], part), 8)
    tokens_in = bell_draw(part_keys[0], (LENGTH, C), 1.0, 6.0, ((0, 16),))
    grad_out = bell_draw(part_keys[1], (LENGTH, C), 1.0, 6.0, ((0, 16),))
    decay_rate = draw_decay_rate(jax.random.fold_in(key_of[7], 71), part)
    w_in = bell_draw(key_of[3], (MLP_DIM,), 3.0, 16.0, (), jnp.float32)
    b_in = bell_draw(key_of[4], (MLP_DIM,), 1.0, 6.0, (), jnp.float32)
    w_mid = bell_draw(key_of[5], (MLP_DIM, MLP_DIM), MLP_DIM ** -0.5, 0.75, (), jnp.float32)
    w_out = bell_draw(key_of[6], (MLP_DIM, C), MLP_DIM ** -0.5, 0.75, (), jnp.float32)
    return {"tokens_in": tokens_in, "grad_out": grad_out, "decay_rate": decay_rate, "w_in": w_in, "b_in": b_in, "w_mid": w_mid, "w_out": w_out}


HIGHEST = lax.Precision.HIGHEST

def envelope(lag_values, decay_rate, length):
    double = 2.0 * decay_rate
    geometric = 1.0 + 2.0 * jnp.exp(-double) * jnp.expm1(-double * (length - 1)) / jnp.expm1(-double)
    distance = jnp.abs(lag_values).astype(jnp.float32)[..., None]
    live_mask = (lag_values != -length).astype(jnp.float32)[..., None]
    return live_mask * lax.rsqrt(geometric) * jnp.exp(-distance * decay_rate)

def position_mlp(scaled, w_first, w_bias, w_middle, w_last):
    hidden_one = jax.nn.silu(scaled[..., None] * w_first + w_bias)
    hidden_two = jax.nn.silu(jnp.dot(hidden_one, w_middle, precision=HIGHEST))
    return jnp.dot(hidden_two, w_last, precision=HIGHEST)

def reference(tokens_in, grad_out, decay_rate, w_in, b_in, w_mid, w_out):
    length = LENGTH
    padded = 2 * length
    circular = jnp.arange(padded, dtype=jnp.int32)
    lag_values = jnp.where(circular < length, circular, circular - padded).astype(jnp.int32)
    scaled = lag_values.astype(jnp.float32) / length
    weights_env = envelope(lag_values, decay_rate, length)

    def position_net(w_first, w_bias, w_middle, w_last):
        return position_mlp(scaled, w_first, w_bias, w_middle, w_last)
    position, pull_back = jax.vjp(position_net, w_in, b_in, w_mid, w_out)
    kernel = lax.optimization_barrier((position * weights_env).astype(jnp.bfloat16)).astype(jnp.float32)
    block_width = math.gcd(C, 128)
    groups_count = C // block_width

    def split_channels(array):
        return array.reshape(array.shape[0], groups_count, block_width).transpose(1, 0, 2)

    def one_block(pieces):
        token_block, cotan_block, kernel_block = pieces
        token_spec = jnp.fft.rfft(token_block.astype(jnp.float32), n=padded, axis=0)
        cotan_spec = jnp.fft.rfft(cotan_block.astype(jnp.float32), n=padded, axis=0)
        kernel_spec = jnp.fft.rfft(kernel_block, axis=0)
        input_block = jnp.fft.irfft(jnp.conj(kernel_spec) * cotan_spec, n=padded, axis=0)[:length]
        lagged_block = jnp.fft.irfft(cotan_spec * jnp.conj(token_spec), n=padded, axis=0)
        return (input_block, lagged_block)
    input_blocks, lagged_blocks = lax.map(one_block, (split_channels(tokens_in), split_channels(grad_out), split_channels(kernel)))
    input_grad = input_blocks.transpose(1, 0, 2).reshape(length, C)
    lag_grad = lagged_blocks.transpose(1, 0, 2).reshape(padded, C)
    gradients = pull_back(lag_grad * weights_env)
    loss_scale = 1.0 / math.sqrt(length)
    return (input_grad.astype(jnp.bfloat16), gradients[0] * loss_scale, gradients[1] * loss_scale, gradients[2] * loss_scale, gradients[3] * loss_scale)
```

```python
import functools
import math

import jax
import jax.numpy as jnp
import numpy as np
from jax import lax
from jax.experimental import pallas as pl
from jax.experimental.pallas import tpu as pltpu
from jax.sharding import PartitionSpec as P

RADIX = 16
HALF = RADIX // 2
CHUNK = 32
F32 = jnp.float32
BF16 = jnp.bfloat16


def split_pair(value):
    high = value.astype(BF16)
    return high, (value - high.astype(F32)).astype(BF16)


def dot(left, right):
    return jnp.dot(left, right, preferred_element_type=F32)


def dot_three(left, right):
    left_high, left_low = left
    right_high, right_low = right
    return dot(left_high, right_high) + (dot(left_low, right_high) + dot(left_high, right_low))


def dft_tables(padded):
    inner = padded // RADIX
    grid = np.outer(np.arange(inner), np.arange(inner)) % inner
    angles = 2.0 * np.pi * grid / inner
    matrix = np.concatenate([np.cos(angles), np.sin(angles)], axis=0)
    high = matrix.astype(jnp.bfloat16)
    low = (matrix - high.astype(np.float64)).astype(jnp.bfloat16)
    turn = 2.0 * np.pi * np.outer(np.arange(inner), np.arange(RADIX)) / padded
    twiddle = np.zeros((inner, 128), np.float32)
    twiddle[:, :RADIX] = np.cos(turn)
    twiddle[:, RADIX : 2 * RADIX] = np.sin(turn)
    return jnp.asarray(high), jnp.asarray(low), jnp.asarray(twiddle)


def cos_of(index):
    return math.cos(2.0 * math.pi * index / RADIX)


def sin_of(index):
    return math.sin(2.0 * math.pi * index / RADIX)


def spread(x):
    plus = [x[q] + x[q + 4] for q in range(4)]
    minus = [x[q] - x[q + 4] for q in range(4)]
    root = math.sqrt(0.5)
    out = [None] * 9
    even, odd = plus[0] + plus[2], plus[1] + plus[3]
    out[0] = (even + odd, None)
    out[8] = (even - odd, None)
    out[4] = (plus[0] - plus[2], plus[3] - plus[1])
    across, along = root * (minus[1] - minus[3]), root * (minus[1] + minus[3])
    out[2] = (minus[0] + across, -minus[2] - along)
    out[6] = (minus[0] - across, minus[2] - along)
    differ = {q: x[q] - x[8 - q] for q in (1, 2, 3)}
    same = {q: x[q] + x[8 - q] for q in (1, 2, 3)}
    for j in (1, 3):
        real_even = x[0] + cos_of(2 * j) * differ[2]
        real_odd = cos_of(j) * differ[1] + cos_of(3 * j) * differ[3]
        imag_even = sin_of(4 * j) * x[4] + sin_of(2 * j) * same[2]
        imag_odd = sin_of(j) * same[1] + sin_of(3 * j) * same[3]
        out[j] = (real_even + real_odd, -(imag_odd + imag_even))
        out[8 - j] = (real_even - real_odd, imag_even - imag_odd)
    return out


def gather_back(real, imag):
    even, odd = [None] * 8, [None] * 8
    total, differ = real[0] + real[8], real[0] - real[8]
    real_sum, real_dif = real[2] + real[6], real[2] - real[6]
    imag_sum, imag_dif = imag[2] + imag[6], imag[2] - imag[6]
    root = math.sqrt(0.5)
    even[0] = total + real_sum + real[4]
    even[4] = total - real_sum + real[4]
    even[2] = total - imag_dif - real[4]
    even[6] = total + imag_dif - real[4]
    first, second = root * (real_dif - imag_sum), root * (real_dif + imag_sum)
    even[1] = differ + first - imag[4]
    even[5] = differ - first - imag[4]
    even[3] = differ - second + imag[4]
    even[7] = differ + second + imag[4]
    one_sum, one_dif = real[1] + real[7], real[1] - real[7]
    three_sum, three_dif = real[3] + real[5], real[3] - real[5]
    ione_sum, ione_dif = imag[1] + imag[7], imag[1] - imag[7]
    ithree_sum, ithree_dif = imag[3] + imag[5], imag[3] - imag[5]
    odd[0] = one_sum + three_sum
    odd[4] = ithree_dif - ione_dif
    for q in (1, 2, 3):
        if q % 2 == 0:
            cosines = cos_of(q) * one_sum + cos_of(3 * q) * three_sum
            sines = sin_of(q) * ione_dif + sin_of(3 * q) * ithree_dif
        else:
            cosines = cos_of(q) * one_dif + cos_of(3 * q) * three_dif
            sines = sin_of(q) * ione_sum + sin_of(3 * q) * ithree_sum
        odd[q] = cosines - sines
        odd[8 - q] = -cosines - sines
    return even, odd


def residues_to_scratch(load, twiddle, high_ref, low_ref, inner):
    def chunk(step, carry):
        start = pl.multiple_of(step * CHUNK, CHUNK)
        rows = pl.ds(start, CHUNK)
        turn = twiddle[rows, :]
        for j, (real, imag) in enumerate(spread([load(q * inner + start) for q in range(HALF)])):
            if j > 0:
                cosine, sine = turn[:, j : j + 1], turn[:, RADIX + j : RADIX + j + 1]
                if imag is None:
                    real, imag = real * cosine, -real * sine
                else:
                    real, imag = real * cosine + imag * sine, imag * cosine - real * sine
            else:
                imag = jnp.zeros_like(real)
            for part, value in enumerate((real, imag)):
                high, low = split_pair(value)
                high_ref[j, rows, 128 * part : 128 * part + 128] = high
                low_ref[j, rows, 128 * part : 128 * part + 128] = low
        return carry

    lax.fori_loop(0, inner // CHUNK, chunk, 0)


def inner_dft(pair, matrix_high, matrix_low, inner, direction):
    high, low = pair
    product = dot_three((matrix_high[...], matrix_low[...]), (high, low))
    cos_real, cos_imag = product[:inner, :128], product[:inner, 128:]
    sin_real, sin_imag = product[inner:, :128], product[inner:, 128:]
    if direction > 0:
        return cos_real + sin_imag, cos_imag - sin_real
    return cos_real - sin_imag, cos_imag + sin_real


def low_lanes(rows):
    return lax.broadcasted_iota(jnp.int32, (rows, 128), 1) < 64


def swap(value):
    return pltpu.roll(value, 64, 1)


def pack_kernel(tokens, cotan, out):
    for block in range(out.shape[0]):
        lanes = slice(64 * block, 64 * block + 64)
        out[block] = jnp.concatenate([tokens[:, lanes], cotan[:, lanes]], axis=1)


def kernel_spectrum_kernel(
    length, rate, scale, w_first, w_bias, w_mid, w_last, matrix_high, matrix_low, twiddle,
    spectrum, env_out, slope_one, slope_two, one_high, one_low, two_high, two_low,
    taps, high_ref, low_ref,
):
    padded = 2 * length
    inner = padded // RADIX
    low_half = low_lanes(inner)
    mid_pair = split_pair(w_mid[...])
    last_pair = split_pair(w_last[...])

    def block(step, carry):
        start = pl.multiple_of(step * inner, inner)
        rows = pl.ds(start, inner)
        place = start + lax.broadcasted_iota(jnp.int32, (inner, 128), 0)
        lag = jnp.where(low_half, place, place - length)
        scaled = lag.astype(F32) / length
        pre_one = scaled * w_first[...] + w_bias[...]
        gate_one = 1.0 / (1.0 + jnp.exp(-pre_one))
        hidden_one = pre_one * gate_one
        slope_one[rows, :] = gate_one * (1.0 + pre_one * (1.0 - gate_one))
        pre_two = dot_three(split_pair(hidden_one), mid_pair)
        gate_two = 1.0 / (1.0 + jnp.exp(-pre_two))
        hidden_two = pre_two * gate_two
        slope_two[rows, :] = gate_two * (1.0 + pre_two * (1.0 - gate_two))
        position = dot_three(split_pair(hidden_two), last_pair)
        live = jnp.where(lag == -length, 0.0, 1.0)
        env = live * scale[...] * jnp.exp(-jnp.abs(lag).astype(F32) * rate[...])
        taps[rows, :] = (position * env).astype(BF16).astype(F32)
        env_out[rows, 0:128] = jnp.where(low_half, 0.0, swap(env))
        env_out[rows, 128:256] = jnp.where(low_half, 0.0, env)
        one_high[:, rows], one_low[:, rows] = split_pair(hidden_one.T)
        two_high[:, rows], two_low[:, rows] = split_pair(hidden_two.T)
        return carry

    lax.fori_loop(0, HALF, block, 0)
    residues_to_scratch(
        lambda start: taps[pl.ds(start, CHUNK), :], twiddle, high_ref, low_ref, inner
    )

    def transform(j, carry):
        real, imag = inner_dft((high_ref[j], low_ref[j]), matrix_high, matrix_low, inner, 1)
        sign = (1 - 2 * (j % 2)).astype(F32)
        spectrum[j, :, 0:128] = real + sign * swap(real)
        spectrum[j, :, 128:256] = imag + sign * swap(imag)
        return carry

    lax.fori_loop(0, HALF + 1, transform, 0)


def gradient_kernel(
    length, signal, spectrum, env, slope_one, slope_two, one_high, one_low, two_high, two_low,
    mid_back, last_back, matrix_high, matrix_low, twiddle, out, high_ref, low_ref, back_ref,
    last_sum, mid_sum, first_sum,
):
    padded = 2 * length
    inner = padded // RADIX
    low_half = low_lanes(inner)
    residues_to_scratch(
        lambda start: signal[pl.ds(start, CHUNK), :].astype(F32), twiddle, high_ref, low_ref, inner
    )

    def transform(j, carry):
        real, imag = inner_dft((high_ref[j], low_ref[j]), matrix_high, matrix_low, inner, 1)
        real_swap, imag_swap = swap(real), swap(imag)
        cotan_real = jnp.where(low_half, real_swap, real)
        cotan_imag = jnp.where(low_half, imag_swap, imag)
        other_real = jnp.where(low_half, spectrum[j, :, 0:128], real_swap)
        other_imag = jnp.where(low_half, spectrum[j, :, 128:256], imag_swap)
        product = jnp.concatenate(
            [
                cotan_real * other_real + cotan_imag * other_imag,
                cotan_imag * other_real - cotan_real * other_imag,
            ],
            axis=1,
        )
        real, imag = inner_dft(split_pair(product), matrix_high, matrix_low, inner, -1)
        back_ref[j, :, 0:128] = real
        back_ref[j, :, 128:256] = imag
        return carry

    lax.fori_loop(0, HALF + 1, transform, 0)

    def unspread(step, carry):
        start = pl.multiple_of(step * CHUNK, CHUNK)
        rows = pl.ds(start, CHUNK)
        turn = twiddle[rows, :]
        real_list, imag_list = [], []
        for j in range(HALF + 1):
            weight = (1.0 if j in (0, HALF) else 2.0) / padded
            real, imag = back_ref[j, rows, 0:128], back_ref[j, rows, 128:256]
            if j == 0:
                real_list.append(real * weight)
                imag_list.append(None)
                continue
            cosine = turn[:, j : j + 1] * weight
            sine = turn[:, RADIX + j : RADIX + j + 1] * weight
            real_list.append(real * cosine - imag * sine)
            imag_list.append(real * sine + imag * cosine)
        even, odd = gather_back(real_list, imag_list)
        for q in range(HALF):
            back_ref[q, rows, 0:128] = even[q] + odd[q]
            back_ref[q, rows, 128:256] = even[q] - odd[q]
        return carry

    lax.fori_loop(0, inner // CHUNK, unspread, 0)
    last_sum[...] = jnp.zeros_like(last_sum)
    mid_sum[...] = jnp.zeros_like(mid_sum)
    first_sum[...] = jnp.zeros_like(first_sum)
    mid_pair = split_pair(mid_back[...])
    last_pair = split_pair(last_back[...])
    local_rows = 128
    half_rows = local_rows // 2

    def block(q, carry):
        start = pl.multiple_of(q * inner, inner)
        rows = pl.ds(start, inner)
        for part in range(inner // local_rows):
            base = part * local_rows
            upper = back_ref[q, base : base + half_rows, 0:128]
            lower = back_ref[q, base + half_rows : base + local_rows, 0:128]
            out[q * (inner // local_rows) + part, 0:half_rows, :] = jnp.where(
                low_half[:half_rows], upper, swap(lower)
            ).astype(BF16)
        slope = split_pair(back_ref[q] * env[rows, :])
        last_sum[...] += dot_three((two_high[:, rows], two_low[:, rows]), slope)
        pre_two = split_pair(dot_three(slope, last_pair) * slope_two[rows, :])
        mid_sum[...] += dot_three((one_high[:, rows], one_low[:, rows]), pre_two)
        pre_one = dot_three(pre_two, mid_pair) * slope_one[rows, :]
        place = start + lax.broadcasted_iota(jnp.int32, (inner, 128), 0)
        scaled = jnp.where(low_half, place, place - length).astype(F32) / length
        first_sum[0:8] += jnp.sum((pre_one * scaled).reshape(inner // 8, 8, 128), axis=0)
        first_sum[8:16] += jnp.sum(pre_one.reshape(inner // 8, 8, 128), axis=0)
        return carry

    lax.fori_loop(0, HALF, block, 0)
    low_64 = low_lanes(64)
    low_32 = low_lanes(32)
    grad_last = swap(last_sum[0:64, 0:128]) + swap(last_sum[64:128, 128:256])
    pair = jnp.where(low_32, grad_last[0:32], swap(grad_last[32:64]))
    mid_total = mid_sum[0:64] + swap(mid_sum[64:128])
    mid_high = mid_total.astype(BF16).astype(F32)
    mid_rows = jnp.where(low_64, mid_high, swap(mid_total - mid_high))
    first = jnp.sum(first_sum[0:8], axis=0, keepdims=True)
    bias = jnp.sum(first_sum[8:16], axis=0, keepdims=True)
    first = first + swap(first)
    bias = bias + swap(bias)
    joined = jnp.where(low_lanes(1), first, bias)
    joined_high = joined.astype(BF16).astype(F32)
    row_index = lax.broadcasted_iota(jnp.int32, (16, 128), 0)
    joined_rows = jnp.where(
        row_index == 0, joined_high, jnp.where(row_index == 1, joined - joined_high, 0.0)
    )
    tail = jnp.concatenate([pair, mid_rows, joined_rows], axis=0).astype(BF16)
    for device in range(out.shape[0]):
        out[device, half_rows:, :] = tail


def unpack_kernel(loss_scale, received, grad_tokens, grad_first, grad_bias, grad_mid, grad_last):
    devices = received.shape[0]
    half_rows = grad_tokens.shape[0] // 2
    mid = jnp.zeros((64, 128), F32)
    joined = jnp.zeros((16, 128), F32)
    for source in range(devices):
        lanes = slice(64 * source, 64 * source + 64)
        tile = received[source, 0:half_rows, :]
        grad_tokens[0:half_rows, lanes] = tile[:, 0:64]
        grad_tokens[half_rows:, lanes] = tile[:, 64:128]
        last = received[source, half_rows : half_rows + 32, :].astype(F32) * loss_scale
        grad_last[0:32, lanes] = last[:, 0:64]
        grad_last[32:64, lanes] = last[:, 64:128]
        mid = mid + received[source, half_rows + 32 : half_rows + 96, :].astype(F32)
        joined = joined + received[source, half_rows + 96 : half_rows + 112, :].astype(F32)
    grad_mid[...] = ((mid + swap(mid)) * loss_scale)[:, 0:64]
    first = (joined[0:1] + joined[1:2]) * loss_scale
    grad_first[...] = first[:, 0:64]
    grad_bias[...] = first[:, 64:128]


def call(kernel, out_shape, scratch=(), flops=0, limit=24):
    return pl.pallas_call(
        kernel,
        out_shape=out_shape,
        scratch_shapes=list(scratch),
        compiler_params=pltpu.CompilerParams(vmem_limit_bytes=limit << 20),
        cost_estimate=pl.CostEstimate(flops=flops, bytes_accessed=1 << 20, transcendentals=0),
    )


def shape(dims, dtype):
    return jax.ShapeDtypeStruct(dims, dtype)


def twice(value):
    return jnp.concatenate([value, value]).reshape(1, -1)


def diagonal(matrix):
    empty = jnp.zeros_like(matrix)
    return jnp.block([[matrix, empty], [empty, matrix]])


def by_channels(tokens_in, grad_out, decay_rate, w_in, b_in, w_mid, w_out):
    devices = lax.axis_size("ctx")
    own_index = lax.axis_index("ctx")
    local_rows = tokens_in.shape[0]
    length = local_rows * devices
    padded = 2 * length
    inner = padded // RADIX
    bins = HALF + 1
    matrix_high, matrix_low, twiddle = dft_tables(padded)
    packed = call(pack_kernel, shape((devices, local_rows, 128), BF16))(tokens_in, grad_out)
    signal = lax.all_to_all(packed, "ctx", split_axis=0, concat_axis=0, tiled=True)
    signal = signal.reshape(length, 128)

    own_last = lax.dynamic_slice_in_dim(w_out, own_index * 64, 64, axis=1)
    own_rate = lax.dynamic_slice_in_dim(decay_rate, own_index * 64, 64, axis=0)
    double = 2.0 * own_rate
    geometric = 1.0 + 2.0 * jnp.exp(-double) * jnp.expm1(-double * (length - 1)) / jnp.expm1(
        -double
    )
    stage = [pltpu.VMEM((bins, inner, 256), BF16)] * 2
    (spectrum, env, slope_one, slope_two, one_high, one_low, two_high, two_low) = call(
        functools.partial(kernel_spectrum_kernel, length),
        [
            shape((bins, inner, 256), F32),
            shape((length, 256), F32),
            shape((length, 128), F32),
            shape((length, 128), F32),
        ]
        + [shape((128, length), BF16)] * 4,
        scratch=[pltpu.VMEM((length, 128), F32)] + stage,
        flops=4 << 30,
    )(
        twice(own_rate),
        twice(lax.rsqrt(geometric)),
        twice(w_in),
        twice(b_in),
        diagonal(w_mid),
        diagonal(own_last),
        matrix_high,
        matrix_low,
        twiddle,
    )
    empty = jnp.zeros((64, 64), F32)
    last_back = jnp.block(
        [[empty, empty], [own_last.T, empty], [empty, empty], [empty, own_last.T]]
    )
    sent_rows = local_rows // 2 + 32 + 64 + 16
    sent = call(
        functools.partial(gradient_kernel, length),
        shape((devices, sent_rows, 128), BF16),
        scratch=stage
        + [
            pltpu.VMEM((bins, inner, 256), F32),
            pltpu.VMEM((128, 256), F32),
            pltpu.VMEM((128, 128), F32),
            pltpu.VMEM((16, 128), F32),
        ],
        flops=8 << 30,
    )(
        signal, spectrum, env, slope_one, slope_two, one_high, one_low, two_high, two_low,
        diagonal(w_mid.T), last_back, matrix_high, matrix_low, twiddle,
    )
    received = lax.all_to_all(sent, "ctx", split_axis=0, concat_axis=0, tiled=True)
    input_grad, grad_first, grad_bias, grad_mid, grad_last = call(
        functools.partial(unpack_kernel, 1.0 / math.sqrt(length)),
        [
            shape(tokens_in.shape, BF16),
            shape((1, 64), F32),
            shape((1, 64), F32),
            shape((64, 64), F32),
            shape(w_out.shape, F32),
        ],
    )(received)
    return input_grad, grad_first.reshape(64), grad_bias.reshape(64), grad_mid, grad_last


HIGHEST = lax.Precision.HIGHEST
TWO_PI = 2.0 * math.pi


def phase_angle(product, period):
    return TWO_PI / period * (product % period).astype(jnp.float32)


def frequency_rows(devices):
    row_index = jnp.arange(2 * devices, dtype=jnp.int32)
    row_block = row_index // 2
    second = row_index % 2
    paired = jnp.where(row_block == 0, devices, 2 * devices - row_block)
    return jnp.where(second == 0, row_block, paired)


def source_rows(devices):
    row_index = jnp.arange(2 * devices, dtype=jnp.int32)
    return row_index // 2 + row_index % 2 * devices


def envelope(lag_values, decay_rate, length):
    double = 2.0 * decay_rate
    geometric = 1.0 + 2.0 * jnp.exp(-double) * jnp.expm1(-double * (length - 1)) / jnp.expm1(
        -double
    )
    distance = jnp.abs(lag_values).astype(jnp.float32)[..., None]
    live_mask = (lag_values != -length).astype(jnp.float32)[..., None]
    return live_mask * lax.rsqrt(geometric) * jnp.exp(-distance * decay_rate)


def position_mlp(scaled, w_first, w_bias, w_middle, w_last):
    hidden_one = jax.nn.silu(scaled[..., None] * w_first + w_bias)
    hidden_two = jax.nn.silu(jnp.dot(hidden_one, w_middle, precision=HIGHEST))
    return jnp.dot(hidden_two, w_last, precision=HIGHEST)


def rotate(real_a, imag_a, real_b, imag_b):
    return (real_a * real_b - imag_a * imag_b, real_a * imag_b + imag_a * real_b)


def first_section(signal, columns, freq_order, local_slab, padded):
    freq_count = freq_order.shape[0]
    angles = phase_angle(freq_order[:, None] * columns[None, :], freq_count)
    real_part = jnp.einsum("fp,prc->frc", jnp.cos(angles), signal, precision=HIGHEST)
    imag_part = jnp.einsum("fp,prc->frc", -jnp.sin(angles), signal, precision=HIGHEST)
    twiddle = phase_angle(freq_order[:, None] * local_slab[None, :], padded)[:, :, None]
    return rotate(real_part, imag_part, jnp.cos(twiddle), -jnp.sin(twiddle))


def along_rows(stacked, direction):
    row_count = stacked.shape[1]
    half_width = stacked.shape[2] // 2
    positions = jnp.arange(row_count, dtype=jnp.int32)
    angles = phase_angle(positions[:, None] * positions[None, :], row_count)
    with_cos = jnp.einsum("gm,imc->igc", jnp.cos(angles), stacked, precision=HIGHEST)
    with_sin = jnp.einsum("gm,imc->igc", direction * jnp.sin(angles), stacked, precision=HIGHEST)
    real_part = with_cos[..., :half_width] - with_sin[..., half_width:]
    imag_part = with_cos[..., half_width:] + with_sin[..., :half_width]
    return (real_part, imag_part)


def last_section(stacked, out_rows, freq_order, padded):
    freq_count = freq_order.shape[0]
    half_width = stacked.shape[2] // 2
    angles = phase_angle(out_rows[:, None] * freq_order[None, :], freq_count)
    cos_table = jnp.cos(angles) / padded
    sin_table = jnp.sin(angles) / padded
    real_in = stacked[..., :half_width]
    imag_in = stacked[..., half_width:]
    leading, trailing, factor = (real_in, imag_in, -1.0)
    return jnp.einsum("pf,frc->prc", cos_table, leading, precision=HIGHEST) + factor * jnp.einsum(
        "pf,frc->prc", sin_table, trailing, precision=HIGHEST
    )


def by_frequencies(tokens_in, grad_out, decay_rate, w_in, b_in, w_mid, w_out):
    devices = lax.axis_size("ctx")
    own_index = lax.axis_index("ctx")
    tok_rows = tokens_in.shape[0]
    slab_rows = tok_rows // devices
    length = tok_rows * devices
    padded = 2 * length
    freq_order = frequency_rows(devices)
    lag_rows = source_rows(devices)
    token_cols = jnp.arange(devices, dtype=jnp.int32)
    local_slab = own_index * slab_rows + jnp.arange(slab_rows, dtype=jnp.int32)
    pair_index = jnp.arange(2, dtype=jnp.int32)
    local_freq = jnp.where(
        pair_index == 0, own_index, jnp.where(own_index == 0, devices, 2 * devices - own_index)
    )
    circular = (own_index + pair_index * devices)[:, None] * tok_rows + jnp.arange(
        tok_rows, dtype=jnp.int32
    )[None, :]
    lag_values = jnp.where(circular < length, circular, circular - padded)
    scaled = lag_values.astype(jnp.float32) / length
    weights_env = envelope(lag_values, decay_rate, length)

    def position_net(w_first, w_bias, w_middle, w_last):
        return position_mlp(scaled, w_first, w_bias, w_middle, w_last)

    position, pull_back = jax.vjp(position_net, w_in, b_in, w_mid, w_out)
    kernel = (position * weights_env).astype(jnp.bfloat16)
    tokens_mid, grads_mid, kernel_mid = (
        lax.all_to_all(tokens_in[None], "ctx", split_axis=1, concat_axis=0, tiled=True),
        lax.all_to_all(grad_out[None], "ctx", split_axis=1, concat_axis=0, tiled=True),
        lax.all_to_all(kernel, "ctx", split_axis=1, concat_axis=0, tiled=True),
    )
    token_real, token_imag = first_section(
        tokens_mid.astype(jnp.float32), token_cols, freq_order, local_slab, padded
    )
    cotan_real, cotan_imag = first_section(
        grads_mid.astype(jnp.float32), token_cols, freq_order, local_slab, padded
    )
    kern_real, kern_imag = first_section(
        kernel_mid.astype(jnp.float32), lag_rows, freq_order, local_slab, padded
    )
    kernel_stack = jnp.concatenate([kern_real, kern_imag], axis=2)
    token_stack = jnp.concatenate([token_real, token_imag], axis=2)
    cotan_stack = jnp.concatenate([cotan_real, cotan_imag], axis=2)
    token_spec, cotan_spec, kernel_spec = (
        lax.all_to_all(token_stack, "ctx", split_axis=0, concat_axis=1, tiled=True),
        lax.all_to_all(cotan_stack, "ctx", split_axis=0, concat_axis=1, tiled=True),
        lax.all_to_all(kernel_stack, "ctx", split_axis=0, concat_axis=1, tiled=True),
    )
    spec_token_real, spec_token_imag = along_rows(token_spec, -1.0)
    spec_cotan_real, spec_cotan_imag = along_rows(cotan_spec, -1.0)
    spec_kern_real, spec_kern_imag = along_rows(kernel_spec, -1.0)
    input_real = spec_kern_real * spec_cotan_real + spec_kern_imag * spec_cotan_imag
    input_imag = spec_kern_real * spec_cotan_imag - spec_kern_imag * spec_cotan_real
    lagged_real = spec_cotan_real * spec_token_real + spec_cotan_imag * spec_token_imag
    lagged_imag = spec_cotan_imag * spec_token_real - spec_cotan_real * spec_token_imag
    positions = jnp.arange(tok_rows, dtype=jnp.int32)
    back_angle = phase_angle(local_freq[:, None] * positions[None, :], padded)[:, :, None]
    back_cos = jnp.cos(back_angle)
    back_sin = jnp.sin(back_angle)

    def inverse_rows(real_part, imag_part):
        stacked = jnp.concatenate([real_part, imag_part], axis=2)
        out_real, out_imag = along_rows(stacked, 1.0)
        turned_real, turned_imag = rotate(out_real, out_imag, back_cos, back_sin)
        return jnp.concatenate([turned_real, turned_imag], axis=2)

    spread_input, spread_lagged = (
        lax.all_to_all(
            inverse_rows(input_real, input_imag), "ctx", split_axis=1, concat_axis=0, tiled=True
        ),
        lax.all_to_all(
            inverse_rows(lagged_real, lagged_imag), "ctx", split_axis=1, concat_axis=0, tiled=True
        ),
    )
    input_rows = last_section(spread_input, token_cols, freq_order, padded)
    lagged_rows = last_section(spread_lagged, lag_rows, freq_order, padded)
    input_back, lag_back = (
        lax.all_to_all(input_rows, "ctx", split_axis=0, concat_axis=1, tiled=True),
        lax.all_to_all(lagged_rows, "ctx", split_axis=0, concat_axis=1, tiled=True),
    )
    input_grad = input_back[0]
    gradients = pull_back(lag_back * weights_env)
    summed = lax.psum((gradients[0], gradients[1], gradients[2], gradients[3]), "ctx")
    loss_scale = 1.0 / math.sqrt(length)
    return (
        input_grad.astype(jnp.bfloat16),
        summed[0] * loss_scale,
        summed[1] * loss_scale,
        summed[2] * loss_scale,
        summed[3] * loss_scale,
    )


def on_device(tokens_in, grad_out, decay_rate, w_in, b_in, w_mid, w_out):
    devices = lax.axis_size("ctx")
    fits = (
        tokens_in.shape == (128, 64 * devices)
        and devices * 128 % (128 * HALF) == 0
        and w_mid.shape == (64, 64)
    )
    form = by_channels if fits else by_frequencies
    return form(tokens_in, grad_out, decay_rate, w_in, b_in, w_mid, w_out)


def solution(mesh):
    in_specs = (P(("groups", "ctx"), None), P(("groups", "ctx"), None), P(), P(), P(), P(), P())
    out_specs = (
        P(("groups", "ctx"), None),
        P("groups"),
        P("groups"),
        P("groups", None),
        P("groups", None),
    )
    return jax.shard_map(
        on_device, mesh=mesh, in_specs=in_specs, out_specs=out_specs, check_vma=False
    )
```

```python
import functools
import math

import jax
import jax.numpy as jnp
import numpy as np
from jax import lax
from jax.experimental import pallas as pl
from jax.experimental.pallas import tpu as pltpu
from jax.sharding import PartitionSpec as P

RADIX = 16
HALF = RADIX // 2
CHUNK = 32
UNROLL_CHUNK = 1
UNROLL_BIN = 1
UNROLL_ROWS = 1
F32 = jnp.float32
BF16 = jnp.bfloat16


def split_pair(value):
    high = value.astype(BF16)
    return high, (value - high.astype(F32)).astype(BF16)


def dot(left, right):
    return jnp.dot(left, right, preferred_element_type=F32)


def wide_three(value):
    high, low = split_pair(value)
    return jnp.concatenate([high, low, high], axis=1)


def tall_three(value):
    high, low = split_pair(value)
    return jnp.concatenate([high, high, low], axis=0)


def dft_tables(padded):
    inner = padded // RADIX
    grid = np.outer(np.arange(inner), np.arange(inner)) % inner
    angles = 2.0 * np.pi * grid / inner
    matrix = np.concatenate([np.cos(angles), np.sin(angles)], axis=0)
    high = matrix.astype(jnp.bfloat16)
    low = (matrix - high.astype(np.float64)).astype(jnp.bfloat16)
    matrix = np.concatenate([high, low, high], axis=1)
    turn = 2.0 * np.pi * np.outer(np.arange(inner), np.arange(RADIX)) / padded
    twiddle = np.zeros((inner, 128), np.float32)
    twiddle[:, :RADIX] = np.cos(turn)
    twiddle[:, RADIX : 2 * RADIX] = np.sin(turn)
    return jnp.asarray(matrix), jnp.asarray(twiddle)


def cos_of(index):
    return math.cos(2.0 * math.pi * index / RADIX)


def sin_of(index):
    return math.sin(2.0 * math.pi * index / RADIX)


def spread(x):
    plus = [x[q] + x[q + 4] for q in range(4)]
    minus = [x[q] - x[q + 4] for q in range(4)]
    root = math.sqrt(0.5)
    out = [None] * 9
    even, odd = plus[0] + plus[2], plus[1] + plus[3]
    out[0] = (even + odd, None)
    out[8] = (even - odd, None)
    out[4] = (plus[0] - plus[2], plus[3] - plus[1])
    across, along = root * (minus[1] - minus[3]), root * (minus[1] + minus[3])
    out[2] = (minus[0] + across, -minus[2] - along)
    out[6] = (minus[0] - across, minus[2] - along)
    differ = {q: x[q] - x[8 - q] for q in (1, 2, 3)}
    same = {q: x[q] + x[8 - q] for q in (1, 2, 3)}
    for j in (1, 3):
        real_even = x[0] + cos_of(2 * j) * differ[2]
        real_odd = cos_of(j) * differ[1] + cos_of(3 * j) * differ[3]
        imag_even = sin_of(4 * j) * x[4] + sin_of(2 * j) * same[2]
        imag_odd = sin_of(j) * same[1] + sin_of(3 * j) * same[3]
        out[j] = (real_even + real_odd, -(imag_odd + imag_even))
        out[8 - j] = (real_even - real_odd, imag_even - imag_odd)
    return out


def gather_back(real, imag):
    even, odd = [None] * 8, [None] * 8
    total, differ = real[0] + real[8], real[0] - real[8]
    real_sum, real_dif = real[2] + real[6], real[2] - real[6]
    imag_sum, imag_dif = imag[2] + imag[6], imag[2] - imag[6]
    root = math.sqrt(0.5)
    even[0] = total + real_sum + real[4]
    even[4] = total - real_sum + real[4]
    even[2] = total - imag_dif - real[4]
    even[6] = total + imag_dif - real[4]
    first, second = root * (real_dif - imag_sum), root * (real_dif + imag_sum)
    even[1] = differ + first - imag[4]
    even[5] = differ - first - imag[4]
    even[3] = differ - second + imag[4]
    even[7] = differ + second + imag[4]
    one_sum, one_dif = real[1] + real[7], real[1] - real[7]
    three_sum, three_dif = real[3] + real[5], real[3] - real[5]
    ione_sum, ione_dif = imag[1] + imag[7], imag[1] - imag[7]
    ithree_sum, ithree_dif = imag[3] + imag[5], imag[3] - imag[5]
    odd[0] = one_sum + three_sum
    odd[4] = ithree_dif - ione_dif
    for q in (1, 2, 3):
        if q % 2 == 0:
            cosines = cos_of(q) * one_sum + cos_of(3 * q) * three_sum
            sines = sin_of(q) * ione_dif + sin_of(3 * q) * ithree_dif
        else:
            cosines = cos_of(q) * one_dif + cos_of(3 * q) * three_dif
            sines = sin_of(q) * ione_sum + sin_of(3 * q) * ithree_sum
        odd[q] = cosines - sines
        odd[8 - q] = -cosines - sines
    return even, odd


def residues_to_scratch(load, twiddle, stage, inner):
    def chunk(step, carry):
        start = pl.multiple_of(step * CHUNK, CHUNK)
        turn = twiddle[pl.ds(start, CHUNK), :]
        for j, (real, imag) in enumerate(spread([load(q * inner + start) for q in range(HALF)])):
            if j > 0:
                cosine, sine = turn[:, j : j + 1], turn[:, RADIX + j : RADIX + j + 1]
                if imag is None:
                    real, imag = real * cosine, -real * sine
                else:
                    real, imag = real * cosine + imag * sine, imag * cosine - real * sine
            else:
                imag = jnp.zeros_like(real)
            for part, value in enumerate((real, imag)):
                high, low = split_pair(value)
                lanes = slice(128 * part, 128 * part + 128)
                stage[j, pl.ds(start, CHUNK), lanes] = high
                stage[j, pl.ds(inner + start, CHUNK), lanes] = high
                stage[j, pl.ds(2 * inner + start, CHUNK), lanes] = low
        return carry

    lax.fori_loop(0, inner // CHUNK, chunk, 0, unroll=UNROLL_CHUNK)


def inner_dft(stacked, matrix, inner, direction):
    product = dot(matrix[...], stacked)
    cos_real, cos_imag = product[:inner, :128], product[:inner, 128:]
    sin_real, sin_imag = product[inner:, :128], product[inner:, 128:]
    if direction > 0:
        return cos_real + sin_imag, cos_imag - sin_real
    return cos_real - sin_imag, cos_imag + sin_real


def low_lanes(rows):
    return lax.broadcasted_iota(jnp.int32, (rows, 128), 1) < 64


def swap(value):
    return pltpu.roll(value, 64, 1)


def fetch(sources, buffers, semaphores):
    copies = [
        pltpu.make_async_copy(source, buffer, semaphores.at[index])
        for index, (source, buffer) in enumerate(zip(sources, buffers))
    ]
    for copy in copies:
        copy.start()
    return copies


def pack_kernel(tokens_hbm, cotan_hbm, out, tokens, cotan, semaphores):
    for copy in fetch((tokens_hbm, cotan_hbm), (tokens, cotan), semaphores):
        copy.wait()
    for block in range(out.shape[0]):
        lanes = slice(64 * block, 64 * block + 64)
        out[block] = jnp.concatenate([tokens[:, lanes], cotan[:, lanes]], axis=1)


def diagonal(matrix):
    empty = jnp.zeros_like(matrix)
    return jnp.concatenate(
        [jnp.concatenate([matrix, empty], axis=1), jnp.concatenate([empty, matrix], axis=1)], axis=0
    )


def twice(row):
    return jnp.concatenate([row, row], axis=1)


def exp_minus_one(value):
    series = jnp.ones_like(value)
    for order in range(9, 1, -1):
        series = 1.0 + series * value * (1.0 / order)
    return jnp.where(jnp.abs(value) < 0.35, value * series, jnp.exp(value) - 1.0)


def kernel_spectrum_kernel(
    length, rates, w_first, w_bias, w_mid, w_last, matrix, twiddle,
    spectrum_hbm, env_hbm, slope_one_hbm, slope_two_hbm, one_high_hbm, one_low_hbm, two_high_hbm,
    two_low_hbm, mid_back, last_back,
    spectrum, env_out, slope_one, slope_two, one_high, one_low, two_high, two_low,
    taps, stage, semaphores,
):
    inner = 2 * length // RADIX
    low_half = low_lanes(inner)
    own = lax.axis_index("ctx")
    lanes = pl.ds(pl.multiple_of(own // 2 * 128, 128), 128)
    odd = own % 2 == 1
    last = w_last[:, lanes]
    last = diagonal(jnp.where(odd, swap(last), last)[:, 0:64])
    rate = rates[:, lanes]
    rate = twice(jnp.where(odd, swap(rate), rate)[:, 0:64])
    double = 2.0 * rate
    ratio = exp_minus_one(-double * (length - 1)) / exp_minus_one(-double)
    geometric = 1.0 + 2.0 * jnp.exp(-double) * ratio
    scale = lax.rsqrt(geometric)
    mid = diagonal(w_mid[...])
    mid_back[...] = tall_three(mid.T)
    last_back[...] = tall_three(last.T)
    mid, last = tall_three(mid), tall_three(last)
    first, bias = twice(w_first[...]), twice(w_bias[...])

    def block(step, carry):
        start = pl.multiple_of(step * inner, inner)
        rows = pl.ds(start, inner)
        place = start + lax.broadcasted_iota(jnp.int32, (inner, 128), 0)
        lag = jnp.where(low_half, place, place - length)
        scaled = lag.astype(F32) / length
        pre_one = scaled * first + bias
        gate_one = 1.0 / (1.0 + jnp.exp(-pre_one))
        hidden_one = pre_one * gate_one
        slope_one[rows, :] = gate_one * (1.0 + pre_one * (1.0 - gate_one))
        pre_two = dot(wide_three(hidden_one), mid)
        gate_two = 1.0 / (1.0 + jnp.exp(-pre_two))
        hidden_two = pre_two * gate_two
        slope_two[rows, :] = gate_two * (1.0 + pre_two * (1.0 - gate_two))
        position = dot(wide_three(hidden_two), last)
        live = jnp.where(lag == -length, 0.0, 1.0)
        env = live * scale * jnp.exp(-jnp.abs(lag).astype(F32) * rate)
        taps[rows, :] = (position * env).astype(BF16).astype(F32)
        env_out[rows, :] = env
        one_high[:, rows], one_low[:, rows] = split_pair(hidden_one.T)
        two_high[:, rows], two_low[:, rows] = split_pair(hidden_two.T)
        return carry

    lax.fori_loop(0, HALF, block, 0, unroll=UNROLL_ROWS)
    copies = fetch(
        (env_out, slope_one, slope_two, one_high, one_low, two_high, two_low),
        (env_hbm, slope_one_hbm, slope_two_hbm, one_high_hbm, one_low_hbm, two_high_hbm, two_low_hbm),
        semaphores,
    )
    residues_to_scratch(lambda start: taps[pl.ds(start, CHUNK), :], twiddle, stage, inner)

    def transform(j, carry):
        real, imag = inner_dft(stage[j], matrix, inner, 1)
        sign = 1.0 - 2.0 * lax.rem(jnp.asarray(j, jnp.int32), 2).astype(F32)
        spectrum[j, :, 0:128] = real + sign * swap(real)
        spectrum[j, :, 128:256] = imag + sign * swap(imag)
        return carry

    lax.fori_loop(0, HALF + 1, transform, 0, unroll=UNROLL_BIN)
    last_copy = pltpu.make_async_copy(spectrum, spectrum_hbm, semaphores.at[len(copies)])
    last_copy.start()
    for copy in copies + [last_copy]:
        copy.wait()


def gradient_kernel(
    length, signal, spectrum_hbm, env_hbm, slope_one_hbm, slope_two_hbm, one_high_hbm, one_low_hbm,
    two_high_hbm, two_low_hbm, mid_back, last_back, matrix, twiddle, out,
    spectrum, env, slope_one, slope_two, one_high, one_low, two_high, two_low, semaphores,
    stage, back_ref, slope_high, slope_low, pre_high, pre_low,
):
    padded = 2 * length
    inner = padded // RADIX
    low_half = low_lanes(inner)
    copies = fetch(
        (spectrum_hbm, env_hbm, slope_one_hbm, slope_two_hbm, one_high_hbm, one_low_hbm,
         two_high_hbm, two_low_hbm),
        (spectrum, env, slope_one, slope_two, one_high, one_low, two_high, two_low),
        semaphores,
    )
    residues_to_scratch(
        lambda start: signal[pl.ds(start, CHUNK), :].astype(F32), twiddle, stage, inner
    )
    copies[0].wait()

    def transform(j, carry):
        real, imag = inner_dft(stage[j], matrix, inner, 1)
        real_swap, imag_swap = swap(real), swap(imag)
        cotan_real = jnp.where(low_half, real_swap, real)
        cotan_imag = jnp.where(low_half, imag_swap, imag)
        other_real = jnp.where(low_half, spectrum[j, :, 0:128], real_swap)
        other_imag = jnp.where(low_half, spectrum[j, :, 128:256], imag_swap)
        product = jnp.concatenate(
            [
                cotan_real * other_real + cotan_imag * other_imag,
                cotan_imag * other_real - cotan_real * other_imag,
            ],
            axis=1,
        )
        real, imag = inner_dft(tall_three(product), matrix, inner, -1)
        back_ref[j, :, 0:128] = real
        back_ref[j, :, 128:256] = imag
        return carry

    lax.fori_loop(0, HALF + 1, transform, 0, unroll=UNROLL_BIN)
    copies[1].wait()

    def unspread(step, carry):
        start = pl.multiple_of(step * CHUNK, CHUNK)
        rows = pl.ds(start, CHUNK)
        turn = twiddle[rows, :]
        real_list, imag_list = [], []
        for j in range(HALF + 1):
            weight = (1.0 if j in (0, HALF) else 2.0) / padded
            real, imag = back_ref[j, rows, 0:128], back_ref[j, rows, 128:256]
            if j == 0:
                real_list.append(real * weight)
                imag_list.append(None)
                continue
            cosine = turn[:, j : j + 1] * weight
            sine = turn[:, RADIX + j : RADIX + j + 1] * weight
            real_list.append(real * cosine - imag * sine)
            imag_list.append(real * sine + imag * cosine)
        even, odd = gather_back(real_list, imag_list)
        for q in range(HALF):
            joined, apart = even[q] + odd[q], even[q] - odd[q]
            back_ref[q, rows, 0:128] = joined
            at = pl.ds(q * inner + start, CHUNK)
            lag_grad = jnp.where(low_lanes(CHUNK), swap(joined), apart)
            slope_high[at, :], slope_low[at, :] = split_pair(lag_grad * env[at, :])
        return carry

    lax.fori_loop(0, inner // CHUNK, unspread, 0, unroll=UNROLL_CHUNK)
    for copy in copies[2:]:
        copy.wait()
    local_rows = 128
    half_rows = local_rows // 2

    def block(q, carry):
        first_sum, bias_sum = carry
        start = pl.multiple_of(q * inner, inner)
        rows = pl.ds(start, inner)
        for part in range(inner // local_rows):
            base = part * local_rows
            upper = back_ref[q, base : base + half_rows, 0:128]
            lower = back_ref[q, base + half_rows : base + local_rows, 0:128]
            out[q * (inner // local_rows) + part, 0:half_rows, :] = jnp.where(
                low_half[:half_rows], upper, swap(lower)
            ).astype(BF16)
        high, low = slope_high[rows, :], slope_low[rows, :]
        slope = jnp.concatenate([high, low, high], axis=1)
        high, low = split_pair(dot(slope, last_back[...]) * slope_two[rows, :])
        pre_high[rows, :], pre_low[rows, :] = high, low
        pre_two = jnp.concatenate([high, low, high], axis=1)
        pre_one = dot(pre_two, mid_back[...]) * slope_one[rows, :]
        place = start + lax.broadcasted_iota(jnp.int32, (inner, 128), 0)
        scaled = jnp.where(low_half, place, place - length).astype(F32) / length
        first_sum = first_sum + jnp.sum((pre_one * scaled).reshape(inner // 8, 8, 128), axis=0)
        bias_sum = bias_sum + jnp.sum(pre_one.reshape(inner // 8, 8, 128), axis=0)
        return first_sum, bias_sum

    none = jnp.zeros((8, 128), F32)
    first_sum, bias_sum = lax.fori_loop(0, HALF, block, (none, none), unroll=UNROLL_ROWS)
    last_sum = dot(two_high[...], slope_high[...]) + (
        dot(two_low[...], slope_high[...]) + dot(two_high[...], slope_low[...])
    )
    mid_sum = dot(one_high[...], pre_high[...]) + (
        dot(one_low[...], pre_high[...]) + dot(one_high[...], pre_low[...])
    )
    low_64 = low_lanes(64)
    low_32 = low_lanes(32)
    grad_last = last_sum[0:64] + swap(last_sum[64:128])
    pair = jnp.where(low_32, grad_last[0:32], swap(grad_last[32:64]))
    mid_total = mid_sum[0:64] + swap(mid_sum[64:128])
    mid_high = mid_total.astype(BF16).astype(F32)
    mid_rows = jnp.where(low_64, mid_high, swap(mid_total - mid_high))
    first = jnp.sum(first_sum, axis=0, keepdims=True)
    bias = jnp.sum(bias_sum, axis=0, keepdims=True)
    first = first + swap(first)
    bias = bias + swap(bias)
    joined = jnp.where(low_lanes(1), first, bias)
    joined_high = joined.astype(BF16).astype(F32)
    row_index = lax.broadcasted_iota(jnp.int32, (16, 128), 0)
    joined_rows = jnp.where(
        row_index == 0, joined_high, jnp.where(row_index == 1, joined - joined_high, 0.0)
    )
    for device in range(out.shape[0]):
        odd = device % 2
        tail = [pair[16 * odd : 16 * odd + 16], mid_rows[32 * odd : 32 * odd + 32], joined_rows]
        out[device, half_rows:, :] = jnp.concatenate(tail, axis=0).astype(BF16)


def sums_kernel(received, half, joined_out):
    half_rows = received.shape[1] - 64
    mid = jnp.zeros((32, 128), F32)
    joined = jnp.zeros((16, 128), F32)
    for source in range(received.shape[0]):
        lanes = slice(64 * source, 64 * source + 64)
        last = received[source, half_rows : half_rows + 16, :]
        half[0:16, lanes] = last[:, 0:64]
        half[16:32, lanes] = last[:, 64:128]
        mid = mid + received[source, half_rows + 16 : half_rows + 48, :].astype(F32)
        joined = joined + received[source, half_rows + 48 : half_rows + 64, :].astype(F32)
    mid = mid + swap(mid)
    high = mid.astype(BF16).astype(F32)
    columns = 64 * received.shape[0]
    half[:, columns : columns + 128] = jnp.where(low_lanes(32), high, mid - high).astype(BF16)
    joined_out[...] = joined


def tokens_kernel(received, grad_tokens):
    half_rows = grad_tokens.shape[0] // 2
    for source in range(received.shape[0]):
        lanes = slice(64 * source, 64 * source + 64)
        tile = received[source, 0:half_rows, :]
        grad_tokens[0:half_rows, lanes] = tile[:, 0:64]
        grad_tokens[half_rows:, lanes] = tile[:, 64:128]


def weights_kernel(loss_scale, joined, mine, other, grad_first, grad_bias, grad_mid, grad_last):
    odd = lax.rem(lax.axis_index("ctx"), 2)
    columns = grad_last.shape[1]
    for source, parity in ((mine, odd), (other, 1 - odd)):
        last = source[:, 0:columns].astype(F32) * loss_scale
        grad_last[pl.ds(pl.multiple_of(16 * parity, 16), 16), :] = last[0:16]
        grad_last[pl.ds(pl.multiple_of(32 + 16 * parity, 16), 16), :] = last[16:32]
        mid = source[:, columns : columns + 128].astype(F32) * loss_scale
        grad_mid[pl.ds(pl.multiple_of(32 * parity, 32), 32), :] = (mid + swap(mid))[:, 0:64]
    first = (joined[0:1] + joined[1:2]) * loss_scale
    grad_first[...] = first[:, 0:64]
    grad_bias[...] = first[:, 64:128]


def call(kernel, out_shape, scratch=(), flops=0, limit=24, **specs):
    return pl.pallas_call(
        kernel,
        out_shape=out_shape,
        **specs,
        scratch_shapes=list(scratch),
        compiler_params=pltpu.CompilerParams(vmem_limit_bytes=limit << 20),
        cost_estimate=pl.CostEstimate(flops=flops, bytes_accessed=1 << 20, transcendentals=0),
    )


def shape(dims, dtype):
    return jax.ShapeDtypeStruct(dims, dtype)


ON_HBM = pl.BlockSpec(memory_space=pltpu.HBM)
ON_VMEM = pl.BlockSpec(memory_space=pltpu.VMEM)


def passed_arrays(length):
    inner = 2 * length // RADIX
    return [
        ((HALF + 1, inner, 256), F32),
        ((length, 128), F32),
        ((length, 128), F32),
        ((length, 128), F32),
    ] + [((128, length), BF16)] * 4


def held_arrays(length):
    passed = passed_arrays(length)
    return [pltpu.VMEM(*one) for one in passed], pltpu.SemaphoreType.DMA((len(passed),))


def spectrum_call(length, *operands):
    inner = 2 * length // RADIX
    passed = passed_arrays(length)
    held, semaphores = held_arrays(length)
    return call(
        functools.partial(kernel_spectrum_kernel, length),
        [shape(*one) for one in passed] + [shape((384, 128), BF16)] * 2,
        scratch=held
        + [
            pltpu.VMEM((length, 128), F32),
            pltpu.VMEM((HALF + 1, 3 * inner, 256), BF16),
            semaphores,
        ],
        flops=4 << 30,
        limit=58,
        out_specs=[ON_HBM] * len(passed) + [ON_VMEM] * 2,
    )(*operands)


def gradient_call(length, signal, *operands):
    inner = 2 * length // RADIX
    held, semaphores = held_arrays(length)
    local_rows = 128
    return call(
        functools.partial(gradient_kernel, length),
        shape((length // local_rows, local_rows // 2 + 64, 128), BF16),
        scratch=held
        + [
            semaphores,
            pltpu.VMEM((HALF + 1, 3 * inner, 256), BF16),
            pltpu.VMEM((HALF + 1, inner, 256), F32),
        ]
        + [pltpu.VMEM((length, 128), BF16)] * 4,
        flops=8 << 30,
        limit=58,
        in_specs=[ON_VMEM] + [ON_HBM] * len(held) + [ON_VMEM] * 4,
    )(signal, *operands)


def by_channels(tokens_in, grad_out, decay_rate, w_in, b_in, w_mid, w_out):
    devices = lax.axis_size("ctx")
    local_rows = tokens_in.shape[0]
    length = local_rows * devices
    matrix, twiddle = dft_tables(2 * length)
    packed = call(
        pack_kernel,
        shape((devices, local_rows, 128), BF16),
        scratch=[pltpu.VMEM(tokens_in.shape, BF16)] * 2 + [pltpu.SemaphoreType.DMA((2,))],
        limit=58,
        in_specs=[ON_HBM] * 2,
    )(tokens_in, grad_out)
    signal = lax.all_to_all(packed, "ctx", split_axis=0, concat_axis=0, tiled=True)
    forward = spectrum_call(
        length, decay_rate.reshape(1, -1), w_in.reshape(1, -1), b_in.reshape(1, -1), w_mid, w_out,
        matrix, twiddle,
    )
    sent = gradient_call(length, signal.reshape(length, 128), *forward, matrix, twiddle)
    received = lax.all_to_all(sent, "ctx", split_axis=0, concat_axis=0, tiled=True)
    half, joined = call(
        sums_kernel, [shape((32, 64 * devices + 128), BF16), shape((16, 128), F32)]
    )(received)
    other = lax.ppermute(half, "ctx", [(index, index ^ 1) for index in range(devices)])
    input_grad = call(tokens_kernel, shape(tokens_in.shape, BF16), flops=1 << 26)(received)
    grad_first, grad_bias, grad_mid, grad_last = call(
        functools.partial(weights_kernel, 1.0 / math.sqrt(length)),
        [shape((1, 64), F32), shape((1, 64), F32), shape((64, 64), F32), shape(w_out.shape, F32)],
    )(joined, half, other)
    return input_grad, grad_first.reshape(64), grad_bias.reshape(64), grad_mid, grad_last


HIGHEST = lax.Precision.HIGHEST
TWO_PI = 2.0 * math.pi


def phase_angle(product, period):
    return TWO_PI / period * (product % period).astype(jnp.float32)


def frequency_rows(devices):
    row_index = jnp.arange(2 * devices, dtype=jnp.int32)
    row_block = row_index // 2
    second = row_index % 2
    paired = jnp.where(row_block == 0, devices, 2 * devices - row_block)
    return jnp.where(second == 0, row_block, paired)


def source_rows(devices):
    row_index = jnp.arange(2 * devices, dtype=jnp.int32)
    return row_index // 2 + row_index % 2 * devices


def envelope(lag_values, decay_rate, length):
    double = 2.0 * decay_rate
    geometric = 1.0 + 2.0 * jnp.exp(-double) * jnp.expm1(-double * (length - 1)) / jnp.expm1(
        -double
    )
    distance = jnp.abs(lag_values).astype(jnp.float32)[..., None]
    live_mask = (lag_values != -length).astype(jnp.float32)[..., None]
    return live_mask * lax.rsqrt(geometric) * jnp.exp(-distance * decay_rate)


def position_mlp(scaled, w_first, w_bias, w_middle, w_last):
    hidden_one = jax.nn.silu(scaled[..., None] * w_first + w_bias)
    hidden_two = jax.nn.silu(jnp.dot(hidden_one, w_middle, precision=HIGHEST))
    return jnp.dot(hidden_two, w_last, precision=HIGHEST)


def rotate(real_a, imag_a, real_b, imag_b):
    return (real_a * real_b - imag_a * imag_b, real_a * imag_b + imag_a * real_b)


def first_section(signal, columns, freq_order, local_slab, padded):
    freq_count = freq_order.shape[0]
    angles = phase_angle(freq_order[:, None] * columns[None, :], freq_count)
    real_part = jnp.einsum("fp,prc->frc", jnp.cos(angles), signal, precision=HIGHEST)
    imag_part = jnp.einsum("fp,prc->frc", -jnp.sin(angles), signal, precision=HIGHEST)
    twiddle = phase_angle(freq_order[:, None] * local_slab[None, :], padded)[:, :, None]
    return rotate(real_part, imag_part, jnp.cos(twiddle), -jnp.sin(twiddle))


def along_rows(stacked, direction):
    row_count = stacked.shape[1]
    half_width = stacked.shape[2] // 2
    positions = jnp.arange(row_count, dtype=jnp.int32)
    angles = phase_angle(positions[:, None] * positions[None, :], row_count)
    with_cos = jnp.einsum("gm,imc->igc", jnp.cos(angles), stacked, precision=HIGHEST)
    with_sin = jnp.einsum("gm,imc->igc", direction * jnp.sin(angles), stacked, precision=HIGHEST)
    real_part = with_cos[..., :half_width] - with_sin[..., half_width:]
    imag_part = with_cos[..., half_width:] + with_sin[..., :half_width]
    return (real_part, imag_part)


def last_section(stacked, out_rows, freq_order, padded):
    freq_count = freq_order.shape[0]
    half_width = stacked.shape[2] // 2
    angles = phase_angle(out_rows[:, None] * freq_order[None, :], freq_count)
    cos_table = jnp.cos(angles) / padded
    sin_table = jnp.sin(angles) / padded
    real_in = stacked[..., :half_width]
    imag_in = stacked[..., half_width:]
    leading, trailing, factor = (real_in, imag_in, -1.0)
    return jnp.einsum("pf,frc->prc", cos_table, leading, precision=HIGHEST) + factor * jnp.einsum(
        "pf,frc->prc", sin_table, trailing, precision=HIGHEST
    )


def by_frequencies(tokens_in, grad_out, decay_rate, w_in, b_in, w_mid, w_out):
    devices = lax.axis_size("ctx")
    own_index = lax.axis_index("ctx")
    tok_rows = tokens_in.shape[0]
    slab_rows = tok_rows // devices
    length = tok_rows * devices
    padded = 2 * length
    freq_order = frequency_rows(devices)
    lag_rows = source_rows(devices)
    token_cols = jnp.arange(devices, dtype=jnp.int32)
    local_slab = own_index * slab_rows + jnp.arange(slab_rows, dtype=jnp.int32)
    pair_index = jnp.arange(2, dtype=jnp.int32)
    local_freq = jnp.where(
        pair_index == 0, own_index, jnp.where(own_index == 0, devices, 2 * devices - own_index)
    )
    circular = (own_index + pair_index * devices)[:, None] * tok_rows + jnp.arange(
        tok_rows, dtype=jnp.int32
    )[None, :]
    lag_values = jnp.where(circular < length, circular, circular - padded)
    scaled = lag_values.astype(jnp.float32) / length
    weights_env = envelope(lag_values, decay_rate, length)

    def position_net(w_first, w_bias, w_middle, w_last):
        return position_mlp(scaled, w_first, w_bias, w_middle, w_last)

    position, pull_back = jax.vjp(position_net, w_in, b_in, w_mid, w_out)
    kernel = (position * weights_env).astype(jnp.bfloat16)
    tokens_mid, grads_mid, kernel_mid = (
        lax.all_to_all(tokens_in[None], "ctx", split_axis=1, concat_axis=0, tiled=True),
        lax.all_to_all(grad_out[None], "ctx", split_axis=1, concat_axis=0, tiled=True),
        lax.all_to_all(kernel, "ctx", split_axis=1, concat_axis=0, tiled=True),
    )
    token_real, token_imag = first_section(
        tokens_mid.astype(jnp.float32), token_cols, freq_order, local_slab, padded
    )
    cotan_real, cotan_imag = first_section(
        grads_mid.astype(jnp.float32), token_cols, freq_order, local_slab, padded
    )
    kern_real, kern_imag = first_section(
        kernel_mid.astype(jnp.float32), lag_rows, freq_order, local_slab, padded
    )
    kernel_stack = jnp.concatenate([kern_real, kern_imag], axis=2)
    token_stack = jnp.concatenate([token_real, token_imag], axis=2)
    cotan_stack = jnp.concatenate([cotan_real, cotan_imag], axis=2)
    token_spec, cotan_spec, kernel_spec = (
        lax.all_to_all(token_stack, "ctx", split_axis=0, concat_axis=1, tiled=True),
        lax.all_to_all(cotan_stack, "ctx", split_axis=0, concat_axis=1, tiled=True),
        lax.all_to_all(kernel_stack, "ctx", split_axis=0, concat_axis=1, tiled=True),
    )
    spec_token_real, spec_token_imag = along_rows(token_spec, -1.0)
    spec_cotan_real, spec_cotan_imag = along_rows(cotan_spec, -1.0)
    spec_kern_real, spec_kern_imag = along_rows(kernel_spec, -1.0)
    input_real = spec_kern_real * spec_cotan_real + spec_kern_imag * spec_cotan_imag
    input_imag = spec_kern_real * spec_cotan_imag - spec_kern_imag * spec_cotan_real
    lagged_real = spec_cotan_real * spec_token_real + spec_cotan_imag * spec_token_imag
    lagged_imag = spec_cotan_imag * spec_token_real - spec_cotan_real * spec_token_imag
    positions = jnp.arange(tok_rows, dtype=jnp.int32)
    back_angle = phase_angle(local_freq[:, None] * positions[None, :], padded)[:, :, None]
    back_cos = jnp.cos(back_angle)
    back_sin = jnp.sin(back_angle)

    def inverse_rows(real_part, imag_part):
        stacked = jnp.concatenate([real_part, imag_part], axis=2)
        out_real, out_imag = along_rows(stacked, 1.0)
        turned_real, turned_imag = rotate(out_real, out_imag, back_cos, back_sin)
        return jnp.concatenate([turned_real, turned_imag], axis=2)

    spread_input, spread_lagged = (
        lax.all_to_all(
            inverse_rows(input_real, input_imag), "ctx", split_axis=1, concat_axis=0, tiled=True
        ),
        lax.all_to_all(
            inverse_rows(lagged_real, lagged_imag), "ctx", split_axis=1, concat_axis=0, tiled=True
        ),
    )
    input_rows = last_section(spread_input, token_cols, freq_order, padded)
    lagged_rows = last_section(spread_lagged, lag_rows, freq_order, padded)
    input_back, lag_back = (
        lax.all_to_all(input_rows, "ctx", split_axis=0, concat_axis=1, tiled=True),
        lax.all_to_all(lagged_rows, "ctx", split_axis=0, concat_axis=1, tiled=True),
    )
    input_grad = input_back[0]
    gradients = pull_back(lag_back * weights_env)
    summed = lax.psum((gradients[0], gradients[1], gradients[2], gradients[3]), "ctx")
    loss_scale = 1.0 / math.sqrt(length)
    return (
        input_grad.astype(jnp.bfloat16),
        summed[0] * loss_scale,
        summed[1] * loss_scale,
        summed[2] * loss_scale,
        summed[3] * loss_scale,
    )


def on_device(tokens_in, grad_out, decay_rate, w_in, b_in, w_mid, w_out):
    devices = lax.axis_size("ctx")
    fits = (
        tokens_in.shape == (128, 64 * devices)
        and devices % 2 == 0
        and devices * 128 % (128 * HALF) == 0
        and w_mid.shape == (64, 64)
    )
    form = by_channels if fits else by_frequencies
    return form(tokens_in, grad_out, decay_rate, w_in, b_in, w_mid, w_out)


def solution(mesh):
    in_specs = (P(("groups", "ctx"), None), P(("groups", "ctx"), None), P(), P(), P(), P(), P())
    out_specs = (
        P(("groups", "ctx"), None),
        P("groups"),
        P("groups"),
        P("groups", None),
        P("groups", None),
    )
    return jax.shard_map(
        on_device, mesh=mesh, in_specs=in_specs, out_specs=out_specs, check_vma=False
    )
```

```python
import functools
import math

import jax
import jax.numpy as jnp
import numpy as np
from jax import lax
from jax.experimental import pallas as pl
from jax.experimental.pallas import tpu as pltpu
from jax.sharding import PartitionSpec as P

RADIX = 16
HALF = RADIX // 2
CHUNK = 32
UNROLL_CHUNK = 8
UNROLL_BIN = 9
UNROLL_ROWS = 8
FIRST_LIMIT = 56
SECOND_LIMIT = 50
F32 = jnp.float32
BF16 = jnp.bfloat16


def split_pair(value):
    high = value.astype(BF16)
    return high, (value - high.astype(F32)).astype(BF16)


def dot(left, right):
    return jnp.dot(left, right, preferred_element_type=F32)


def wide_three(value):
    high, low = split_pair(value)
    return jnp.concatenate([high, low, high], axis=1)


def tall_three(value):
    high, low = split_pair(value)
    return jnp.concatenate([high, high, low], axis=0)


def dft_tables(padded):
    inner = padded // RADIX
    grid = np.outer(np.arange(inner), np.arange(inner)) % inner
    angles = 2.0 * np.pi * grid / inner
    matrix = np.concatenate([np.cos(angles), np.sin(angles)], axis=0)
    high = matrix.astype(jnp.bfloat16)
    low = (matrix - high.astype(np.float64)).astype(jnp.bfloat16)
    matrix = np.concatenate([high, low, high], axis=1)
    turn = 2.0 * np.pi * np.outer(np.arange(inner), np.arange(RADIX)) / padded
    twiddle = np.zeros((inner, 128), np.float32)
    twiddle[:, :RADIX] = np.cos(turn)
    twiddle[:, RADIX : 2 * RADIX] = np.sin(turn)
    return jnp.asarray(matrix), jnp.asarray(twiddle)


def cos_of(index):
    return math.cos(2.0 * math.pi * index / RADIX)


def sin_of(index):
    return math.sin(2.0 * math.pi * index / RADIX)


def spread(x):
    plus = [x[q] + x[q + 4] for q in range(4)]
    minus = [x[q] - x[q + 4] for q in range(4)]
    root = math.sqrt(0.5)
    out = [None] * 9
    even, odd = plus[0] + plus[2], plus[1] + plus[3]
    out[0] = (even + odd, None)
    out[8] = (even - odd, None)
    out[4] = (plus[0] - plus[2], plus[3] - plus[1])
    across, along = root * (minus[1] - minus[3]), root * (minus[1] + minus[3])
    out[2] = (minus[0] + across, -minus[2] - along)
    out[6] = (minus[0] - across, minus[2] - along)
    differ = {q: x[q] - x[8 - q] for q in (1, 2, 3)}
    same = {q: x[q] + x[8 - q] for q in (1, 2, 3)}
    for j in (1, 3):
        real_even = x[0] + cos_of(2 * j) * differ[2]
        real_odd = cos_of(j) * differ[1] + cos_of(3 * j) * differ[3]
        imag_even = sin_of(4 * j) * x[4] + sin_of(2 * j) * same[2]
        imag_odd = sin_of(j) * same[1] + sin_of(3 * j) * same[3]
        out[j] = (real_even + real_odd, -(imag_odd + imag_even))
        out[8 - j] = (real_even - real_odd, imag_even - imag_odd)
    return out


def gather_back(real, imag):
    even, odd = [None] * 8, [None] * 8
    total, differ = real[0] + real[8], real[0] - real[8]
    real_sum, real_dif = real[2] + real[6], real[2] - real[6]
    imag_sum, imag_dif = imag[2] + imag[6], imag[2] - imag[6]
    root = math.sqrt(0.5)
    even[0] = total + real_sum + real[4]
    even[4] = total - real_sum + real[4]
    even[2] = total - imag_dif - real[4]
    even[6] = total + imag_dif - real[4]
    first, second = root * (real_dif - imag_sum), root * (real_dif + imag_sum)
    even[1] = differ + first - imag[4]
    even[5] = differ - first - imag[4]
    even[3] = differ - second + imag[4]
    even[7] = differ + second + imag[4]
    one_sum, one_dif = real[1] + real[7], real[1] - real[7]
    three_sum, three_dif = real[3] + real[5], real[3] - real[5]
    ione_sum, ione_dif = imag[1] + imag[7], imag[1] - imag[7]
    ithree_sum, ithree_dif = imag[3] + imag[5], imag[3] - imag[5]
    odd[0] = one_sum + three_sum
    odd[4] = ithree_dif - ione_dif
    for q in (1, 2, 3):
        if q % 2 == 0:
            cosines = cos_of(q) * one_sum + cos_of(3 * q) * three_sum
            sines = sin_of(q) * ione_dif + sin_of(3 * q) * ithree_dif
        else:
            cosines = cos_of(q) * one_dif + cos_of(3 * q) * three_dif
            sines = sin_of(q) * ione_sum + sin_of(3 * q) * ithree_sum
        odd[q] = cosines - sines
        odd[8 - q] = -cosines - sines
    return even, odd


def residues_to_scratch(load, twiddle, stage, inner):
    def chunk(step, carry):
        start = pl.multiple_of(step * CHUNK, CHUNK)
        turn = twiddle[pl.ds(start, CHUNK), :]
        for j, (real, imag) in enumerate(spread([load(q * inner + start) for q in range(HALF)])):
            if j > 0:
                cosine, sine = turn[:, j : j + 1], turn[:, RADIX + j : RADIX + j + 1]
                if imag is None:
                    real, imag = real * cosine, -real * sine
                else:
                    real, imag = real * cosine + imag * sine, imag * cosine - real * sine
            else:
                imag = jnp.zeros_like(real)
            for part, value in enumerate((real, imag)):
                high, low = split_pair(value)
                lanes = slice(128 * part, 128 * part + 128)
                stage[j, pl.ds(start, CHUNK), lanes] = high
                stage[j, pl.ds(inner + start, CHUNK), lanes] = high
                stage[j, pl.ds(2 * inner + start, CHUNK), lanes] = low
        return carry

    lax.fori_loop(0, inner // CHUNK, chunk, 0, unroll=UNROLL_CHUNK)


def inner_dft(stacked, matrix, inner, direction):
    product = dot(matrix[...], stacked)
    cos_real, cos_imag = product[:inner, :128], product[:inner, 128:]
    sin_real, sin_imag = product[inner:, :128], product[inner:, 128:]
    if direction > 0:
        return cos_real + sin_imag, cos_imag - sin_real
    return cos_real - sin_imag, cos_imag + sin_real


def low_lanes(rows):
    return lax.broadcasted_iota(jnp.int32, (rows, 128), 1) < 64


def swap(value):
    return pltpu.roll(value, 64, 1)


def fetch(sources, buffers, semaphores):
    copies = [
        pltpu.make_async_copy(source, buffer, semaphores.at[index])
        for index, (source, buffer) in enumerate(zip(sources, buffers))
    ]
    for copy in copies:
        copy.start()
    return copies


def pack_kernel(tokens_hbm, cotan_hbm, out, tokens, cotan, semaphores):
    for copy in fetch((tokens_hbm, cotan_hbm), (tokens, cotan), semaphores):
        copy.wait()
    for block in range(out.shape[0]):
        lanes = slice(64 * block, 64 * block + 64)
        out[block] = jnp.concatenate([tokens[:, lanes], cotan[:, lanes]], axis=1)


def diagonal(matrix):
    empty = jnp.zeros_like(matrix)
    return jnp.concatenate(
        [jnp.concatenate([matrix, empty], axis=1), jnp.concatenate([empty, matrix], axis=1)], axis=0
    )


def twice(row):
    return jnp.concatenate([row, row], axis=1)


def exp_minus_one(value):
    series = jnp.ones_like(value)
    for order in range(9, 1, -1):
        series = 1.0 + series * value * (1.0 / order)
    return jnp.where(jnp.abs(value) < 0.35, value * series, jnp.exp(value) - 1.0)


def kernel_spectrum_kernel(
    length, rates, w_first, w_bias, w_mid, w_last, matrix, twiddle, wide_hbm, narrow_hbm,
    spectrum, env_out, slope_one, slope_two, one_high, one_low, two_high, two_low, mid_back,
    last_back, semaphores, taps, stage,
):
    inner = 2 * length // RADIX
    low_half = low_lanes(inner)
    own = lax.axis_index("ctx")
    lanes = pl.ds(pl.multiple_of(own // 2 * 128, 128), 128)
    odd = own % 2 == 1
    last = w_last[:, lanes]
    last = diagonal(jnp.where(odd, swap(last), last)[:, 0:64])
    rate = rates[:, lanes]
    rate = twice(jnp.where(odd, swap(rate), rate)[:, 0:64])
    double = 2.0 * rate
    ratio = exp_minus_one(-double * (length - 1)) / exp_minus_one(-double)
    geometric = 1.0 + 2.0 * jnp.exp(-double) * ratio
    scale = lax.rsqrt(geometric)
    mid = diagonal(w_mid[...])
    mid_back[...] = tall_three(mid.T)
    last_back[...] = tall_three(last.T)
    mid, last = tall_three(mid), tall_three(last)
    first, bias = twice(w_first[...]), twice(w_bias[...])

    def block(step, carry):
        start = pl.multiple_of(step * inner, inner)
        rows = pl.ds(start, inner)
        place = start + lax.broadcasted_iota(jnp.int32, (inner, 128), 0)
        lag = jnp.where(low_half, place, place - length)
        scaled = lag.astype(F32) / length
        pre_one = scaled * first + bias
        gate_one = 1.0 / (1.0 + jnp.exp(-pre_one))
        hidden_one = pre_one * gate_one
        slope_one[rows, :] = gate_one * (1.0 + pre_one * (1.0 - gate_one))
        pre_two = dot(wide_three(hidden_one), mid)
        gate_two = 1.0 / (1.0 + jnp.exp(-pre_two))
        hidden_two = pre_two * gate_two
        slope_two[rows, :] = gate_two * (1.0 + pre_two * (1.0 - gate_two))
        position = dot(wide_three(hidden_two), last)
        live = jnp.where(lag == -length, 0.0, 1.0)
        env = live * scale * jnp.exp(-jnp.abs(lag).astype(F32) * rate)
        taps[rows, :] = (position * env).astype(BF16).astype(F32)
        env_out[rows, :] = env
        one_high[:, rows], one_low[:, rows] = split_pair(hidden_one.T)
        two_high[:, rows], two_low[:, rows] = split_pair(hidden_two.T)
        return carry

    lax.fori_loop(0, HALF, block, 0, unroll=UNROLL_ROWS)
    places = passed_places(length, wide_hbm, narrow_hbm)
    held = (env_out, slope_one, slope_two, one_high, one_low, two_high, two_low, mid_back, last_back)
    copies = fetch(held, places[1:], semaphores)
    residues_to_scratch(lambda start: taps[pl.ds(start, CHUNK), :], twiddle, stage, inner)

    def transform(j, carry):
        real, imag = inner_dft(stage[j], matrix, inner, 1)
        sign = 1.0 - 2.0 * lax.rem(jnp.asarray(j, jnp.int32), 2).astype(F32)
        spectrum[pl.ds((2 * j + 0) * inner, inner), :] = real + sign * swap(real)
        spectrum[pl.ds((2 * j + 1) * inner, inner), :] = imag + sign * swap(imag)
        return carry

    lax.fori_loop(0, HALF + 1, transform, 0, unroll=UNROLL_BIN)
    last_copy = pltpu.make_async_copy(spectrum, places[0], semaphores.at[len(copies)])
    last_copy.start()
    for copy in copies + [last_copy]:
        copy.wait()


def gradient_kernel(
    length, signal, wide_hbm, narrow_hbm, matrix, twiddle, out,
    spectrum, env, slope_one, slope_two, one_high, one_low, two_high, two_low, mid_back, last_back,
    semaphores, stage, back_ref, slope_high, slope_low, pre_high, pre_low,
):
    padded = 2 * length
    inner = padded // RADIX
    low_half = low_lanes(inner)
    held = (spectrum, env, slope_one, slope_two, one_high, one_low, two_high, two_low, mid_back, last_back)
    copies = fetch(passed_places(length, wide_hbm, narrow_hbm), held, semaphores)
    residues_to_scratch(
        lambda start: signal[pl.ds(start, CHUNK), :].astype(F32), twiddle, stage, inner
    )
    copies[0].wait()

    def transform(j, carry):
        real, imag = inner_dft(stage[j], matrix, inner, 1)
        real_swap, imag_swap = swap(real), swap(imag)
        cotan_real = jnp.where(low_half, real_swap, real)
        cotan_imag = jnp.where(low_half, imag_swap, imag)
        other_real = jnp.where(low_half, spectrum[pl.ds((2 * j + 0) * inner, inner), :], real_swap)
        other_imag = jnp.where(low_half, spectrum[pl.ds((2 * j + 1) * inner, inner), :], imag_swap)
        product = jnp.concatenate(
            [
                cotan_real * other_real + cotan_imag * other_imag,
                cotan_imag * other_real - cotan_real * other_imag,
            ],
            axis=1,
        )
        real, imag = inner_dft(tall_three(product), matrix, inner, -1)
        back_ref[j, :, 0:128] = real
        back_ref[j, :, 128:256] = imag
        return carry

    lax.fori_loop(0, HALF + 1, transform, 0, unroll=UNROLL_BIN)
    copies[1].wait()

    def unspread(step, carry):
        start = pl.multiple_of(step * CHUNK, CHUNK)
        rows = pl.ds(start, CHUNK)
        turn = twiddle[rows, :]
        real_list, imag_list = [], []
        for j in range(HALF + 1):
            weight = (1.0 if j in (0, HALF) else 2.0) / padded
            real, imag = back_ref[j, rows, 0:128], back_ref[j, rows, 128:256]
            if j == 0:
                real_list.append(real * weight)
                imag_list.append(None)
                continue
            cosine = turn[:, j : j + 1] * weight
            sine = turn[:, RADIX + j : RADIX + j + 1] * weight
            real_list.append(real * cosine - imag * sine)
            imag_list.append(real * sine + imag * cosine)
        even, odd = gather_back(real_list, imag_list)
        for q in range(HALF):
            joined, apart = even[q] + odd[q], even[q] - odd[q]
            back_ref[q, rows, 0:128] = joined
            at = pl.ds(q * inner + start, CHUNK)
            lag_grad = jnp.where(low_lanes(CHUNK), swap(joined), apart)
            slope_high[at, :], slope_low[at, :] = split_pair(lag_grad * env[at, :])
        return carry

    lax.fori_loop(0, inner // CHUNK, unspread, 0, unroll=UNROLL_CHUNK)
    for copy in copies[2:]:
        copy.wait()
    local_rows = 128
    half_rows = local_rows // 2

    def block(q, carry):
        first_sum, bias_sum = carry
        start = pl.multiple_of(q * inner, inner)
        rows = pl.ds(start, inner)
        for part in range(inner // local_rows):
            base = part * local_rows
            upper = back_ref[q, base : base + half_rows, 0:128]
            lower = back_ref[q, base + half_rows : base + local_rows, 0:128]
            out[q * (inner // local_rows) + part, 0:half_rows, :] = jnp.where(
                low_half[:half_rows], upper, swap(lower)
            ).astype(BF16)
        high, low = slope_high[rows, :], slope_low[rows, :]
        slope = jnp.concatenate([high, low, high], axis=1)
        high, low = split_pair(dot(slope, last_back[...]) * slope_two[rows, :])
        pre_high[rows, :], pre_low[rows, :] = high, low
        pre_two = jnp.concatenate([high, low, high], axis=1)
        pre_one = dot(pre_two, mid_back[...]) * slope_one[rows, :]
        place = start + lax.broadcasted_iota(jnp.int32, (inner, 128), 0)
        scaled = jnp.where(low_half, place, place - length).astype(F32) / length
        first_sum = first_sum + jnp.sum((pre_one * scaled).reshape(inner // 8, 8, 128), axis=0)
        bias_sum = bias_sum + jnp.sum(pre_one.reshape(inner // 8, 8, 128), axis=0)
        return first_sum, bias_sum

    none = jnp.zeros((8, 128), F32)
    first_sum, bias_sum = lax.fori_loop(0, HALF, block, (none, none), unroll=UNROLL_ROWS)
    last_sum = dot(two_high[...], slope_high[...]) + (
        dot(two_low[...], slope_high[...]) + dot(two_high[...], slope_low[...])
    )
    mid_sum = dot(one_high[...], pre_high[...]) + (
        dot(one_low[...], pre_high[...]) + dot(one_high[...], pre_low[...])
    )
    low_64 = low_lanes(64)
    low_32 = low_lanes(32)
    grad_last = last_sum[0:64] + swap(last_sum[64:128])
    pair = jnp.where(low_32, grad_last[0:32], swap(grad_last[32:64]))
    mid_total = mid_sum[0:64] + swap(mid_sum[64:128])
    mid_high = mid_total.astype(BF16).astype(F32)
    mid_rows = jnp.where(low_64, mid_high, swap(mid_total - mid_high))
    first = jnp.sum(first_sum, axis=0, keepdims=True)
    bias = jnp.sum(bias_sum, axis=0, keepdims=True)
    first = first + swap(first)
    bias = bias + swap(bias)
    joined = jnp.where(low_lanes(1), first, bias)
    joined_high = joined.astype(BF16).astype(F32)
    row_index = lax.broadcasted_iota(jnp.int32, (16, 128), 0)
    joined_rows = jnp.where(
        row_index == 0, joined_high, jnp.where(row_index == 1, joined - joined_high, 0.0)
    )
    for device in range(out.shape[0]):
        odd = device % 2
        tail = [pair[16 * odd : 16 * odd + 16], mid_rows[32 * odd : 32 * odd + 32], joined_rows]
        out[device, half_rows:, :] = jnp.concatenate(tail, axis=0).astype(BF16)


def sums_kernel(received, half, joined_out):
    half_rows = received.shape[1] - 64
    mid = jnp.zeros((32, 128), F32)
    joined = jnp.zeros((16, 128), F32)
    for source in range(received.shape[0]):
        lanes = slice(64 * source, 64 * source + 64)
        last = received[source, half_rows : half_rows + 16, :]
        half[0:16, lanes] = last[:, 0:64]
        half[16:32, lanes] = last[:, 64:128]
        mid = mid + received[source, half_rows + 16 : half_rows + 48, :].astype(F32)
        joined = joined + received[source, half_rows + 48 : half_rows + 64, :].astype(F32)
    mid = mid + swap(mid)
    high = mid.astype(BF16).astype(F32)
    columns = 64 * received.shape[0]
    half[:, columns : columns + 128] = jnp.where(low_lanes(32), high, mid - high).astype(BF16)
    joined_out[...] = joined


def tokens_kernel(received, grad_tokens):
    half_rows = grad_tokens.shape[0] // 2
    for source in range(received.shape[0]):
        lanes = slice(64 * source, 64 * source + 64)
        tile = received[source, 0:half_rows, :]
        grad_tokens[0:half_rows, lanes] = tile[:, 0:64]
        grad_tokens[half_rows:, lanes] = tile[:, 64:128]


def weights_kernel(loss_scale, joined, mine, other, grad_first, grad_bias, grad_mid, grad_last):
    odd = lax.rem(lax.axis_index("ctx"), 2)
    columns = grad_last.shape[1]
    for source, parity in ((mine, odd), (other, 1 - odd)):
        last = source[:, 0:columns].astype(F32) * loss_scale
        grad_last[pl.ds(pl.multiple_of(16 * parity, 16), 16), :] = last[0:16]
        grad_last[pl.ds(pl.multiple_of(32 + 16 * parity, 16), 16), :] = last[16:32]
        mid = source[:, columns : columns + 128].astype(F32) * loss_scale
        grad_mid[pl.ds(pl.multiple_of(32 * parity, 32), 32), :] = (mid + swap(mid))[:, 0:64]
    first = (joined[0:1] + joined[1:2]) * loss_scale
    grad_first[...] = first[:, 0:64]
    grad_bias[...] = first[:, 64:128]


def call(kernel, out_shape, scratch=(), flops=0, limit=24, **specs):
    return pl.pallas_call(
        kernel,
        out_shape=out_shape,
        **specs,
        scratch_shapes=list(scratch),
        compiler_params=pltpu.CompilerParams(vmem_limit_bytes=limit << 20),
        cost_estimate=pl.CostEstimate(flops=flops, bytes_accessed=1 << 20, transcendentals=0),
    )


def shape(dims, dtype):
    return jax.ShapeDtypeStruct(dims, dtype)


ON_HBM = pl.BlockSpec(memory_space=pltpu.HBM)
ON_VMEM = pl.BlockSpec(memory_space=pltpu.VMEM)


def passed_places(length, wide, narrow):
    bins = 2 * (HALF + 1) * (2 * length // RADIX)
    parts = [wide.at[pl.ds(0, bins), :]]
    parts += [wide.at[pl.ds(bins + index * length, length), :] for index in range(3)]
    parts += [narrow.at[pl.ds(128 * index, 128), :] for index in range(4)]
    return parts + [narrow.at[pl.ds(512, 384), pl.ds(128 * index, 128)] for index in range(2)]


def passed_shapes(length):
    bins = 2 * (HALF + 1) * (2 * length // RADIX)
    return [shape((bins + 3 * length, 128), F32), shape((512 + 384, length), BF16)]


def held_arrays(length):
    bins = 2 * (HALF + 1) * (2 * length // RADIX)
    held = [pltpu.VMEM((bins, 128), F32)] + [pltpu.VMEM((length, 128), F32)] * 3
    held += [pltpu.VMEM((128, length), BF16)] * 4 + [pltpu.VMEM((384, 128), BF16)] * 2
    return held + [pltpu.SemaphoreType.DMA((len(held),))]


def spectrum_call(length, *operands):
    inner = 2 * length // RADIX
    return call(
        functools.partial(kernel_spectrum_kernel, length),
        passed_shapes(length),
        scratch=held_arrays(length)
        + [pltpu.VMEM((length, 128), F32), pltpu.VMEM((HALF + 1, 3 * inner, 256), BF16)],
        flops=4 << 30,
        limit=FIRST_LIMIT,
        out_specs=[ON_HBM] * 2,
    )(*operands)


def gradient_call(length, *operands):
    inner = 2 * length // RADIX
    local_rows = 128
    return call(
        functools.partial(gradient_kernel, length),
        shape((length // local_rows, local_rows // 2 + 64, 128), BF16),
        scratch=held_arrays(length)
        + [
            pltpu.VMEM((HALF + 1, 3 * inner, 256), BF16),
            pltpu.VMEM((HALF + 1, inner, 256), F32),
        ]
        + [pltpu.VMEM((length, 128), BF16)] * 4,
        flops=8 << 30,
        limit=SECOND_LIMIT,
        in_specs=[ON_VMEM] + [ON_HBM] * 2 + [ON_VMEM] * 2,
    )(*operands)


def by_channels(tokens_in, grad_out, decay_rate, w_in, b_in, w_mid, w_out):
    devices = lax.axis_size("ctx")
    local_rows = tokens_in.shape[0]
    length = local_rows * devices
    matrix, twiddle = dft_tables(2 * length)
    packed = call(
        pack_kernel,
        shape((devices, local_rows, 128), BF16),
        scratch=[pltpu.VMEM(tokens_in.shape, BF16)] * 2 + [pltpu.SemaphoreType.DMA((2,))],
        limit=58,
        in_specs=[ON_HBM] * 2,
    )(tokens_in, grad_out)
    signal = lax.all_to_all(packed, "ctx", split_axis=0, concat_axis=0, tiled=True)
    forward = spectrum_call(
        length, decay_rate.reshape(1, -1), w_in.reshape(1, -1), b_in.reshape(1, -1), w_mid, w_out,
        matrix, twiddle,
    )
    sent = gradient_call(length, signal.reshape(length, 128), *forward, matrix, twiddle)
    received = lax.all_to_all(sent, "ctx", split_axis=0, concat_axis=0, tiled=True)
    half, joined = call(
        sums_kernel, [shape((32, 64 * devices + 128), BF16), shape((16, 128), F32)]
    )(received)
    other = lax.ppermute(half, "ctx", [(index, index ^ 1) for index in range(devices)])
    input_grad = call(tokens_kernel, shape(tokens_in.shape, BF16), flops=1 << 26)(received)
    grad_first, grad_bias, grad_mid, grad_last = call(
        functools.partial(weights_kernel, 1.0 / math.sqrt(length)),
        [shape((1, 64), F32), shape((1, 64), F32), shape((64, 64), F32), shape(w_out.shape, F32)],
    )(joined, half, other)
    return input_grad, grad_first.reshape(64), grad_bias.reshape(64), grad_mid, grad_last


HIGHEST = lax.Precision.HIGHEST
TWO_PI = 2.0 * math.pi


def phase_angle(product, period):
    return TWO_PI / period * (product % period).astype(jnp.float32)


def frequency_rows(devices):
    row_index = jnp.arange(2 * devices, dtype=jnp.int32)
    row_block = row_index // 2
    second = row_index % 2
    paired = jnp.where(row_block == 0, devices, 2 * devices - row_block)
    return jnp.where(second == 0, row_block, paired)


def source_rows(devices):
    row_index = jnp.arange(2 * devices, dtype=jnp.int32)
    return row_index // 2 + row_index % 2 * devices


def envelope(lag_values, decay_rate, length):
    double = 2.0 * decay_rate
    geometric = 1.0 + 2.0 * jnp.exp(-double) * jnp.expm1(-double * (length - 1)) / jnp.expm1(
        -double
    )
    distance = jnp.abs(lag_values).astype(jnp.float32)[..., None]
    live_mask = (lag_values != -length).astype(jnp.float32)[..., None]
    return live_mask * lax.rsqrt(geometric) * jnp.exp(-distance * decay_rate)


def position_mlp(scaled, w_first, w_bias, w_middle, w_last):
    hidden_one = jax.nn.silu(scaled[..., None] * w_first + w_bias)
    hidden_two = jax.nn.silu(jnp.dot(hidden_one, w_middle, precision=HIGHEST))
    return jnp.dot(hidden_two, w_last, precision=HIGHEST)


def rotate(real_a, imag_a, real_b, imag_b):
    return (real_a * real_b - imag_a * imag_b, real_a * imag_b + imag_a * real_b)


def first_section(signal, columns, freq_order, local_slab, padded):
    freq_count = freq_order.shape[0]
    angles = phase_angle(freq_order[:, None] * columns[None, :], freq_count)
    real_part = jnp.einsum("fp,prc->frc", jnp.cos(angles), signal, precision=HIGHEST)
    imag_part = jnp.einsum("fp,prc->frc", -jnp.sin(angles), signal, precision=HIGHEST)
    twiddle = phase_angle(freq_order[:, None] * local_slab[None, :], padded)[:, :, None]
    return rotate(real_part, imag_part, jnp.cos(twiddle), -jnp.sin(twiddle))


def along_rows(stacked, direction):
    row_count = stacked.shape[1]
    half_width = stacked.shape[2] // 2
    positions = jnp.arange(row_count, dtype=jnp.int32)
    angles = phase_angle(positions[:, None] * positions[None, :], row_count)
    with_cos = jnp.einsum("gm,imc->igc", jnp.cos(angles), stacked, precision=HIGHEST)
    with_sin = jnp.einsum("gm,imc->igc", direction * jnp.sin(angles), stacked, precision=HIGHEST)
    real_part = with_cos[..., :half_width] - with_sin[..., half_width:]
    imag_part = with_cos[..., half_width:] + with_sin[..., :half_width]
    return (real_part, imag_part)


def last_section(stacked, out_rows, freq_order, padded):
    freq_count = freq_order.shape[0]
    half_width = stacked.shape[2] // 2
    angles = phase_angle(out_rows[:, None] * freq_order[None, :], freq_count)
    cos_table = jnp.cos(angles) / padded
    sin_table = jnp.sin(angles) / padded
    real_in = stacked[..., :half_width]
    imag_in = stacked[..., half_width:]
    leading, trailing, factor = (real_in, imag_in, -1.0)
    return jnp.einsum("pf,frc->prc", cos_table, leading, precision=HIGHEST) + factor * jnp.einsum(
        "pf,frc->prc", sin_table, trailing, precision=HIGHEST
    )


def by_frequencies(tokens_in, grad_out, decay_rate, w_in, b_in, w_mid, w_out):
    devices = lax.axis_size("ctx")
    own_index = lax.axis_index("ctx")
    tok_rows = tokens_in.shape[0]
    slab_rows = tok_rows // devices
    length = tok_rows * devices
    padded = 2 * length
    freq_order = frequency_rows(devices)
    lag_rows = source_rows(devices)
    token_cols = jnp.arange(devices, dtype=jnp.int32)
    local_slab = own_index * slab_rows + jnp.arange(slab_rows, dtype=jnp.int32)
    pair_index = jnp.arange(2, dtype=jnp.int32)
    local_freq = jnp.where(
        pair_index == 0, own_index, jnp.where(own_index == 0, devices, 2 * devices - own_index)
    )
    circular = (own_index + pair_index * devices)[:, None] * tok_rows + jnp.arange(
        tok_rows, dtype=jnp.int32
    )[None, :]
    lag_values = jnp.where(circular < length, circular, circular - padded)
    scaled = lag_values.astype(jnp.float32) / length
    weights_env = envelope(lag_values, decay_rate, length)

    def position_net(w_first, w_bias, w_middle, w_last):
        return position_mlp(scaled, w_first, w_bias, w_middle, w_last)

    position, pull_back = jax.vjp(position_net, w_in, b_in, w_mid, w_out)
    kernel = (position * weights_env).astype(jnp.bfloat16)
    tokens_mid, grads_mid, kernel_mid = (
        lax.all_to_all(tokens_in[None], "ctx", split_axis=1, concat_axis=0, tiled=True),
        lax.all_to_all(grad_out[None], "ctx", split_axis=1, concat_axis=0, tiled=True),
        lax.all_to_all(kernel, "ctx", split_axis=1, concat_axis=0, tiled=True),
    )
    token_real, token_imag = first_section(
        tokens_mid.astype(jnp.float32), token_cols, freq_order, local_slab, padded
    )
    cotan_real, cotan_imag = first_section(
        grads_mid.astype(jnp.float32), token_cols, freq_order, local_slab, padded
    )
    kern_real, kern_imag = first_section(
        kernel_mid.astype(jnp.float32), lag_rows, freq_order, local_slab, padded
    )
    kernel_stack = jnp.concatenate([kern_real, kern_imag], axis=2)
    token_stack = jnp.concatenate([token_real, token_imag], axis=2)
    cotan_stack = jnp.concatenate([cotan_real, cotan_imag], axis=2)
    token_spec, cotan_spec, kernel_spec = (
        lax.all_to_all(token_stack, "ctx", split_axis=0, concat_axis=1, tiled=True),
        lax.all_to_all(cotan_stack, "ctx", split_axis=0, concat_axis=1, tiled=True),
        lax.all_to_all(kernel_stack, "ctx", split_axis=0, concat_axis=1, tiled=True),
    )
    spec_token_real, spec_token_imag = along_rows(token_spec, -1.0)
    spec_cotan_real, spec_cotan_imag = along_rows(cotan_spec, -1.0)
    spec_kern_real, spec_kern_imag = along_rows(kernel_spec, -1.0)
    input_real = spec_kern_real * spec_cotan_real + spec_kern_imag * spec_cotan_imag
    input_imag = spec_kern_real * spec_cotan_imag - spec_kern_imag * spec_cotan_real
    lagged_real = spec_cotan_real * spec_token_real + spec_cotan_imag * spec_token_imag
    lagged_imag = spec_cotan_imag * spec_token_real - spec_cotan_real * spec_token_imag
    positions = jnp.arange(tok_rows, dtype=jnp.int32)
    back_angle = phase_angle(local_freq[:, None] * positions[None, :], padded)[:, :, None]
    back_cos = jnp.cos(back_angle)
    back_sin = jnp.sin(back_angle)

    def inverse_rows(real_part, imag_part):
        stacked = jnp.concatenate([real_part, imag_part], axis=2)
        out_real, out_imag = along_rows(stacked, 1.0)
        turned_real, turned_imag = rotate(out_real, out_imag, back_cos, back_sin)
        return jnp.concatenate([turned_real, turned_imag], axis=2)

    spread_input, spread_lagged = (
        lax.all_to_all(
            inverse_rows(input_real, input_imag), "ctx", split_axis=1, concat_axis=0, tiled=True
        ),
        lax.all_to_all(
            inverse_rows(lagged_real, lagged_imag), "ctx", split_axis=1, concat_axis=0, tiled=True
        ),
    )
    input_rows = last_section(spread_input, token_cols, freq_order, padded)
    lagged_rows = last_section(spread_lagged, lag_rows, freq_order, padded)
    input_back, lag_back = (
        lax.all_to_all(input_rows, "ctx", split_axis=0, concat_axis=1, tiled=True),
        lax.all_to_all(lagged_rows, "ctx", split_axis=0, concat_axis=1, tiled=True),
    )
    input_grad = input_back[0]
    gradients = pull_back(lag_back * weights_env)
    summed = lax.psum((gradients[0], gradients[1], gradients[2], gradients[3]), "ctx")
    loss_scale = 1.0 / math.sqrt(length)
    return (
        input_grad.astype(jnp.bfloat16),
        summed[0] * loss_scale,
        summed[1] * loss_scale,
        summed[2] * loss_scale,
        summed[3] * loss_scale,
    )


def on_device(tokens_in, grad_out, decay_rate, w_in, b_in, w_mid, w_out):
    devices = lax.axis_size("ctx")
    fits = (
        tokens_in.shape == (128, 64 * devices)
        and devices % 2 == 0
        and devices * 128 % (128 * HALF) == 0
        and w_mid.shape == (64, 64)
    )
    form = by_channels if fits else by_frequencies
    return form(tokens_in, grad_out, decay_rate, w_in, b_in, w_mid, w_out)


def solution(mesh):
    in_specs = (P(("groups", "ctx"), None), P(("groups", "ctx"), None), P(), P(), P(), P(), P())
    out_specs = (
        P(("groups", "ctx"), None),
        P("groups"),
        P("groups"),
        P("groups", None),
        P("groups", None),
    )
    return jax.shard_map(
        on_device, mesh=mesh, in_specs=in_specs, out_specs=out_specs, check_vma=False
    )
```

```python
import functools
import math

import jax
import jax.numpy as jnp
import numpy as np
from jax import lax
from jax.experimental import pallas as pl
from jax.experimental.pallas import tpu as pltpu
from jax.sharding import PartitionSpec as P

RADIX = 16
HALF = RADIX // 2
CHUNK = 32
UNROLL_CHUNK = 8
UNROLL_BIN = 9
UNROLL_ROWS = 8
PACK_PARTS = 4
FIRST_LIMIT = 56
SECOND_LIMIT = 50
F32 = jnp.float32
BF16 = jnp.bfloat16


def split_pair(value):
    high = value.astype(BF16)
    return high, (value - high.astype(F32)).astype(BF16)


def dot(left, right):
    return jnp.dot(left, right, preferred_element_type=F32)


def wide_three(value):
    high, low = split_pair(value)
    return jnp.concatenate([high, low, high], axis=1)


def tall_three(value):
    high, low = split_pair(value)
    return jnp.concatenate([high, high, low], axis=0)


def dft_tables(padded):
    inner = padded // RADIX
    grid = np.outer(np.arange(inner), np.arange(inner)) % inner
    angles = 2.0 * np.pi * grid / inner
    matrix = np.concatenate([np.cos(angles), np.sin(angles)], axis=0)
    high = matrix.astype(jnp.bfloat16)
    low = (matrix - high.astype(np.float64)).astype(jnp.bfloat16)
    matrix = np.concatenate([high, low, high], axis=1)
    turn = 2.0 * np.pi * np.outer(np.arange(inner), np.arange(RADIX)) / padded
    twiddle = np.zeros((inner, 128), np.float32)
    twiddle[:, :RADIX] = np.cos(turn)
    twiddle[:, RADIX : 2 * RADIX] = np.sin(turn)
    return jnp.asarray(matrix), jnp.asarray(twiddle)


def cos_of(index):
    return math.cos(2.0 * math.pi * index / RADIX)


def sin_of(index):
    return math.sin(2.0 * math.pi * index / RADIX)


def spread(x):
    plus = [x[q] + x[q + 4] for q in range(4)]
    minus = [x[q] - x[q + 4] for q in range(4)]
    root = math.sqrt(0.5)
    out = [None] * 9
    even, odd = plus[0] + plus[2], plus[1] + plus[3]
    out[0] = (even + odd, None)
    out[8] = (even - odd, None)
    out[4] = (plus[0] - plus[2], plus[3] - plus[1])
    across, along = root * (minus[1] - minus[3]), root * (minus[1] + minus[3])
    out[2] = (minus[0] + across, -minus[2] - along)
    out[6] = (minus[0] - across, minus[2] - along)
    differ = {q: x[q] - x[8 - q] for q in (1, 2, 3)}
    same = {q: x[q] + x[8 - q] for q in (1, 2, 3)}
    for j in (1, 3):
        real_even = x[0] + cos_of(2 * j) * differ[2]
        real_odd = cos_of(j) * differ[1] + cos_of(3 * j) * differ[3]
        imag_even = sin_of(4 * j) * x[4] + sin_of(2 * j) * same[2]
        imag_odd = sin_of(j) * same[1] + sin_of(3 * j) * same[3]
        out[j] = (real_even + real_odd, -(imag_odd + imag_even))
        out[8 - j] = (real_even - real_odd, imag_even - imag_odd)
    return out


def gather_back(real, imag):
    even, odd = [None] * 8, [None] * 8
    total, differ = real[0] + real[8], real[0] - real[8]
    real_sum, real_dif = real[2] + real[6], real[2] - real[6]
    imag_sum, imag_dif = imag[2] + imag[6], imag[2] - imag[6]
    root = math.sqrt(0.5)
    even[0] = total + real_sum + real[4]
    even[4] = total - real_sum + real[4]
    even[2] = total - imag_dif - real[4]
    even[6] = total + imag_dif - real[4]
    first, second = root * (real_dif - imag_sum), root * (real_dif + imag_sum)
    even[1] = differ + first - imag[4]
    even[5] = differ - first - imag[4]
    even[3] = differ - second + imag[4]
    even[7] = differ + second + imag[4]
    one_sum, one_dif = real[1] + real[7], real[1] - real[7]
    three_sum, three_dif = real[3] + real[5], real[3] - real[5]
    ione_sum, ione_dif = imag[1] + imag[7], imag[1] - imag[7]
    ithree_sum, ithree_dif = imag[3] + imag[5], imag[3] - imag[5]
    odd[0] = one_sum + three_sum
    odd[4] = ithree_dif - ione_dif
    for q in (1, 2, 3):
        if q % 2 == 0:
            cosines = cos_of(q) * one_sum + cos_of(3 * q) * three_sum
            sines = sin_of(q) * ione_dif + sin_of(3 * q) * ithree_dif
        else:
            cosines = cos_of(q) * one_dif + cos_of(3 * q) * three_dif
            sines = sin_of(q) * ione_sum + sin_of(3 * q) * ithree_sum
        odd[q] = cosines - sines
        odd[8 - q] = -cosines - sines
    return even, odd


def residues_to_scratch(load, twiddle, stage, inner):
    def chunk(step, carry):
        start = pl.multiple_of(step * CHUNK, CHUNK)
        turn = twiddle[pl.ds(start, CHUNK), :]
        for j, (real, imag) in enumerate(spread([load(q * inner + start) for q in range(HALF)])):
            if j > 0:
                cosine, sine = turn[:, j : j + 1], turn[:, RADIX + j : RADIX + j + 1]
                if imag is None:
                    real, imag = real * cosine, -real * sine
                else:
                    real, imag = real * cosine + imag * sine, imag * cosine - real * sine
            else:
                imag = jnp.zeros_like(real)
            for part, value in enumerate((real, imag)):
                high, low = split_pair(value)
                lanes = slice(128 * part, 128 * part + 128)
                stage[j, pl.ds(start, CHUNK), lanes] = high
                stage[j, pl.ds(inner + start, CHUNK), lanes] = high
                stage[j, pl.ds(2 * inner + start, CHUNK), lanes] = low
        return carry

    lax.fori_loop(0, inner // CHUNK, chunk, 0, unroll=UNROLL_CHUNK)


def inner_dft(stacked, matrix, inner, direction):
    product = dot(matrix[...], stacked)
    cos_real, cos_imag = product[:inner, :128], product[:inner, 128:]
    sin_real, sin_imag = product[inner:, :128], product[inner:, 128:]
    if direction > 0:
        return cos_real + sin_imag, cos_imag - sin_real
    return cos_real - sin_imag, cos_imag + sin_real


def low_lanes(rows):
    return lax.broadcasted_iota(jnp.int32, (rows, 128), 1) < 64


def swap(value):
    return pltpu.roll(value, 64, 1)


def fetch(sources, buffers, semaphores):
    copies = [
        pltpu.make_async_copy(source, buffer, semaphores.at[index])
        for index, (source, buffer) in enumerate(zip(sources, buffers))
    ]
    for copy in copies:
        copy.start()
    return copies


def pack_kernel(tokens_hbm, cotan_hbm, out_hbm, tokens, cotan, out, load_semaphores, store_semaphores):
    loads, stores = [], []
    rows_each = tokens.shape[0] // PACK_PARTS
    for part in range(PACK_PARTS):
        rows = pl.ds(part * rows_each, rows_each)
        loads.append(
            fetch(
                (tokens_hbm.at[rows, :], cotan_hbm.at[rows, :]),
                (tokens.at[rows, :], cotan.at[rows, :]),
                load_semaphores.at[part],
            )
        )
    for part in range(PACK_PARTS):
        rows = pl.ds(part * rows_each, rows_each)
        for copy in loads[part]:
            copy.wait()
        for block in range(out.shape[0]):
            lanes = slice(64 * block, 64 * block + 64)
            out[block, rows, :] = jnp.concatenate([tokens[rows, lanes], cotan[rows, lanes]], axis=1)
        store = pltpu.make_async_copy(
            out.at[:, rows, :], out_hbm.at[:, rows, :], store_semaphores.at[part]
        )
        store.start()
        stores.append(store)
    for store in stores:
        store.wait()


def diagonal(matrix):
    empty = jnp.zeros_like(matrix)
    return jnp.concatenate(
        [jnp.concatenate([matrix, empty], axis=1), jnp.concatenate([empty, matrix], axis=1)], axis=0
    )


def twice(row):
    return jnp.concatenate([row, row], axis=1)


def exp_minus_one(value):
    series = jnp.ones_like(value)
    for order in range(9, 1, -1):
        series = 1.0 + series * value * (1.0 / order)
    return jnp.where(jnp.abs(value) < 0.35, value * series, jnp.exp(value) - 1.0)


def kernel_spectrum_kernel(
    length, rates, w_first, w_bias, w_mid, w_last, matrix, twiddle, wide_hbm, narrow_hbm,
    spectrum, slope_two, consts, two_high, two_low, mid_back, last_back, semaphores, taps, stage,
):
    inner = 2 * length // RADIX
    low_half = low_lanes(inner)
    own = lax.axis_index("ctx")
    lanes = pl.ds(pl.multiple_of(own // 2 * 128, 128), 128)
    odd = own % 2 == 1
    last = w_last[:, lanes]
    last = diagonal(jnp.where(odd, swap(last), last)[:, 0:64])
    rate = rates[:, lanes]
    rate = twice(jnp.where(odd, swap(rate), rate)[:, 0:64])
    double = 2.0 * rate
    ratio = exp_minus_one(-double * (length - 1)) / exp_minus_one(-double)
    geometric = 1.0 + 2.0 * jnp.exp(-double) * ratio
    scale = lax.rsqrt(geometric)
    mid = diagonal(w_mid[...])
    mid_back[...] = tall_three(mid.T)
    last_back[...] = tall_three(last.T)
    mid, last = tall_three(mid), tall_three(last)
    first, bias = twice(w_first[...]), twice(w_bias[...])
    consts[...] = jnp.concatenate([rate, scale, first, bias, jnp.zeros((4, 128), F32)], axis=0)

    def block(step, carry):
        start = pl.multiple_of(step * inner, inner)
        rows = pl.ds(start, inner)
        place = start + lax.broadcasted_iota(jnp.int32, (inner, 128), 0)
        lag = jnp.where(low_half, place, place - length)
        scaled = lag.astype(F32) / length
        pre_one = scaled * first + bias
        gate_one = 1.0 / (1.0 + jnp.exp(-pre_one))
        hidden_one = pre_one * gate_one
        pre_two = dot(wide_three(hidden_one), mid)
        gate_two = 1.0 / (1.0 + jnp.exp(-pre_two))
        hidden_two = pre_two * gate_two
        slope_two[rows, :] = gate_two * (1.0 + pre_two * (1.0 - gate_two))
        position = dot(wide_three(hidden_two), last)
        live = jnp.where(lag == -length, 0.0, 1.0)
        env = live * scale * jnp.exp(-jnp.abs(lag).astype(F32) * rate)
        taps[rows, :] = (position * env).astype(BF16).astype(F32)
        two_high[:, rows], two_low[:, rows] = split_pair(hidden_two.T)
        return carry

    lax.fori_loop(0, HALF, block, 0, unroll=UNROLL_ROWS)
    places = passed_places(length, wide_hbm, narrow_hbm)
    held = (slope_two, consts, two_high, two_low, mid_back, last_back)
    copies = fetch(held, places[1:], semaphores)
    residues_to_scratch(lambda start: taps[pl.ds(start, CHUNK), :], twiddle, stage, inner)

    def transform(j, carry):
        real, imag = inner_dft(stage[j], matrix, inner, 1)
        sign = 1.0 - 2.0 * lax.rem(jnp.asarray(j, jnp.int32), 2).astype(F32)
        spectrum[pl.ds((2 * j + 0) * inner, inner), :] = real + sign * swap(real)
        spectrum[pl.ds((2 * j + 1) * inner, inner), :] = imag + sign * swap(imag)
        return carry

    lax.fori_loop(0, HALF + 1, transform, 0, unroll=UNROLL_BIN)
    last_copy = pltpu.make_async_copy(spectrum, places[0], semaphores.at[len(copies)])
    last_copy.start()
    for copy in copies + [last_copy]:
        copy.wait()


def gradient_kernel(
    length, signal, wide_hbm, narrow_hbm, matrix, twiddle, out,
    spectrum, slope_two, consts, two_high, two_low, mid_back, last_back, semaphores, stage, back_ref, slope_high, slope_low, pre_high, pre_low,
    one_high, one_low, decay,
):
    padded = 2 * length
    inner = padded // RADIX
    low_half = low_lanes(inner)
    held = (spectrum, slope_two, consts, two_high, two_low, mid_back, last_back)
    copies = fetch(passed_places(length, wide_hbm, narrow_hbm), held, semaphores)
    residues_to_scratch(
        lambda start: signal[pl.ds(start, CHUNK), :].astype(F32), twiddle, stage, inner
    )
    copies[0].wait()

    def transform(j, carry):
        real, imag = inner_dft(stage[j], matrix, inner, 1)
        real_swap, imag_swap = swap(real), swap(imag)
        cotan_real = jnp.where(low_half, real_swap, real)
        cotan_imag = jnp.where(low_half, imag_swap, imag)
        other_real = jnp.where(low_half, spectrum[pl.ds((2 * j + 0) * inner, inner), :], real_swap)
        other_imag = jnp.where(low_half, spectrum[pl.ds((2 * j + 1) * inner, inner), :], imag_swap)
        product = jnp.concatenate(
            [
                cotan_real * other_real + cotan_imag * other_imag,
                cotan_imag * other_real - cotan_real * other_imag,
            ],
            axis=1,
        )
        real, imag = inner_dft(tall_three(product), matrix, inner, -1)
        back_ref[j, :, 0:128] = real
        back_ref[j, :, 128:256] = imag
        return carry

    lax.fori_loop(0, HALF + 1, transform, 0, unroll=UNROLL_BIN)
    for copy in copies[1:]:
        copy.wait()
    rate, scale, first, bias = (consts[index : index + 1, :] for index in range(4))
    place = lax.broadcasted_iota(jnp.int32, (inner, 128), 0)
    near = jnp.where(low_half, place, inner - 1 - place).astype(F32)
    decay[...] = jnp.exp(-near * rate)
    low_row = low_lanes(1)

    def unspread(step, carry):
        start = pl.multiple_of(step * CHUNK, CHUNK)
        rows = pl.ds(start, CHUNK)
        turn = twiddle[rows, :]
        real_list, imag_list = [], []
        for j in range(HALF + 1):
            weight = (1.0 if j in (0, HALF) else 2.0) / padded
            real, imag = back_ref[j, rows, 0:128], back_ref[j, rows, 128:256]
            if j == 0:
                real_list.append(real * weight)
                imag_list.append(None)
                continue
            cosine = turn[:, j : j + 1] * weight
            sine = turn[:, RADIX + j : RADIX + j + 1] * weight
            real_list.append(real * cosine - imag * sine)
            imag_list.append(real * sine + imag * cosine)
        even, odd = gather_back(real_list, imag_list)
        for q in range(HALF):
            joined, apart = even[q] + odd[q], even[q] - odd[q]
            back_ref[q, rows, 0:128] = joined
            at = pl.ds(q * inner + start, CHUNK)
            lag_grad = jnp.where(low_lanes(CHUNK), swap(joined), apart)
            far = jnp.where(low_row, q * inner, length - q * inner - inner + 1).astype(F32)
            weighted = lag_grad * (scale * jnp.exp(-far * rate)) * decay[rows, :]
            if q == 0:
                row = start + lax.broadcasted_iota(jnp.int32, (CHUNK, 128), 0)
                weighted = jnp.where((row == 0) & ~low_lanes(CHUNK), 0.0, weighted)
            slope_high[at, :], slope_low[at, :] = split_pair(weighted)
        return carry

    lax.fori_loop(0, inner // CHUNK, unspread, 0, unroll=UNROLL_CHUNK)
    local_rows = 128
    rise = jnp.exp(place.astype(F32) * (first * (-1.0 / length)))
    first_column = jnp.broadcast_to(first, (8, 128)).T[:, 0:1]
    bias_column = jnp.broadcast_to(bias, (8, 128)).T[:, 0:1]
    along = lax.broadcasted_iota(jnp.int32, (128, inner), 1)
    low_column = lax.broadcasted_iota(jnp.int32, (128, 1), 0) < 64
    rise_across = jnp.exp(along.astype(F32) * (first_column * (-1.0 / length)))
    half_rows = local_rows // 2

    def block(q, carry):
        first_sum, bias_sum = carry
        start = pl.multiple_of(q * inner, inner)
        rows = pl.ds(start, inner)
        for part in range(inner // local_rows):
            base = part * local_rows
            upper = back_ref[q, base : base + half_rows, 0:128]
            lower = back_ref[q, base + half_rows : base + local_rows, 0:128]
            out[q * (inner // local_rows) + part, 0:half_rows, :] = jnp.where(
                low_half[:half_rows], upper, swap(lower)
            ).astype(BF16)
        high, low = slope_high[rows, :], slope_low[rows, :]
        slope = jnp.concatenate([high, low, high], axis=1)
        high, low = split_pair(dot(slope, last_back[...]) * slope_two[rows, :])
        pre_high[rows, :], pre_low[rows, :] = high, low
        pre_two = jnp.concatenate([high, low, high], axis=1)
        base = jnp.where(low_row, start, start - length)
        scaled = (place + base).astype(F32) * (1.0 / length)
        before = scaled * first + bias
        gate = 1.0 / (1.0 + rise * jnp.exp(-(base.astype(F32) * (1.0 / length) * first + bias)))
        slope_one = gate * (1.0 + before * (1.0 - gate))
        base = jnp.where(low_column, start, start - length)
        across = (along + base).astype(F32) * (1.0 / length) * first_column + bias_column
        offset = base.astype(F32) * (1.0 / length) * first_column + bias_column
        across = across * (1.0 / (1.0 + rise_across * jnp.exp(-offset)))
        one_high[:, rows], one_low[:, rows] = split_pair(across)
        pre_one = dot(pre_two, mid_back[...]) * slope_one
        first_sum = first_sum + jnp.sum((pre_one * scaled).reshape(inner // 8, 8, 128), axis=0)
        bias_sum = bias_sum + jnp.sum(pre_one.reshape(inner // 8, 8, 128), axis=0)
        return first_sum, bias_sum

    none = jnp.zeros((8, 128), F32)
    first_sum, bias_sum = lax.fori_loop(0, HALF, block, (none, none), unroll=UNROLL_ROWS)
    last_sum = dot(two_high[...], slope_high[...]) + (
        dot(two_low[...], slope_high[...]) + dot(two_high[...], slope_low[...])
    )
    mid_sum = dot(one_high[...], pre_high[...]) + (
        dot(one_low[...], pre_high[...]) + dot(one_high[...], pre_low[...])
    )
    low_32 = low_lanes(32)
    grad_last = last_sum[0:64] + swap(last_sum[64:128])
    last_rows = jnp.where(low_32, grad_last[0:32], swap(grad_last[32:64]))
    grad_mid = mid_sum[0:64] + swap(mid_sum[64:128])
    mid_rows = jnp.where(low_32, grad_mid[0:32], swap(grad_mid[32:64]))
    first = jnp.sum(first_sum, axis=0, keepdims=True)
    bias = jnp.sum(bias_sum, axis=0, keepdims=True)
    first = first + swap(first)
    bias = bias + swap(bias)
    joined = jnp.where(low_lanes(1), first, bias)
    joined_high = joined.astype(BF16).astype(F32)
    row_index = lax.broadcasted_iota(jnp.int32, (8, 128), 0)
    joined_rows = jnp.where(
        row_index == 0, joined_high, jnp.where(row_index == 1, joined - joined_high, 0.0)
    )
    for device in range(out.shape[0]):
        half = slice(16 * (device % 2), 16 * (device % 2) + 16)
        tail = [last_rows[half], mid_rows[half], joined_rows]
        out[device, half_rows:, :] = jnp.concatenate(tail, axis=0).astype(BF16)


def sums_kernel(received, half, joined_out):
    half_rows = received.shape[1] - 40
    mid = jnp.zeros((16, 128), F32)
    joined = jnp.zeros((8, 128), F32)
    for source in range(received.shape[0]):
        lanes = slice(64 * source, 64 * source + 64)
        last = received[source, half_rows : half_rows + 16, :]
        half[0:16, lanes] = last[:, 0:64]
        half[16:32, lanes] = last[:, 64:128]
        mid = mid + received[source, half_rows + 16 : half_rows + 32, :].astype(F32)
        joined = joined + received[source, half_rows + 32 : half_rows + 40, :].astype(F32)
    mid = jnp.concatenate([mid, swap(mid)], axis=0)
    high = mid.astype(BF16).astype(F32)
    columns = 64 * received.shape[0]
    rest = swap(mid - high)
    half[:, columns : columns + 128] = jnp.where(low_lanes(32), high, rest).astype(BF16)
    joined_out[...] = joined


def tokens_kernel(received, grad_tokens):
    half_rows = grad_tokens.shape[0] // 2
    for source in range(received.shape[0]):
        lanes = slice(64 * source, 64 * source + 64)
        tile = received[source, 0:half_rows, :]
        grad_tokens[0:half_rows, lanes] = tile[:, 0:64]
        grad_tokens[half_rows:, lanes] = tile[:, 64:128]


def weights_kernel(loss_scale, joined, mine, other, grad_first, grad_bias, grad_mid, grad_last):
    odd = lax.rem(lax.axis_index("ctx"), 2)
    columns = grad_last.shape[1]
    for source, parity in ((mine, odd), (other, 1 - odd)):
        last = source[:, 0:columns].astype(F32) * loss_scale
        grad_last[pl.ds(pl.multiple_of(16 * parity, 16), 16), :] = last[0:16]
        grad_last[pl.ds(pl.multiple_of(32 + 16 * parity, 16), 16), :] = last[16:32]
        mid = source[:, columns : columns + 128].astype(F32) * loss_scale
        mid = (mid + swap(mid))[:, 0:64]
        grad_mid[pl.ds(pl.multiple_of(16 * parity, 16), 16), :] = mid[0:16]
        grad_mid[pl.ds(pl.multiple_of(32 + 16 * parity, 16), 16), :] = mid[16:32]
    first = (joined[0:1] + joined[1:2]) * loss_scale
    grad_first[...] = first[:, 0:64]
    grad_bias[...] = first[:, 64:128]


def call(kernel, out_shape, scratch=(), flops=0, limit=24, **specs):
    return pl.pallas_call(
        kernel,
        out_shape=out_shape,
        **specs,
        scratch_shapes=list(scratch),
        compiler_params=pltpu.CompilerParams(vmem_limit_bytes=limit << 20),
        cost_estimate=pl.CostEstimate(flops=flops, bytes_accessed=1 << 20, transcendentals=0),
    )


def shape(dims, dtype):
    return jax.ShapeDtypeStruct(dims, dtype)


ON_HBM = pl.BlockSpec(memory_space=pltpu.HBM)
ON_VMEM = pl.BlockSpec(memory_space=pltpu.VMEM)


def passed_places(length, wide, narrow):
    bins = 2 * (HALF + 1) * (2 * length // RADIX)
    parts = [wide.at[pl.ds(0, bins), :], wide.at[pl.ds(bins, length), :]]
    parts += [wide.at[pl.ds(bins + length, 8), :]]
    parts += [narrow.at[pl.ds(128 * index, 128), :] for index in range(2)]
    return parts + [narrow.at[pl.ds(256, 384), pl.ds(128 * index, 128)] for index in range(2)]


def passed_shapes(length):
    bins = 2 * (HALF + 1) * (2 * length // RADIX)
    return [shape((bins + length + 8, 128), F32), shape((256 + 384, length), BF16)]


def held_arrays(length):
    bins = 2 * (HALF + 1) * (2 * length // RADIX)
    held = [pltpu.VMEM((rows, 128), F32) for rows in (bins, length, 8)]
    held += [pltpu.VMEM((128, length), BF16)] * 2 + [pltpu.VMEM((384, 128), BF16)] * 2
    return held + [pltpu.SemaphoreType.DMA((len(held),))]


def spectrum_call(length, *operands):
    inner = 2 * length // RADIX
    return call(
        functools.partial(kernel_spectrum_kernel, length),
        passed_shapes(length),
        scratch=held_arrays(length)
        + [pltpu.VMEM((length, 128), F32), pltpu.VMEM((HALF + 1, 3 * inner, 256), BF16)],
        flops=4 << 30,
        limit=FIRST_LIMIT,
        out_specs=[ON_HBM] * 2,
    )(*operands)


def gradient_call(length, *operands):
    inner = 2 * length // RADIX
    local_rows = 128
    return call(
        functools.partial(gradient_kernel, length),
        shape((length // local_rows, local_rows // 2 + 40, 128), BF16),
        scratch=held_arrays(length)
        + [
            pltpu.VMEM((HALF + 1, 3 * inner, 256), BF16),
            pltpu.VMEM((HALF + 1, inner, 256), F32),
        ]
        + [pltpu.VMEM((length, 128), BF16)] * 4
        + [pltpu.VMEM((128, length), BF16)] * 2
        + [pltpu.VMEM((inner, 128), F32)],
        flops=8 << 30,
        limit=SECOND_LIMIT,
        in_specs=[ON_VMEM] + [ON_HBM] * 2 + [ON_VMEM] * 2,
    )(*operands)


def by_channels(tokens_in, grad_out, decay_rate, w_in, b_in, w_mid, w_out):
    devices = lax.axis_size("ctx")
    local_rows = tokens_in.shape[0]
    length = local_rows * devices
    matrix, twiddle = dft_tables(2 * length)
    packed = call(
        pack_kernel,
        shape((devices, local_rows, 128), BF16),
        scratch=[pltpu.VMEM(tokens_in.shape, BF16)] * 2
        + [
            pltpu.VMEM((devices, local_rows, 128), BF16),
            pltpu.SemaphoreType.DMA((PACK_PARTS, 2)),
            pltpu.SemaphoreType.DMA((PACK_PARTS,)),
        ],
        limit=58,
        in_specs=[ON_HBM] * 2,
        out_specs=ON_HBM,
    )(tokens_in, grad_out)
    signal = lax.all_to_all(packed, "ctx", split_axis=0, concat_axis=0, tiled=True)
    forward = spectrum_call(
        length, decay_rate.reshape(1, -1), w_in.reshape(1, -1), b_in.reshape(1, -1), w_mid, w_out,
        matrix, twiddle,
    )
    sent = gradient_call(length, signal.reshape(length, 128), *forward, matrix, twiddle)
    received = lax.all_to_all(sent, "ctx", split_axis=0, concat_axis=0, tiled=True)
    half, joined = call(
        sums_kernel, [shape((32, 64 * devices + 128), BF16), shape((8, 128), F32)]
    )(received)
    other = lax.ppermute(half, "ctx", [(index, index ^ 1) for index in range(devices)])
    input_grad = call(tokens_kernel, shape(tokens_in.shape, BF16), flops=1 << 26)(received)
    grad_first, grad_bias, grad_mid, grad_last = call(
        functools.partial(weights_kernel, 1.0 / math.sqrt(length)),
        [shape((1, 64), F32), shape((1, 64), F32), shape((64, 64), F32), shape(w_out.shape, F32)],
    )(joined, half, other)
    return input_grad, grad_first.reshape(64), grad_bias.reshape(64), grad_mid, grad_last


HIGHEST = lax.Precision.HIGHEST
TWO_PI = 2.0 * math.pi


def phase_angle(product, period):
    return TWO_PI / period * (product % period).astype(jnp.float32)


def frequency_rows(devices):
    row_index = jnp.arange(2 * devices, dtype=jnp.int32)
    row_block = row_index // 2
    second = row_index % 2
    paired = jnp.where(row_block == 0, devices, 2 * devices - row_block)
    return jnp.where(second == 0, row_block, paired)


def source_rows(devices):
    row_index = jnp.arange(2 * devices, dtype=jnp.int32)
    return row_index // 2 + row_index % 2 * devices


def envelope(lag_values, decay_rate, length):
    double = 2.0 * decay_rate
    geometric = 1.0 + 2.0 * jnp.exp(-double) * jnp.expm1(-double * (length - 1)) / jnp.expm1(
        -double
    )
    distance = jnp.abs(lag_values).astype(jnp.float32)[..., None]
    live_mask = (lag_values != -length).astype(jnp.float32)[..., None]
    return live_mask * lax.rsqrt(geometric) * jnp.exp(-distance * decay_rate)


def position_mlp(scaled, w_first, w_bias, w_middle, w_last):
    hidden_one = jax.nn.silu(scaled[..., None] * w_first + w_bias)
    hidden_two = jax.nn.silu(jnp.dot(hidden_one, w_middle, precision=HIGHEST))
    return jnp.dot(hidden_two, w_last, precision=HIGHEST)


def rotate(real_a, imag_a, real_b, imag_b):
    return (real_a * real_b - imag_a * imag_b, real_a * imag_b + imag_a * real_b)


def first_section(signal, columns, freq_order, local_slab, padded):
    freq_count = freq_order.shape[0]
    angles = phase_angle(freq_order[:, None] * columns[None, :], freq_count)
    real_part = jnp.einsum("fp,prc->frc", jnp.cos(angles), signal, precision=HIGHEST)
    imag_part = jnp.einsum("fp,prc->frc", -jnp.sin(angles), signal, precision=HIGHEST)
    twiddle = phase_angle(freq_order[:, None] * local_slab[None, :], padded)[:, :, None]
    return rotate(real_part, imag_part, jnp.cos(twiddle), -jnp.sin(twiddle))


def along_rows(stacked, direction):
    row_count = stacked.shape[1]
    half_width = stacked.shape[2] // 2
    positions = jnp.arange(row_count, dtype=jnp.int32)
    angles = phase_angle(positions[:, None] * positions[None, :], row_count)
    with_cos = jnp.einsum("gm,imc->igc", jnp.cos(angles), stacked, precision=HIGHEST)
    with_sin = jnp.einsum("gm,imc->igc", direction * jnp.sin(angles), stacked, precision=HIGHEST)
    real_part = with_cos[..., :half_width] - with_sin[..., half_width:]
    imag_part = with_cos[..., half_width:] + with_sin[..., :half_width]
    return (real_part, imag_part)


def last_section(stacked, out_rows, freq_order, padded):
    freq_count = freq_order.shape[0]
    half_width = stacked.shape[2] // 2
    angles = phase_angle(out_rows[:, None] * freq_order[None, :], freq_count)
    cos_table = jnp.cos(angles) / padded
    sin_table = jnp.sin(angles) / padded
    real_in = stacked[..., :half_width]
    imag_in = stacked[..., half_width:]
    leading, trailing, factor = (real_in, imag_in, -1.0)
    return jnp.einsum("pf,frc->prc", cos_table, leading, precision=HIGHEST) + factor * jnp.einsum(
        "pf,frc->prc", sin_table, trailing, precision=HIGHEST
    )


def by_frequencies(tokens_in, grad_out, decay_rate, w_in, b_in, w_mid, w_out):
    devices = lax.axis_size("ctx")
    own_index = lax.axis_index("ctx")
    tok_rows = tokens_in.shape[0]
    slab_rows = tok_rows // devices
    length = tok_rows * devices
    padded = 2 * length
    freq_order = frequency_rows(devices)
    lag_rows = source_rows(devices)
    token_cols = jnp.arange(devices, dtype=jnp.int32)
    local_slab = own_index * slab_rows + jnp.arange(slab_rows, dtype=jnp.int32)
    pair_index = jnp.arange(2, dtype=jnp.int32)
    local_freq = jnp.where(
        pair_index == 0, own_index, jnp.where(own_index == 0, devices, 2 * devices - own_index)
    )
    circular = (own_index + pair_index * devices)[:, None] * tok_rows + jnp.arange(
        tok_rows, dtype=jnp.int32
    )[None, :]
    lag_values = jnp.where(circular < length, circular, circular - padded)
    scaled = lag_values.astype(jnp.float32) / length
    weights_env = envelope(lag_values, decay_rate, length)

    def position_net(w_first, w_bias, w_middle, w_last):
        return position_mlp(scaled, w_first, w_bias, w_middle, w_last)

    position, pull_back = jax.vjp(position_net, w_in, b_in, w_mid, w_out)
    kernel = (position * weights_env).astype(jnp.bfloat16)
    tokens_mid, grads_mid, kernel_mid = (
        lax.all_to_all(tokens_in[None], "ctx", split_axis=1, concat_axis=0, tiled=True),
        lax.all_to_all(grad_out[None], "ctx", split_axis=1, concat_axis=0, tiled=True),
        lax.all_to_all(kernel, "ctx", split_axis=1, concat_axis=0, tiled=True),
    )
    token_real, token_imag = first_section(
        tokens_mid.astype(jnp.float32), token_cols, freq_order, local_slab, padded
    )
    cotan_real, cotan_imag = first_section(
        grads_mid.astype(jnp.float32), token_cols, freq_order, local_slab, padded
    )
    kern_real, kern_imag = first_section(
        kernel_mid.astype(jnp.float32), lag_rows, freq_order, local_slab, padded
    )
    kernel_stack = jnp.concatenate([kern_real, kern_imag], axis=2)
    token_stack = jnp.concatenate([token_real, token_imag], axis=2)
    cotan_stack = jnp.concatenate([cotan_real, cotan_imag], axis=2)
    token_spec, cotan_spec, kernel_spec = (
        lax.all_to_all(token_stack, "ctx", split_axis=0, concat_axis=1, tiled=True),
        lax.all_to_all(cotan_stack, "ctx", split_axis=0, concat_axis=1, tiled=True),
        lax.all_to_all(kernel_stack, "ctx", split_axis=0, concat_axis=1, tiled=True),
    )
    spec_token_real, spec_token_imag = along_rows(token_spec, -1.0)
    spec_cotan_real, spec_cotan_imag = along_rows(cotan_spec, -1.0)
    spec_kern_real, spec_kern_imag = along_rows(kernel_spec, -1.0)
    input_real = spec_kern_real * spec_cotan_real + spec_kern_imag * spec_cotan_imag
    input_imag = spec_kern_real * spec_cotan_imag - spec_kern_imag * spec_cotan_real
    lagged_real = spec_cotan_real * spec_token_real + spec_cotan_imag * spec_token_imag
    lagged_imag = spec_cotan_imag * spec_token_real - spec_cotan_real * spec_token_imag
    positions = jnp.arange(tok_rows, dtype=jnp.int32)
    back_angle = phase_angle(local_freq[:, None] * positions[None, :], padded)[:, :, None]
    back_cos = jnp.cos(back_angle)
    back_sin = jnp.sin(back_angle)

    def inverse_rows(real_part, imag_part):
        stacked = jnp.concatenate([real_part, imag_part], axis=2)
        out_real, out_imag = along_rows(stacked, 1.0)
        turned_real, turned_imag = rotate(out_real, out_imag, back_cos, back_sin)
        return jnp.concatenate([turned_real, turned_imag], axis=2)

    spread_input, spread_lagged = (
        lax.all_to_all(
            inverse_rows(input_real, input_imag), "ctx", split_axis=1, concat_axis=0, tiled=True
        ),
        lax.all_to_all(
            inverse_rows(lagged_real, lagged_imag), "ctx", split_axis=1, concat_axis=0, tiled=True
        ),
    )
    input_rows = last_section(spread_input, token_cols, freq_order, padded)
    lagged_rows = last_section(spread_lagged, lag_rows, freq_order, padded)
    input_back, lag_back = (
        lax.all_to_all(input_rows, "ctx", split_axis=0, concat_axis=1, tiled=True),
        lax.all_to_all(lagged_rows, "ctx", split_axis=0, concat_axis=1, tiled=True),
    )
    input_grad = input_back[0]
    gradients = pull_back(lag_back * weights_env)
    summed = lax.psum((gradients[0], gradients[1], gradients[2], gradients[3]), "ctx")
    loss_scale = 1.0 / math.sqrt(length)
    return (
        input_grad.astype(jnp.bfloat16),
        summed[0] * loss_scale,
        summed[1] * loss_scale,
        summed[2] * loss_scale,
        summed[3] * loss_scale,
    )


def on_device(tokens_in, grad_out, decay_rate, w_in, b_in, w_mid, w_out):
    devices = lax.axis_size("ctx")
    fits = (
        tokens_in.shape == (128, 64 * devices)
        and devices % 2 == 0
        and devices * 128 % (128 * HALF) == 0
        and w_mid.shape == (64, 64)
    )
    form = by_channels if fits else by_frequencies
    return form(tokens_in, grad_out, decay_rate, w_in, b_in, w_mid, w_out)


def solution(mesh):
    in_specs = (P(("groups", "ctx"), None), P(("groups", "ctx"), None), P(), P(), P(), P(), P())
    out_specs = (
        P(("groups", "ctx"), None),
        P("groups"),
        P("groups"),
        P("groups", None),
        P("groups", None),
    )
    return jax.shard_map(
        on_device, mesh=mesh, in_specs=in_specs, out_specs=out_specs, check_vma=False
    )
```

```python
import functools
import math

import jax
import jax.numpy as jnp
import numpy as np
from jax import lax
from jax.experimental import pallas as pl
from jax.experimental.pallas import tpu as pltpu
from jax.sharding import PartitionSpec as P

RADIX = 16
HALF = RADIX // 2
CHUNK = 32
UNROLL_CHUNK = 8
UNROLL_BIN = 9
UNROLL_ROWS = 8
PACK_PARTS = 4
FIRST_LIMIT = 56
SECOND_LIMIT = 50
F32 = jnp.float32
BF16 = jnp.bfloat16


def split_pair(value):
    high = value.astype(BF16)
    return high, (value - high.astype(F32)).astype(BF16)


def dot(left, right):
    return jnp.dot(left, right, preferred_element_type=F32)


def pair_lanes(value):
    return jnp.concatenate(split_pair(value), axis=1)


def square(matrix):
    high, low = split_pair(matrix)
    return jnp.concatenate(
        [
            jnp.concatenate([high, low], axis=1),
            jnp.concatenate([high, jnp.zeros_like(low)], axis=1),
        ],
        axis=0,
    )


def dot_pair(rows, squared):
    product = dot(rows, squared)
    return product[:, 0:128] + product[:, 128:256]


def tall_three(value):
    high, low = split_pair(value)
    return jnp.concatenate([high, high, low], axis=0)


def dft_tables(padded):
    inner = padded // RADIX
    grid = np.outer(np.arange(inner), np.arange(inner)) % inner
    angles = 2.0 * np.pi * grid / inner
    matrix = np.concatenate([np.cos(angles), np.sin(angles)], axis=0)
    high = matrix.astype(jnp.bfloat16)
    low = (matrix - high.astype(np.float64)).astype(jnp.bfloat16)
    matrix = np.concatenate([high, low, high], axis=1)
    turn = 2.0 * np.pi * np.outer(np.arange(inner), np.arange(RADIX)) / padded
    twiddle = np.zeros((inner, 128), np.float32)
    twiddle[:, :RADIX] = np.cos(turn)
    twiddle[:, RADIX : 2 * RADIX] = np.sin(turn)
    return jnp.asarray(matrix), jnp.asarray(twiddle)


def cos_of(index):
    return math.cos(2.0 * math.pi * index / RADIX)


def sin_of(index):
    return math.sin(2.0 * math.pi * index / RADIX)


def spread(x):
    plus = [x[q] + x[q + 4] for q in range(4)]
    minus = [x[q] - x[q + 4] for q in range(4)]
    root = math.sqrt(0.5)
    out = [None] * 9
    even, odd = plus[0] + plus[2], plus[1] + plus[3]
    out[0] = (even + odd, None)
    out[8] = (even - odd, None)
    out[4] = (plus[0] - plus[2], plus[3] - plus[1])
    across, along = root * (minus[1] - minus[3]), root * (minus[1] + minus[3])
    out[2] = (minus[0] + across, -minus[2] - along)
    out[6] = (minus[0] - across, minus[2] - along)
    differ = {q: x[q] - x[8 - q] for q in (1, 2, 3)}
    same = {q: x[q] + x[8 - q] for q in (1, 2, 3)}
    for j in (1, 3):
        real_even = x[0] + cos_of(2 * j) * differ[2]
        real_odd = cos_of(j) * differ[1] + cos_of(3 * j) * differ[3]
        imag_even = sin_of(4 * j) * x[4] + sin_of(2 * j) * same[2]
        imag_odd = sin_of(j) * same[1] + sin_of(3 * j) * same[3]
        out[j] = (real_even + real_odd, -(imag_odd + imag_even))
        out[8 - j] = (real_even - real_odd, imag_even - imag_odd)
    return out


def gather_back(real, imag):
    even, odd = [None] * 8, [None] * 8
    total, differ = real[0] + real[8], real[0] - real[8]
    real_sum, real_dif = real[2] + real[6], real[2] - real[6]
    imag_sum, imag_dif = imag[2] + imag[6], imag[2] - imag[6]
    root = math.sqrt(0.5)
    even[0] = total + real_sum + real[4]
    even[4] = total - real_sum + real[4]
    even[2] = total - imag_dif - real[4]
    even[6] = total + imag_dif - real[4]
    first, second = root * (real_dif - imag_sum), root * (real_dif + imag_sum)
    even[1] = differ + first - imag[4]
    even[5] = differ - first - imag[4]
    even[3] = differ - second + imag[4]
    even[7] = differ + second + imag[4]
    one_sum, one_dif = real[1] + real[7], real[1] - real[7]
    three_sum, three_dif = real[3] + real[5], real[3] - real[5]
    ione_sum, ione_dif = imag[1] + imag[7], imag[1] - imag[7]
    ithree_sum, ithree_dif = imag[3] + imag[5], imag[3] - imag[5]
    odd[0] = one_sum + three_sum
    odd[4] = ithree_dif - ione_dif
    for q in (1, 2, 3):
        if q % 2 == 0:
            cosines = cos_of(q) * one_sum + cos_of(3 * q) * three_sum
            sines = sin_of(q) * ione_dif + sin_of(3 * q) * ithree_dif
        else:
            cosines = cos_of(q) * one_dif + cos_of(3 * q) * three_dif
            sines = sin_of(q) * ione_sum + sin_of(3 * q) * ithree_sum
        odd[q] = cosines - sines
        odd[8 - q] = -cosines - sines
    return even, odd


def residues_to_scratch(load, twiddle, stage, inner):
    def chunk(step, carry):
        start = pl.multiple_of(step * CHUNK, CHUNK)
        turn = twiddle[pl.ds(start, CHUNK), :]
        for j, (real, imag) in enumerate(spread([load(q * inner + start) for q in range(HALF)])):
            if j > 0:
                cosine, sine = turn[:, j : j + 1], turn[:, RADIX + j : RADIX + j + 1]
                if imag is None:
                    real, imag = real * cosine, -real * sine
                else:
                    real, imag = real * cosine + imag * sine, imag * cosine - real * sine
            else:
                imag = jnp.zeros_like(real)
            for part, value in enumerate((real, imag)):
                high, low = split_pair(value)
                lanes = slice(128 * part, 128 * part + 128)
                stage[j, pl.ds(start, CHUNK), lanes] = high
                stage[j, pl.ds(inner + start, CHUNK), lanes] = high
                stage[j, pl.ds(2 * inner + start, CHUNK), lanes] = low
        return carry

    lax.fori_loop(0, inner // CHUNK, chunk, 0, unroll=UNROLL_CHUNK)


def inner_dft(stacked, matrix, inner, direction):
    product = dot(matrix[...], stacked)
    cos_real, cos_imag = product[:inner, :128], product[:inner, 128:]
    sin_real, sin_imag = product[inner:, :128], product[inner:, 128:]
    if direction > 0:
        return cos_real + sin_imag, cos_imag - sin_real
    return cos_real - sin_imag, cos_imag + sin_real


def low_lanes(rows):
    return lax.broadcasted_iota(jnp.int32, (rows, 128), 1) < 64


def swap(value):
    return pltpu.roll(value, 64, 1)


def fetch(sources, buffers, semaphores):
    copies = [
        pltpu.make_async_copy(source, buffer, semaphores.at[index])
        for index, (source, buffer) in enumerate(zip(sources, buffers))
    ]
    for copy in copies:
        copy.start()
    return copies


def pack_kernel(tokens_hbm, cotan_hbm, out_hbm, tokens, cotan, out, load_semaphores, store_semaphores):
    loads, stores = [], []
    rows_each = tokens.shape[0] // PACK_PARTS
    for part in range(PACK_PARTS):
        rows = pl.ds(part * rows_each, rows_each)
        loads.append(
            fetch(
                (tokens_hbm.at[rows, :], cotan_hbm.at[rows, :]),
                (tokens.at[rows, :], cotan.at[rows, :]),
                load_semaphores.at[part],
            )
        )
    for part in range(PACK_PARTS):
        rows = pl.ds(part * rows_each, rows_each)
        for copy in loads[part]:
            copy.wait()
        for block in range(out.shape[0]):
            lanes = slice(64 * block, 64 * block + 64)
            out[block, rows, :] = jnp.concatenate([tokens[rows, lanes], cotan[rows, lanes]], axis=1)
        store = pltpu.make_async_copy(
            out.at[:, rows, :], out_hbm.at[:, rows, :], store_semaphores.at[part]
        )
        store.start()
        stores.append(store)
    for store in stores:
        store.wait()


def diagonal(matrix):
    empty = jnp.zeros_like(matrix)
    return jnp.concatenate(
        [jnp.concatenate([matrix, empty], axis=1), jnp.concatenate([empty, matrix], axis=1)], axis=0
    )


def twice(row):
    return jnp.concatenate([row, row], axis=1)


def exp_minus_one(value):
    series = jnp.ones_like(value)
    for order in range(9, 1, -1):
        series = 1.0 + series * value * (1.0 / order)
    return jnp.where(jnp.abs(value) < 0.35, value * series, jnp.exp(value) - 1.0)


def kernel_spectrum_kernel(
    length, rates, w_first, w_bias, w_mid, w_last, matrix, twiddle, wide_hbm, narrow_hbm,
    spectrum, slope_two, consts, one, two, mid_back, last_back, semaphores, taps, stage,
):
    inner = 2 * length // RADIX
    low_half = low_lanes(inner)
    own = lax.axis_index("ctx")
    lanes = pl.ds(pl.multiple_of(own // 2 * 128, 128), 128)
    odd = own % 2 == 1
    last = w_last[:, lanes]
    last = diagonal(jnp.where(odd, swap(last), last)[:, 0:64])
    rate = rates[:, lanes]
    rate = twice(jnp.where(odd, swap(rate), rate)[:, 0:64])
    double = 2.0 * rate
    ratio = exp_minus_one(-double * (length - 1)) / exp_minus_one(-double)
    geometric = 1.0 + 2.0 * jnp.exp(-double) * ratio
    scale = lax.rsqrt(geometric)
    mid = diagonal(w_mid[...])
    mid_back[...] = square(mid.T)
    last_back[...] = square(last.T)
    mid, last = square(mid), square(last)
    first, bias = twice(w_first[...]), twice(w_bias[...])
    consts[...] = jnp.concatenate([rate, scale, first, bias, jnp.zeros((4, 128), F32)], axis=0)

    def block(step, carry):
        start = pl.multiple_of(step * inner, inner)
        rows = pl.ds(start, inner)
        place = start + lax.broadcasted_iota(jnp.int32, (inner, 128), 0)
        lag = jnp.where(low_half, place, place - length)
        scaled = lag.astype(F32) / length
        pre_one = scaled * first + bias
        gate_one = 1.0 / (1.0 + jnp.exp(-pre_one))
        hidden_one = pre_one * gate_one
        pre_two = dot_pair(pair_lanes(hidden_one), mid)
        gate_two = 1.0 / (1.0 + jnp.exp(-pre_two))
        hidden_two = pre_two * gate_two
        slope_two[rows, :] = gate_two * (1.0 + pre_two * (1.0 - gate_two))
        position = dot_pair(pair_lanes(hidden_two), last)
        live = jnp.where(lag == -length, 0.0, 1.0)
        env = live * scale * jnp.exp(-jnp.abs(lag).astype(F32) * rate)
        taps[rows, :] = (position * env).astype(BF16).astype(F32)
        one[0:128, rows], one[128:256, rows] = split_pair(hidden_one.T)
        two[0:128, rows], two[128:256, rows] = split_pair(hidden_two.T)
        return carry

    lax.fori_loop(0, HALF, block, 0, unroll=UNROLL_ROWS)
    places = passed_places(length, wide_hbm, narrow_hbm)
    held = (slope_two, consts, one, two, mid_back, last_back)
    copies = fetch(held, places[1:], semaphores)
    residues_to_scratch(lambda start: taps[pl.ds(start, CHUNK), :], twiddle, stage, inner)

    def transform(j, carry):
        real, imag = inner_dft(stage[j], matrix, inner, 1)
        sign = 1.0 - 2.0 * lax.rem(jnp.asarray(j, jnp.int32), 2).astype(F32)
        spectrum[pl.ds((2 * j + 0) * inner, inner), :] = real + sign * swap(real)
        spectrum[pl.ds((2 * j + 1) * inner, inner), :] = imag + sign * swap(imag)
        return carry

    lax.fori_loop(0, HALF + 1, transform, 0, unroll=UNROLL_BIN)
    last_copy = pltpu.make_async_copy(spectrum, places[0], semaphores.at[len(copies)])
    last_copy.start()
    for copy in copies + [last_copy]:
        copy.wait()


def gradient_kernel(
    length, signal, wide_hbm, narrow_hbm, matrix, twiddle, out,
    spectrum, slope_two, consts, one, two, mid_back, last_back, semaphores, stage, back_ref, slopes,
    pre, decay,
):
    padded = 2 * length
    inner = padded // RADIX
    low_half = low_lanes(inner)
    held = (spectrum, slope_two, consts, one, two, mid_back, last_back)
    copies = fetch(passed_places(length, wide_hbm, narrow_hbm), held, semaphores)
    residues_to_scratch(
        lambda start: signal[pl.ds(start, CHUNK), :].astype(F32), twiddle, stage, inner
    )

    def analyse(j, carry):
        real, imag = inner_dft(stage[j], matrix, inner, 1)
        back_ref[j, :, 0:128] = real
        back_ref[j, :, 128:256] = imag
        return carry

    lax.fori_loop(0, HALF + 1, analyse, 0, unroll=UNROLL_BIN)
    copies[0].wait()

    def transform(j, carry):
        real, imag = back_ref[j, :, 0:128], back_ref[j, :, 128:256]
        real_swap, imag_swap = swap(real), swap(imag)
        cotan_real = jnp.where(low_half, real_swap, real)
        cotan_imag = jnp.where(low_half, imag_swap, imag)
        other_real = jnp.where(low_half, spectrum[pl.ds((2 * j + 0) * inner, inner), :], real_swap)
        other_imag = jnp.where(low_half, spectrum[pl.ds((2 * j + 1) * inner, inner), :], imag_swap)
        product = jnp.concatenate(
            [
                cotan_real * other_real + cotan_imag * other_imag,
                cotan_imag * other_real - cotan_real * other_imag,
            ],
            axis=1,
        )
        real, imag = inner_dft(tall_three(product), matrix, inner, -1)
        back_ref[j, :, 0:128] = real
        back_ref[j, :, 128:256] = imag
        return carry

    lax.fori_loop(0, HALF + 1, transform, 0, unroll=UNROLL_BIN)
    for copy in copies[1:]:
        copy.wait()
    rate, scale, first, bias = (consts[index : index + 1, :] for index in range(4))
    place = lax.broadcasted_iota(jnp.int32, (inner, 128), 0)
    near = jnp.where(low_half, place, inner - 1 - place).astype(F32)
    decay[...] = jnp.exp(-near * rate)
    low_row = low_lanes(1)

    def unspread(step, carry):
        start = pl.multiple_of(step * CHUNK, CHUNK)
        rows = pl.ds(start, CHUNK)
        turn = twiddle[rows, :]
        real_list, imag_list = [], []
        for j in range(HALF + 1):
            weight = (1.0 if j in (0, HALF) else 2.0) / padded
            real, imag = back_ref[j, rows, 0:128], back_ref[j, rows, 128:256]
            if j == 0:
                real_list.append(real * weight)
                imag_list.append(None)
                continue
            cosine = turn[:, j : j + 1] * weight
            sine = turn[:, RADIX + j : RADIX + j + 1] * weight
            real_list.append(real * cosine - imag * sine)
            imag_list.append(real * sine + imag * cosine)
        even, odd = gather_back(real_list, imag_list)
        for q in range(HALF):
            joined, apart = even[q] + odd[q], even[q] - odd[q]
            back_ref[q, rows, 0:128] = joined
            at = pl.ds(q * inner + start, CHUNK)
            lag_grad = jnp.where(low_lanes(CHUNK), swap(joined), apart)
            far = jnp.where(low_row, q * inner, length - q * inner - inner + 1).astype(F32)
            weighted = lag_grad * (scale * jnp.exp(-far * rate)) * decay[rows, :]
            if q == 0:
                row = start + lax.broadcasted_iota(jnp.int32, (CHUNK, 128), 0)
                weighted = jnp.where((row == 0) & ~low_lanes(CHUNK), 0.0, weighted)
            slopes[at, :] = pair_lanes(weighted)
        return carry

    lax.fori_loop(0, inner // CHUNK, unspread, 0, unroll=UNROLL_CHUNK)
    local_rows = 128
    half_rows = local_rows // 2
    rise = jnp.exp(place.astype(F32) * (first * (-1.0 / length)))

    def block(q, carry):
        first_sum, bias_sum = carry
        start = pl.multiple_of(q * inner, inner)
        rows = pl.ds(start, inner)
        for part in range(inner // local_rows):
            base = part * local_rows
            upper = back_ref[q, base : base + half_rows, 0:128]
            lower = back_ref[q, base + half_rows : base + local_rows, 0:128]
            out[q * (inner // local_rows) + part, 0:half_rows, :] = jnp.where(
                low_half[:half_rows], upper, swap(lower)
            ).astype(BF16)
        pre_two = pair_lanes(dot_pair(slopes[rows, :], last_back[...]) * slope_two[rows, :])
        pre[rows, :] = pre_two
        base = jnp.where(low_row, start, start - length)
        scaled = (place + base).astype(F32) * (1.0 / length)
        before = scaled * first + bias
        gate = 1.0 / (1.0 + rise * jnp.exp(-(base.astype(F32) * (1.0 / length) * first + bias)))
        slope_one = gate * (1.0 + before * (1.0 - gate))
        pre_one = dot_pair(pre_two, mid_back[...]) * slope_one
        first_sum = first_sum + jnp.sum((pre_one * scaled).reshape(inner // 8, 8, 128), axis=0)
        bias_sum = bias_sum + jnp.sum(pre_one.reshape(inner // 8, 8, 128), axis=0)
        return first_sum, bias_sum

    none = jnp.zeros((8, 128), F32)
    first_sum, bias_sum = lax.fori_loop(0, HALF, block, (none, none), unroll=UNROLL_ROWS)
    last_sum, mid_sum = (
        product[0:128, 0:128] + (product[0:128, 128:256] + product[128:256, 0:128])
        for product in (dot(two[...], slopes[...]), dot(one[...], pre[...]))
    )
    low_32 = low_lanes(32)
    grad_last = last_sum[0:64] + swap(last_sum[64:128])
    last_rows = jnp.where(low_32, grad_last[0:32], swap(grad_last[32:64]))
    grad_mid = mid_sum[0:64] + swap(mid_sum[64:128])
    mid_rows = jnp.where(low_32, grad_mid[0:32], swap(grad_mid[32:64]))
    first = jnp.sum(first_sum, axis=0, keepdims=True)
    bias = jnp.sum(bias_sum, axis=0, keepdims=True)
    first = first + swap(first)
    bias = bias + swap(bias)
    joined = jnp.where(low_lanes(1), first, bias)
    joined_high = joined.astype(BF16).astype(F32)
    row_index = lax.broadcasted_iota(jnp.int32, (8, 128), 0)
    joined_rows = jnp.where(
        row_index == 0, joined_high, jnp.where(row_index == 1, joined - joined_high, 0.0)
    )
    for device in range(out.shape[0]):
        half = slice(16 * (device % 2), 16 * (device % 2) + 16)
        tail = [last_rows[half], mid_rows[half], joined_rows]
        out[device, half_rows:, :] = jnp.concatenate(tail, axis=0).astype(BF16)


def sums_kernel(received, half, joined_out):
    half_rows = received.shape[1] - 40
    mid = jnp.zeros((16, 128), F32)
    joined = jnp.zeros((8, 128), F32)
    for source in range(received.shape[0]):
        lanes = slice(64 * source, 64 * source + 64)
        last = received[source, half_rows : half_rows + 16, :]
        half[0:16, lanes] = last[:, 0:64]
        half[16:32, lanes] = last[:, 64:128]
        mid = mid + received[source, half_rows + 16 : half_rows + 32, :].astype(F32)
        joined = joined + received[source, half_rows + 32 : half_rows + 40, :].astype(F32)
    mid = jnp.concatenate([mid, swap(mid)], axis=0)
    high = mid.astype(BF16).astype(F32)
    columns = 64 * received.shape[0]
    rest = swap(mid - high)
    half[:, columns : columns + 128] = jnp.where(low_lanes(32), high, rest).astype(BF16)
    joined_out[...] = joined


def tokens_kernel(received, grad_tokens):
    half_rows = grad_tokens.shape[0] // 2
    for source in range(received.shape[0]):
        lanes = slice(64 * source, 64 * source + 64)
        tile = received[source, 0:half_rows, :]
        grad_tokens[0:half_rows, lanes] = tile[:, 0:64]
        grad_tokens[half_rows:, lanes] = tile[:, 64:128]


def weights_kernel(loss_scale, joined, mine, other, grad_first, grad_bias, grad_mid, grad_last):
    odd = lax.rem(lax.axis_index("ctx"), 2)
    columns = grad_last.shape[1]
    for source, parity in ((mine, odd), (other, 1 - odd)):
        last = source[:, 0:columns].astype(F32) * loss_scale
        grad_last[pl.ds(pl.multiple_of(16 * parity, 16), 16), :] = last[0:16]
        grad_last[pl.ds(pl.multiple_of(32 + 16 * parity, 16), 16), :] = last[16:32]
        mid = source[:, columns : columns + 128].astype(F32) * loss_scale
        mid = (mid + swap(mid))[:, 0:64]
        grad_mid[pl.ds(pl.multiple_of(16 * parity, 16), 16), :] = mid[0:16]
        grad_mid[pl.ds(pl.multiple_of(32 + 16 * parity, 16), 16), :] = mid[16:32]
    first = (joined[0:1] + joined[1:2]) * loss_scale
    grad_first[...] = first[:, 0:64]
    grad_bias[...] = first[:, 64:128]


def call(kernel, out_shape, scratch=(), flops=0, limit=24, **specs):
    return pl.pallas_call(
        kernel,
        out_shape=out_shape,
        **specs,
        scratch_shapes=list(scratch),
        compiler_params=pltpu.CompilerParams(vmem_limit_bytes=limit << 20),
        cost_estimate=pl.CostEstimate(flops=flops, bytes_accessed=1 << 20, transcendentals=0),
    )


def shape(dims, dtype):
    return jax.ShapeDtypeStruct(dims, dtype)


ON_HBM = pl.BlockSpec(memory_space=pltpu.HBM)
ON_VMEM = pl.BlockSpec(memory_space=pltpu.VMEM)


def passed_places(length, wide, narrow):
    bins = 2 * (HALF + 1) * (2 * length // RADIX)
    parts = [wide.at[pl.ds(0, bins), :], wide.at[pl.ds(bins, length), :]]
    parts += [wide.at[pl.ds(bins + length, 8), :]]
    parts += [narrow.at[pl.ds(256 * index, 256), :] for index in range(2)]
    return parts + [narrow.at[pl.ds(512, 256), pl.ds(256 * index, 256)] for index in range(2)]


def passed_shapes(length):
    bins = 2 * (HALF + 1) * (2 * length // RADIX)
    return [shape((bins + length + 8, 128), F32), shape((512 + 256, length), BF16)]


def held_arrays(length):
    bins = 2 * (HALF + 1) * (2 * length // RADIX)
    held = [pltpu.VMEM((rows, 128), F32) for rows in (bins, length, 8)]
    held += [pltpu.VMEM((256, length), BF16)] * 2 + [pltpu.VMEM((256, 256), BF16)] * 2
    return held + [pltpu.SemaphoreType.DMA((len(held),))]


def spectrum_call(length, *operands):
    inner = 2 * length // RADIX
    return call(
        functools.partial(kernel_spectrum_kernel, length),
        passed_shapes(length),
        scratch=held_arrays(length)
        + [pltpu.VMEM((length, 128), F32), pltpu.VMEM((HALF + 1, 3 * inner, 256), BF16)],
        flops=4 << 30,
        limit=FIRST_LIMIT,
        out_specs=[ON_HBM] * 2,
    )(*operands)


def gradient_call(length, *operands):
    inner = 2 * length // RADIX
    local_rows = 128
    return call(
        functools.partial(gradient_kernel, length),
        shape((length // local_rows, local_rows // 2 + 40, 128), BF16),
        scratch=held_arrays(length)
        + [
            pltpu.VMEM((HALF + 1, 3 * inner, 256), BF16),
            pltpu.VMEM((HALF + 1, inner, 256), F32),
        ]
        + [pltpu.VMEM((length, 256), BF16)] * 2
        + [pltpu.VMEM((inner, 128), F32)],
        flops=8 << 30,
        limit=SECOND_LIMIT,
        in_specs=[ON_VMEM] + [ON_HBM] * 2 + [ON_VMEM] * 2,
    )(*operands)


def by_channels(tokens_in, grad_out, decay_rate, w_in, b_in, w_mid, w_out):
    devices = lax.axis_size("ctx")
    local_rows = tokens_in.shape[0]
    length = local_rows * devices
    matrix, twiddle = dft_tables(2 * length)
    packed = call(
        pack_kernel,
        shape((devices, local_rows, 128), BF16),
        scratch=[pltpu.VMEM(tokens_in.shape, BF16)] * 2
        + [
            pltpu.VMEM((devices, local_rows, 128), BF16),
            pltpu.SemaphoreType.DMA((PACK_PARTS, 2)),
            pltpu.SemaphoreType.DMA((PACK_PARTS,)),
        ],
        limit=58,
        in_specs=[ON_HBM] * 2,
        out_specs=ON_HBM,
    )(tokens_in, grad_out)
    signal = lax.all_to_all(packed, "ctx", split_axis=0, concat_axis=0, tiled=True)
    forward = spectrum_call(
        length, decay_rate.reshape(1, -1), w_in.reshape(1, -1), b_in.reshape(1, -1), w_mid, w_out,
        matrix, twiddle,
    )
    sent = gradient_call(length, signal.reshape(length, 128), *forward, matrix, twiddle)
    received = lax.all_to_all(sent, "ctx", split_axis=0, concat_axis=0, tiled=True)
    half, joined = call(
        sums_kernel, [shape((32, 64 * devices + 128), BF16), shape((8, 128), F32)]
    )(received)
    other = lax.ppermute(half, "ctx", [(index, index ^ 1) for index in range(devices)])
    input_grad = call(tokens_kernel, shape(tokens_in.shape, BF16), flops=1 << 26)(received)
    grad_first, grad_bias, grad_mid, grad_last = call(
        functools.partial(weights_kernel, 1.0 / math.sqrt(length)),
        [shape((1, 64), F32), shape((1, 64), F32), shape((64, 64), F32), shape(w_out.shape, F32)],
    )(joined, half, other)
    return input_grad, grad_first.reshape(64), grad_bias.reshape(64), grad_mid, grad_last


HIGHEST = lax.Precision.HIGHEST
TWO_PI = 2.0 * math.pi


def phase_angle(product, period):
    return TWO_PI / period * (product % period).astype(jnp.float32)


def frequency_rows(devices):
    row_index = jnp.arange(2 * devices, dtype=jnp.int32)
    row_block = row_index // 2
    second = row_index % 2
    paired = jnp.where(row_block == 0, devices, 2 * devices - row_block)
    return jnp.where(second == 0, row_block, paired)


def source_rows(devices):
    row_index = jnp.arange(2 * devices, dtype=jnp.int32)
    return row_index // 2 + row_index % 2 * devices


def envelope(lag_values, decay_rate, length):
    double = 2.0 * decay_rate
    geometric = 1.0 + 2.0 * jnp.exp(-double) * jnp.expm1(-double * (length - 1)) / jnp.expm1(
        -double
    )
    distance = jnp.abs(lag_values).astype(jnp.float32)[..., None]
    live_mask = (lag_values != -length).astype(jnp.float32)[..., None]
    return live_mask * lax.rsqrt(geometric) * jnp.exp(-distance * decay_rate)


def position_mlp(scaled, w_first, w_bias, w_middle, w_last):
    hidden_one = jax.nn.silu(scaled[..., None] * w_first + w_bias)
    hidden_two = jax.nn.silu(jnp.dot(hidden_one, w_middle, precision=HIGHEST))
    return jnp.dot(hidden_two, w_last, precision=HIGHEST)


def rotate(real_a, imag_a, real_b, imag_b):
    return (real_a * real_b - imag_a * imag_b, real_a * imag_b + imag_a * real_b)


def first_section(signal, columns, freq_order, local_slab, padded):
    freq_count = freq_order.shape[0]
    angles = phase_angle(freq_order[:, None] * columns[None, :], freq_count)
    real_part = jnp.einsum("fp,prc->frc", jnp.cos(angles), signal, precision=HIGHEST)
    imag_part = jnp.einsum("fp,prc->frc", -jnp.sin(angles), signal, precision=HIGHEST)
    twiddle = phase_angle(freq_order[:, None] * local_slab[None, :], padded)[:, :, None]
    return rotate(real_part, imag_part, jnp.cos(twiddle), -jnp.sin(twiddle))


def along_rows(stacked, direction):
    row_count = stacked.shape[1]
    half_width = stacked.shape[2] // 2
    positions = jnp.arange(row_count, dtype=jnp.int32)
    angles = phase_angle(positions[:, None] * positions[None, :], row_count)
    with_cos = jnp.einsum("gm,imc->igc", jnp.cos(angles), stacked, precision=HIGHEST)
    with_sin = jnp.einsum("gm,imc->igc", direction * jnp.sin(angles), stacked, precision=HIGHEST)
    real_part = with_cos[..., :half_width] - with_sin[..., half_width:]
    imag_part = with_cos[..., half_width:] + with_sin[..., :half_width]
    return (real_part, imag_part)


def last_section(stacked, out_rows, freq_order, padded):
    freq_count = freq_order.shape[0]
    half_width = stacked.shape[2] // 2
    angles = phase_angle(out_rows[:, None] * freq_order[None, :], freq_count)
    cos_table = jnp.cos(angles) / padded
    sin_table = jnp.sin(angles) / padded
    real_in = stacked[..., :half_width]
    imag_in = stacked[..., half_width:]
    leading, trailing, factor = (real_in, imag_in, -1.0)
    return jnp.einsum("pf,frc->prc", cos_table, leading, precision=HIGHEST) + factor * jnp.einsum(
        "pf,frc->prc", sin_table, trailing, precision=HIGHEST
    )


def by_frequencies(tokens_in, grad_out, decay_rate, w_in, b_in, w_mid, w_out):
    devices = lax.axis_size("ctx")
    own_index = lax.axis_index("ctx")
    tok_rows = tokens_in.shape[0]
    slab_rows = tok_rows // devices
    length = tok_rows * devices
    padded = 2 * length
    freq_order = frequency_rows(devices)
    lag_rows = source_rows(devices)
    token_cols = jnp.arange(devices, dtype=jnp.int32)
    local_slab = own_index * slab_rows + jnp.arange(slab_rows, dtype=jnp.int32)
    pair_index = jnp.arange(2, dtype=jnp.int32)
    local_freq = jnp.where(
        pair_index == 0, own_index, jnp.where(own_index == 0, devices, 2 * devices - own_index)
    )
    circular = (own_index + pair_index * devices)[:, None] * tok_rows + jnp.arange(
        tok_rows, dtype=jnp.int32
    )[None, :]
    lag_values = jnp.where(circular < length, circular, circular - padded)
    scaled = lag_values.astype(jnp.float32) / length
    weights_env = envelope(lag_values, decay_rate, length)

    def position_net(w_first, w_bias, w_middle, w_last):
        return position_mlp(scaled, w_first, w_bias, w_middle, w_last)

    position, pull_back = jax.vjp(position_net, w_in, b_in, w_mid, w_out)
    kernel = (position * weights_env).astype(jnp.bfloat16)
    tokens_mid, grads_mid, kernel_mid = (
        lax.all_to_all(tokens_in[None], "ctx", split_axis=1, concat_axis=0, tiled=True),
        lax.all_to_all(grad_out[None], "ctx", split_axis=1, concat_axis=0, tiled=True),
        lax.all_to_all(kernel, "ctx", split_axis=1, concat_axis=0, tiled=True),
    )
    token_real, token_imag = first_section(
        tokens_mid.astype(jnp.float32), token_cols, freq_order, local_slab, padded
    )
    cotan_real, cotan_imag = first_section(
        grads_mid.astype(jnp.float32), token_cols, freq_order, local_slab, padded
    )
    kern_real, kern_imag = first_section(
        kernel_mid.astype(jnp.float32), lag_rows, freq_order, local_slab, padded
    )
    kernel_stack = jnp.concatenate([kern_real, kern_imag], axis=2)
    token_stack = jnp.concatenate([token_real, token_imag], axis=2)
    cotan_stack = jnp.concatenate([cotan_real, cotan_imag], axis=2)
    token_spec, cotan_spec, kernel_spec = (
        lax.all_to_all(token_stack, "ctx", split_axis=0, concat_axis=1, tiled=True),
        lax.all_to_all(cotan_stack, "ctx", split_axis=0, concat_axis=1, tiled=True),
        lax.all_to_all(kernel_stack, "ctx", split_axis=0, concat_axis=1, tiled=True),
    )
    spec_token_real, spec_token_imag = along_rows(token_spec, -1.0)
    spec_cotan_real, spec_cotan_imag = along_rows(cotan_spec, -1.0)
    spec_kern_real, spec_kern_imag = along_rows(kernel_spec, -1.0)
    input_real = spec_kern_real * spec_cotan_real + spec_kern_imag * spec_cotan_imag
    input_imag = spec_kern_real * spec_cotan_imag - spec_kern_imag * spec_cotan_real
    lagged_real = spec_cotan_real * spec_token_real + spec_cotan_imag * spec_token_imag
    lagged_imag = spec_cotan_imag * spec_token_real - spec_cotan_real * spec_token_imag
    positions = jnp.arange(tok_rows, dtype=jnp.int32)
    back_angle = phase_angle(local_freq[:, None] * positions[None, :], padded)[:, :, None]
    back_cos = jnp.cos(back_angle)
    back_sin = jnp.sin(back_angle)

    def inverse_rows(real_part, imag_part):
        stacked = jnp.concatenate([real_part, imag_part], axis=2)
        out_real, out_imag = along_rows(stacked, 1.0)
        turned_real, turned_imag = rotate(out_real, out_imag, back_cos, back_sin)
        return jnp.concatenate([turned_real, turned_imag], axis=2)

    spread_input, spread_lagged = (
        lax.all_to_all(
            inverse_rows(input_real, input_imag), "ctx", split_axis=1, concat_axis=0, tiled=True
        ),
        lax.all_to_all(
            inverse_rows(lagged_real, lagged_imag), "ctx", split_axis=1, concat_axis=0, tiled=True
        ),
    )
    input_rows = last_section(spread_input, token_cols, freq_order, padded)
    lagged_rows = last_section(spread_lagged, lag_rows, freq_order, padded)
    input_back, lag_back = (
        lax.all_to_all(input_rows, "ctx", split_axis=0, concat_axis=1, tiled=True),
        lax.all_to_all(lagged_rows, "ctx", split_axis=0, concat_axis=1, tiled=True),
    )
    input_grad = input_back[0]
    gradients = pull_back(lag_back * weights_env)
    summed = lax.psum((gradients[0], gradients[1], gradients[2], gradients[3]), "ctx")
    loss_scale = 1.0 / math.sqrt(length)
    return (
        input_grad.astype(jnp.bfloat16),
        summed[0] * loss_scale,
        summed[1] * loss_scale,
        summed[2] * loss_scale,
        summed[3] * loss_scale,
    )


def on_device(tokens_in, grad_out, decay_rate, w_in, b_in, w_mid, w_out):
    devices = lax.axis_size("ctx")
    fits = (
        tokens_in.shape == (128, 64 * devices)
        and devices % 2 == 0
        and devices * 128 % (128 * HALF) == 0
        and w_mid.shape == (64, 64)
    )
    form = by_channels if fits else by_frequencies
    return form(tokens_in, grad_out, decay_rate, w_in, b_in, w_mid, w_out)


def solution(mesh):
    in_specs = (P(("groups", "ctx"), None), P(("groups", "ctx"), None), P(), P(), P(), P(), P())
    out_specs = (
        P(("groups", "ctx"), None),
        P("groups"),
        P("groups"),
        P("groups", None),
        P("groups", None),
    )
    return jax.shard_map(
        on_device, mesh=mesh, in_specs=in_specs, out_specs=out_specs, check_vma=False
    )
```

```python
import functools
import math

import jax
import jax.numpy as jnp
import numpy as np
from jax import lax
from jax.experimental import pallas as pl
from jax.experimental.pallas import tpu as pltpu
from jax.sharding import PartitionSpec as P

RADIX = 16
HALF = RADIX // 2
CHUNK = 32
UNROLL_CHUNK = 8
UNROLL_BIN = 9
UNROLL_ROWS = 8
PACK_PARTS = 4
FIRST_LIMIT = 56
SECOND_LIMIT = 50
F32 = jnp.float32
BF16 = jnp.bfloat16


def split_pair(value):
    high = value.astype(BF16)
    return high, (value - high.astype(F32)).astype(BF16)


def dot(left, right):
    return jnp.dot(left, right, preferred_element_type=F32)


def pair_lanes(value):
    return jnp.concatenate(split_pair(value), axis=1)


def square(matrix):
    high, low = split_pair(matrix)
    return jnp.concatenate(
        [
            jnp.concatenate([high, low], axis=1),
            jnp.concatenate([high, jnp.zeros_like(low)], axis=1),
        ],
        axis=0,
    )


def dot_pair(rows, squared):
    product = dot(rows, squared)
    return product[:, 0:128] + product[:, 128:256]


def tall_three(value):
    high, low = split_pair(value)
    return jnp.concatenate([high, high, low], axis=0)


def dft_tables(padded):
    inner = padded // RADIX
    grid = np.outer(np.arange(inner), np.arange(inner)) % inner
    angles = 2.0 * np.pi * grid / inner
    matrix = np.concatenate([np.cos(angles), np.sin(angles)], axis=0)
    high = matrix.astype(jnp.bfloat16)
    low = (matrix - high.astype(np.float64)).astype(jnp.bfloat16)
    matrix = np.concatenate([high, low, high], axis=1)
    turn = 2.0 * np.pi * np.outer(np.arange(inner), np.arange(RADIX)) / padded
    twiddle = np.zeros((inner, 128), np.float32)
    twiddle[:, :RADIX] = np.cos(turn)
    twiddle[:, RADIX : 2 * RADIX] = np.sin(turn)
    return jnp.asarray(matrix), jnp.asarray(twiddle)


def cos_of(index):
    return math.cos(2.0 * math.pi * index / RADIX)


def sin_of(index):
    return math.sin(2.0 * math.pi * index / RADIX)


def spread(x):
    plus = [x[q] + x[q + 4] for q in range(4)]
    minus = [x[q] - x[q + 4] for q in range(4)]
    root = math.sqrt(0.5)
    out = [None] * 9
    even, odd = plus[0] + plus[2], plus[1] + plus[3]
    out[0] = (even + odd, None)
    out[8] = (even - odd, None)
    out[4] = (plus[0] - plus[2], plus[3] - plus[1])
    across, along = root * (minus[1] - minus[3]), root * (minus[1] + minus[3])
    out[2] = (minus[0] + across, -minus[2] - along)
    out[6] = (minus[0] - across, minus[2] - along)
    differ = {q: x[q] - x[8 - q] for q in (1, 2, 3)}
    same = {q: x[q] + x[8 - q] for q in (1, 2, 3)}
    for j in (1, 3):
        real_even = x[0] + cos_of(2 * j) * differ[2]
        real_odd = cos_of(j) * differ[1] + cos_of(3 * j) * differ[3]
        imag_even = sin_of(4 * j) * x[4] + sin_of(2 * j) * same[2]
        imag_odd = sin_of(j) * same[1] + sin_of(3 * j) * same[3]
        out[j] = (real_even + real_odd, -(imag_odd + imag_even))
        out[8 - j] = (real_even - real_odd, imag_even - imag_odd)
    return out


def gather_back(real, imag):
    even, odd = [None] * 8, [None] * 8
    total, differ = real[0] + real[8], real[0] - real[8]
    real_sum, real_dif = real[2] + real[6], real[2] - real[6]
    imag_sum, imag_dif = imag[2] + imag[6], imag[2] - imag[6]
    root = math.sqrt(0.5)
    even[0] = total + real_sum + real[4]
    even[4] = total - real_sum + real[4]
    even[2] = total - imag_dif - real[4]
    even[6] = total + imag_dif - real[4]
    first, second = root * (real_dif - imag_sum), root * (real_dif + imag_sum)
    even[1] = differ + first - imag[4]
    even[5] = differ - first - imag[4]
    even[3] = differ - second + imag[4]
    even[7] = differ + second + imag[4]
    one_sum, one_dif = real[1] + real[7], real[1] - real[7]
    three_sum, three_dif = real[3] + real[5], real[3] - real[5]
    ione_sum, ione_dif = imag[1] + imag[7], imag[1] - imag[7]
    ithree_sum, ithree_dif = imag[3] + imag[5], imag[3] - imag[5]
    odd[0] = one_sum + three_sum
    odd[4] = ithree_dif - ione_dif
    for q in (1, 2, 3):
        if q % 2 == 0:
            cosines = cos_of(q) * one_sum + cos_of(3 * q) * three_sum
            sines = sin_of(q) * ione_dif + sin_of(3 * q) * ithree_dif
        else:
            cosines = cos_of(q) * one_dif + cos_of(3 * q) * three_dif
            sines = sin_of(q) * ione_sum + sin_of(3 * q) * ithree_sum
        odd[q] = cosines - sines
        odd[8 - q] = -cosines - sines
    return even, odd


def residues_to_scratch(load, twiddle, stage, inner):
    def chunk(step, carry):
        start = pl.multiple_of(step * CHUNK, CHUNK)
        turn = twiddle[pl.ds(start, CHUNK), :]
        for j, (real, imag) in enumerate(spread([load(q * inner + start) for q in range(HALF)])):
            if j > 0:
                cosine, sine = turn[:, j : j + 1], turn[:, RADIX + j : RADIX + j + 1]
                if imag is None:
                    real, imag = real * cosine, -real * sine
                else:
                    real, imag = real * cosine + imag * sine, imag * cosine - real * sine
            else:
                imag = jnp.zeros_like(real)
            for part, value in enumerate((real, imag)):
                high, low = split_pair(value)
                lanes = slice(128 * part, 128 * part + 128)
                stage[j, pl.ds(start, CHUNK), lanes] = high
                stage[j, pl.ds(inner + start, CHUNK), lanes] = high
                stage[j, pl.ds(2 * inner + start, CHUNK), lanes] = low
        return carry

    lax.fori_loop(0, inner // CHUNK, chunk, 0, unroll=UNROLL_CHUNK)


def inner_dft(stacked, matrix, inner, direction):
    product = dot(matrix[...], stacked)
    cos_real, cos_imag = product[:inner, :128], product[:inner, 128:]
    sin_real, sin_imag = product[inner:, :128], product[inner:, 128:]
    if direction > 0:
        return cos_real + sin_imag, cos_imag - sin_real
    return cos_real - sin_imag, cos_imag + sin_real


def low_lanes(rows):
    return lax.broadcasted_iota(jnp.int32, (rows, 128), 1) < 64


def swap(value):
    return pltpu.roll(value, 64, 1)


def copies_of(sources, buffers, semaphores):
    return [
        pltpu.make_async_copy(source, buffer, semaphores.at[index])
        for index, (source, buffer) in enumerate(zip(sources, buffers))
    ]


def fetch(sources, buffers, semaphores):
    copies = copies_of(sources, buffers, semaphores)
    for copy in copies:
        copy.start()
    return copies


def pack_kernel(tokens_hbm, cotan_hbm, out_hbm, tokens, cotan, out, load_semaphores, store_semaphores):
    loads, stores = [], []
    rows_each = tokens.shape[0] // PACK_PARTS
    for part in range(PACK_PARTS):
        rows = pl.ds(part * rows_each, rows_each)
        loads.append(
            fetch(
                (tokens_hbm.at[rows, :], cotan_hbm.at[rows, :]),
                (tokens.at[rows, :], cotan.at[rows, :]),
                load_semaphores.at[part],
            )
        )
    for part in range(PACK_PARTS):
        rows = pl.ds(part * rows_each, rows_each)
        for copy in loads[part]:
            copy.wait()
        for block in range(out.shape[0]):
            lanes = slice(64 * block, 64 * block + 64)
            out[block, rows, :] = jnp.concatenate([tokens[rows, lanes], cotan[rows, lanes]], axis=1)
        store = pltpu.make_async_copy(
            out.at[:, rows, :], out_hbm.at[:, rows, :], store_semaphores.at[part]
        )
        store.start()
        stores.append(store)
    for store in stores:
        store.wait()


def diagonal(matrix):
    empty = jnp.zeros_like(matrix)
    return jnp.concatenate(
        [jnp.concatenate([matrix, empty], axis=1), jnp.concatenate([empty, matrix], axis=1)], axis=0
    )


def twice(row):
    return jnp.concatenate([row, row], axis=1)


def exp_minus_one(value):
    series = jnp.ones_like(value)
    for order in range(9, 1, -1):
        series = 1.0 + series * value * (1.0 / order)
    return jnp.where(jnp.abs(value) < 0.35, value * series, jnp.exp(value) - 1.0)


def kernel_spectrum_kernel(
    length, rates, w_first, w_bias, w_mid, w_last, matrix, twiddle, wide_hbm, narrow_hbm,
    spectrum, slope_two, slope_one, consts, one, two, mid_back, last_back, semaphores, taps, stage,
):
    inner = 2 * length // RADIX
    low_half = low_lanes(inner)
    own = lax.axis_index("ctx")
    lanes = pl.ds(pl.multiple_of(own // 2 * 128, 128), 128)
    odd = own % 2 == 1
    last = w_last[:, lanes]
    last = diagonal(jnp.where(odd, swap(last), last)[:, 0:64])
    rate = rates[:, lanes]
    rate = twice(jnp.where(odd, swap(rate), rate)[:, 0:64])
    double = 2.0 * rate
    ratio = exp_minus_one(-double * (length - 1)) / exp_minus_one(-double)
    geometric = 1.0 + 2.0 * jnp.exp(-double) * ratio
    scale = lax.rsqrt(geometric)
    mid = diagonal(w_mid[...])
    mid_back[...] = square(mid.T)
    last_back[...] = square(last.T)
    mid, last = square(mid), square(last)
    first, bias = twice(w_first[...]), twice(w_bias[...])
    consts[...] = jnp.concatenate([rate, scale, first, bias, jnp.zeros((4, 128), F32)], axis=0)

    def block(step, carry):
        start = pl.multiple_of(step * inner, inner)
        rows = pl.ds(start, inner)
        place = start + lax.broadcasted_iota(jnp.int32, (inner, 128), 0)
        lag = jnp.where(low_half, place, place - length)
        scaled = lag.astype(F32) / length
        pre_one = scaled * first + bias
        gate_one = 1.0 / (1.0 + jnp.exp(-pre_one))
        hidden_one = pre_one * gate_one
        slope_one[rows, :] = gate_one * (1.0 + pre_one * (1.0 - gate_one))
        pre_two = dot_pair(pair_lanes(hidden_one), mid)
        gate_two = 1.0 / (1.0 + jnp.exp(-pre_two))
        hidden_two = pre_two * gate_two
        slope_two[rows, :] = gate_two * (1.0 + pre_two * (1.0 - gate_two))
        position = dot_pair(pair_lanes(hidden_two), last)
        live = jnp.where(lag == -length, 0.0, 1.0)
        env = live * scale * jnp.exp(-jnp.abs(lag).astype(F32) * rate)
        taps[rows, :] = (position * env).astype(BF16).astype(F32)
        one[0:128, rows], one[128:256, rows] = split_pair(hidden_one.T)
        two[0:128, rows], two[128:256, rows] = split_pair(hidden_two.T)
        return carry

    lax.fori_loop(0, HALF, block, 0, unroll=UNROLL_ROWS)
    places = passed_places(length, wide_hbm, narrow_hbm)
    held = (slope_two, slope_one, consts, one, two, mid_back, last_back)
    copies = fetch(held, places[1:], semaphores)
    residues_to_scratch(lambda start: taps[pl.ds(start, CHUNK), :], twiddle, stage, inner)

    def transform(j, carry):
        real, imag = inner_dft(stage[j], matrix, inner, 1)
        sign = 1.0 - 2.0 * lax.rem(jnp.asarray(j, jnp.int32), 2).astype(F32)
        spectrum[pl.ds((2 * j + 0) * inner, inner), :] = real + sign * swap(real)
        spectrum[pl.ds((2 * j + 1) * inner, inner), :] = imag + sign * swap(imag)
        return carry

    lax.fori_loop(0, HALF + 1, transform, 0, unroll=UNROLL_BIN)
    last_copy = pltpu.make_async_copy(spectrum, places[0], semaphores.at[len(copies)])
    last_copy.start()
    for copy in copies + [last_copy]:
        copy.wait()


def gradient_kernel(
    length, signal, wide_hbm, narrow_hbm, matrix, twiddle, out,
    spectrum, slope_two, slope_one, consts, one, two, mid_back, last_back, semaphores, stage, back_ref,
    slopes, pre, decay,
):
    padded = 2 * length
    inner = padded // RADIX
    low_half = low_lanes(inner)
    held = (spectrum, slope_two, slope_one, consts, one, two, mid_back, last_back)
    copies = copies_of(passed_places(length, wide_hbm, narrow_hbm), held, semaphores)
    first_needed, needed_later = (copies[0], copies[3]), copies[1:3] + copies[4:]
    for copy in first_needed:
        copy.start()
    residues_to_scratch(
        lambda start: signal[pl.ds(start, CHUNK), :].astype(F32), twiddle, stage, inner
    )
    for copy in needed_later:
        copy.start()

    def analyse(j, carry):
        real, imag = inner_dft(stage[j], matrix, inner, 1)
        back_ref[j, :, 0:128] = real
        back_ref[j, :, 128:256] = imag
        return carry

    lax.fori_loop(0, HALF + 1, analyse, 0, unroll=UNROLL_BIN)
    for copy in first_needed:
        copy.wait()

    def transform(j, carry):
        real, imag = back_ref[j, :, 0:128], back_ref[j, :, 128:256]
        real_swap, imag_swap = swap(real), swap(imag)
        cotan_real = jnp.where(low_half, real_swap, real)
        cotan_imag = jnp.where(low_half, imag_swap, imag)
        other_real = jnp.where(low_half, spectrum[pl.ds((2 * j + 0) * inner, inner), :], real_swap)
        other_imag = jnp.where(low_half, spectrum[pl.ds((2 * j + 1) * inner, inner), :], imag_swap)
        product = jnp.concatenate(
            [
                cotan_real * other_real + cotan_imag * other_imag,
                cotan_imag * other_real - cotan_real * other_imag,
            ],
            axis=1,
        )
        real, imag = inner_dft(tall_three(product), matrix, inner, -1)
        back_ref[j, :, 0:128] = real
        back_ref[j, :, 128:256] = imag
        return carry

    lax.fori_loop(0, HALF + 1, transform, 0, unroll=UNROLL_BIN)
    rate, scale, first, bias = (consts[index : index + 1, :] for index in range(4))
    place = lax.broadcasted_iota(jnp.int32, (inner, 128), 0)
    near = jnp.where(low_half, place, inner - 1 - place).astype(F32)
    decay[...] = jnp.exp(-near * rate)
    low_row = low_lanes(1)

    def unspread(step, carry):
        start = pl.multiple_of(step * CHUNK, CHUNK)
        rows = pl.ds(start, CHUNK)
        turn = twiddle[rows, :]
        real_list, imag_list = [], []
        for j in range(HALF + 1):
            weight = (1.0 if j in (0, HALF) else 2.0) / padded
            real, imag = back_ref[j, rows, 0:128], back_ref[j, rows, 128:256]
            if j == 0:
                real_list.append(real * weight)
                imag_list.append(None)
                continue
            cosine = turn[:, j : j + 1] * weight
            sine = turn[:, RADIX + j : RADIX + j + 1] * weight
            real_list.append(real * cosine - imag * sine)
            imag_list.append(real * sine + imag * cosine)
        even, odd = gather_back(real_list, imag_list)
        for q in range(HALF):
            joined, apart = even[q] + odd[q], even[q] - odd[q]
            back_ref[q, rows, 0:128] = joined
            at = pl.ds(q * inner + start, CHUNK)
            lag_grad = jnp.where(low_lanes(CHUNK), swap(joined), apart)
            far = jnp.where(low_row, q * inner, length - q * inner - inner + 1).astype(F32)
            weighted = lag_grad * (scale * jnp.exp(-far * rate)) * decay[rows, :]
            if q == 0:
                row = start + lax.broadcasted_iota(jnp.int32, (CHUNK, 128), 0)
                weighted = jnp.where((row == 0) & ~low_lanes(CHUNK), 0.0, weighted)
            slopes[at, :] = pair_lanes(weighted)
        return carry

    lax.fori_loop(0, inner // CHUNK, unspread, 0, unroll=UNROLL_CHUNK)
    for copy in needed_later:
        copy.wait()
    local_rows = 128
    half_rows = local_rows // 2

    def block(q, carry):
        first_sum, bias_sum = carry
        start = pl.multiple_of(q * inner, inner)
        rows = pl.ds(start, inner)
        for part in range(inner // local_rows):
            base = part * local_rows
            upper = back_ref[q, base : base + half_rows, 0:128]
            lower = back_ref[q, base + half_rows : base + local_rows, 0:128]
            out[q * (inner // local_rows) + part, 0:half_rows, :] = jnp.where(
                low_half[:half_rows], upper, swap(lower)
            ).astype(BF16)
        pre_two = pair_lanes(dot_pair(slopes[rows, :], last_back[...]) * slope_two[rows, :])
        pre[rows, :] = pre_two
        base = jnp.where(low_row, start, start - length)
        scaled = (place + base).astype(F32) * (1.0 / length)
        pre_one = dot_pair(pre_two, mid_back[...]) * slope_one[rows, :]
        first_sum = first_sum + jnp.sum((pre_one * scaled).reshape(inner // 8, 8, 128), axis=0)
        bias_sum = bias_sum + jnp.sum(pre_one.reshape(inner // 8, 8, 128), axis=0)
        return first_sum, bias_sum

    none = jnp.zeros((8, 128), F32)
    first_sum, bias_sum = lax.fori_loop(0, HALF, block, (none, none), unroll=UNROLL_ROWS)
    last_sum, mid_sum = (
        product[0:128, 0:128] + (product[0:128, 128:256] + product[128:256, 0:128])
        for product in (dot(two[...], slopes[...]), dot(one[...], pre[...]))
    )
    low_32 = low_lanes(32)
    grad_last = last_sum[0:64] + swap(last_sum[64:128])
    last_rows = jnp.where(low_32, grad_last[0:32], swap(grad_last[32:64]))
    grad_mid = mid_sum[0:64] + swap(mid_sum[64:128])
    mid_rows = jnp.where(low_32, grad_mid[0:32], swap(grad_mid[32:64]))
    first = jnp.sum(first_sum, axis=0, keepdims=True)
    bias = jnp.sum(bias_sum, axis=0, keepdims=True)
    first = first + swap(first)
    bias = bias + swap(bias)
    joined = jnp.where(low_lanes(1), first, bias)
    joined_high = joined.astype(BF16).astype(F32)
    row_index = lax.broadcasted_iota(jnp.int32, (8, 128), 0)
    joined_rows = jnp.where(
        row_index == 0, joined_high, jnp.where(row_index == 1, joined - joined_high, 0.0)
    )
    for device in range(out.shape[0]):
        half = slice(16 * (device % 2), 16 * (device % 2) + 16)
        tail = [last_rows[half], mid_rows[half], joined_rows]
        out[device, half_rows:, :] = jnp.concatenate(tail, axis=0).astype(BF16)


def sums_kernel(received, half, joined_out):
    half_rows = received.shape[1] - 40
    mid = jnp.zeros((16, 128), F32)
    joined = jnp.zeros((8, 128), F32)
    for source in range(received.shape[0]):
        lanes = slice(64 * source, 64 * source + 64)
        last = received[source, half_rows : half_rows + 16, :]
        half[0:16, lanes] = last[:, 0:64]
        half[16:32, lanes] = last[:, 64:128]
        mid = mid + received[source, half_rows + 16 : half_rows + 32, :].astype(F32)
        joined = joined + received[source, half_rows + 32 : half_rows + 40, :].astype(F32)
    mid = jnp.concatenate([mid, swap(mid)], axis=0)
    high = mid.astype(BF16).astype(F32)
    columns = 64 * received.shape[0]
    rest = swap(mid - high)
    half[:, columns : columns + 128] = jnp.where(low_lanes(32), high, rest).astype(BF16)
    joined_out[...] = joined


def tokens_kernel(received, grad_tokens):
    half_rows = grad_tokens.shape[0] // 2
    for source in range(received.shape[0]):
        lanes = slice(64 * source, 64 * source + 64)
        tile = received[source, 0:half_rows, :]
        grad_tokens[0:half_rows, lanes] = tile[:, 0:64]
        grad_tokens[half_rows:, lanes] = tile[:, 64:128]


def weights_kernel(loss_scale, joined, mine, other, grad_first, grad_bias, grad_mid, grad_last):
    odd = lax.rem(lax.axis_index("ctx"), 2)
    columns = grad_last.shape[1]
    for source, parity in ((mine, odd), (other, 1 - odd)):
        last = source[:, 0:columns].astype(F32) * loss_scale
        grad_last[pl.ds(pl.multiple_of(16 * parity, 16), 16), :] = last[0:16]
        grad_last[pl.ds(pl.multiple_of(32 + 16 * parity, 16), 16), :] = last[16:32]
        mid = source[:, columns : columns + 128].astype(F32) * loss_scale
        mid = (mid + swap(mid))[:, 0:64]
        grad_mid[pl.ds(pl.multiple_of(16 * parity, 16), 16), :] = mid[0:16]
        grad_mid[pl.ds(pl.multiple_of(32 + 16 * parity, 16), 16), :] = mid[16:32]
    first = (joined[0:1] + joined[1:2]) * loss_scale
    grad_first[...] = first[:, 0:64]
    grad_bias[...] = first[:, 64:128]


def call(kernel, out_shape, scratch=(), flops=0, limit=24, **specs):
    return pl.pallas_call(
        kernel,
        out_shape=out_shape,
        **specs,
        scratch_shapes=list(scratch),
        compiler_params=pltpu.CompilerParams(vmem_limit_bytes=limit << 20),
        cost_estimate=pl.CostEstimate(flops=flops, bytes_accessed=1 << 20, transcendentals=0),
    )


def shape(dims, dtype):
    return jax.ShapeDtypeStruct(dims, dtype)


ON_HBM = pl.BlockSpec(memory_space=pltpu.HBM)
ON_VMEM = pl.BlockSpec(memory_space=pltpu.VMEM)


def passed_places(length, wide, narrow):
    bins = 2 * (HALF + 1) * (2 * length // RADIX)
    parts = [wide.at[pl.ds(0, bins), :]]
    parts += [wide.at[pl.ds(bins + index * length, length), :] for index in range(2)]
    parts += [wide.at[pl.ds(bins + 2 * length, 8), :]]
    parts += [narrow.at[pl.ds(256 * index, 256), :] for index in range(2)]
    return parts + [narrow.at[pl.ds(512, 256), pl.ds(256 * index, 256)] for index in range(2)]


def passed_shapes(length):
    bins = 2 * (HALF + 1) * (2 * length // RADIX)
    return [shape((bins + 2 * length + 8, 128), F32), shape((512 + 256, length), BF16)]


def held_arrays(length):
    bins = 2 * (HALF + 1) * (2 * length // RADIX)
    held = [pltpu.VMEM((rows, 128), F32) for rows in (bins, length, length, 8)]
    held += [pltpu.VMEM((256, length), BF16)] * 2 + [pltpu.VMEM((256, 256), BF16)] * 2
    return held + [pltpu.SemaphoreType.DMA((len(held),))]


def spectrum_call(length, *operands):
    inner = 2 * length // RADIX
    return call(
        functools.partial(kernel_spectrum_kernel, length),
        passed_shapes(length),
        scratch=held_arrays(length)
        + [pltpu.VMEM((length, 128), F32), pltpu.VMEM((HALF + 1, 3 * inner, 256), BF16)],
        flops=4 << 30,
        limit=FIRST_LIMIT,
        out_specs=[ON_HBM] * 2,
    )(*operands)


def gradient_call(length, *operands):
    inner = 2 * length // RADIX
    local_rows = 128
    return call(
        functools.partial(gradient_kernel, length),
        shape((length // local_rows, local_rows // 2 + 40, 128), BF16),
        scratch=held_arrays(length)
        + [
            pltpu.VMEM((HALF + 1, 3 * inner, 256), BF16),
            pltpu.VMEM((HALF + 1, inner, 256), F32),
        ]
        + [pltpu.VMEM((length, 256), BF16)] * 2
        + [pltpu.VMEM((inner, 128), F32)],
        flops=8 << 30,
        limit=SECOND_LIMIT,
        in_specs=[ON_VMEM] + [ON_HBM] * 2 + [ON_VMEM] * 2,
    )(*operands)


def by_channels(tokens_in, grad_out, decay_rate, w_in, b_in, w_mid, w_out):
    devices = lax.axis_size("ctx")
    local_rows = tokens_in.shape[0]
    length = local_rows * devices
    matrix, twiddle = dft_tables(2 * length)
    packed = call(
        pack_kernel,
        shape((devices, local_rows, 128), BF16),
        scratch=[pltpu.VMEM(tokens_in.shape, BF16)] * 2
        + [
            pltpu.VMEM((devices, local_rows, 128), BF16),
            pltpu.SemaphoreType.DMA((PACK_PARTS, 2)),
            pltpu.SemaphoreType.DMA((PACK_PARTS,)),
        ],
        limit=58,
        in_specs=[ON_HBM] * 2,
        out_specs=ON_HBM,
    )(tokens_in, grad_out)
    signal = lax.all_to_all(packed, "ctx", split_axis=0, concat_axis=0, tiled=True)
    forward = spectrum_call(
        length, decay_rate.reshape(1, -1), w_in.reshape(1, -1), b_in.reshape(1, -1), w_mid, w_out,
        matrix, twiddle,
    )
    sent = gradient_call(length, signal.reshape(length, 128), *forward, matrix, twiddle)
    received = lax.all_to_all(sent, "ctx", split_axis=0, concat_axis=0, tiled=True)
    half, joined = call(
        sums_kernel, [shape((32, 64 * devices + 128), BF16), shape((8, 128), F32)]
    )(received)
    other = lax.ppermute(half, "ctx", [(index, index ^ 1) for index in range(devices)])
    input_grad = call(tokens_kernel, shape(tokens_in.shape, BF16), flops=1 << 26)(received)
    grad_first, grad_bias, grad_mid, grad_last = call(
        functools.partial(weights_kernel, 1.0 / math.sqrt(length)),
        [shape((1, 64), F32), shape((1, 64), F32), shape((64, 64), F32), shape(w_out.shape, F32)],
    )(joined, half, other)
    return input_grad, grad_first.reshape(64), grad_bias.reshape(64), grad_mid, grad_last


HIGHEST = lax.Precision.HIGHEST
TWO_PI = 2.0 * math.pi


def phase_angle(product, period):
    return TWO_PI / period * (product % period).astype(jnp.float32)


def frequency_rows(devices):
    row_index = jnp.arange(2 * devices, dtype=jnp.int32)
    row_block = row_index // 2
    second = row_index % 2
    paired = jnp.where(row_block == 0, devices, 2 * devices - row_block)
    return jnp.where(second == 0, row_block, paired)


def source_rows(devices):
    row_index = jnp.arange(2 * devices, dtype=jnp.int32)
    return row_index // 2 + row_index % 2 * devices


def envelope(lag_values, decay_rate, length):
    double = 2.0 * decay_rate
    geometric = 1.0 + 2.0 * jnp.exp(-double) * jnp.expm1(-double * (length - 1)) / jnp.expm1(
        -double
    )
    distance = jnp.abs(lag_values).astype(jnp.float32)[..., None]
    live_mask = (lag_values != -length).astype(jnp.float32)[..., None]
    return live_mask * lax.rsqrt(geometric) * jnp.exp(-distance * decay_rate)


def position_mlp(scaled, w_first, w_bias, w_middle, w_last):
    hidden_one = jax.nn.silu(scaled[..., None] * w_first + w_bias)
    hidden_two = jax.nn.silu(jnp.dot(hidden_one, w_middle, precision=HIGHEST))
    return jnp.dot(hidden_two, w_last, precision=HIGHEST)


def rotate(real_a, imag_a, real_b, imag_b):
    return (real_a * real_b - imag_a * imag_b, real_a * imag_b + imag_a * real_b)


def first_section(signal, columns, freq_order, local_slab, padded):
    freq_count = freq_order.shape[0]
    angles = phase_angle(freq_order[:, None] * columns[None, :], freq_count)
    real_part = jnp.einsum("fp,prc->frc", jnp.cos(angles), signal, precision=HIGHEST)
    imag_part = jnp.einsum("fp,prc->frc", -jnp.sin(angles), signal, precision=HIGHEST)
    twiddle = phase_angle(freq_order[:, None] * local_slab[None, :], padded)[:, :, None]
    return rotate(real_part, imag_part, jnp.cos(twiddle), -jnp.sin(twiddle))


def along_rows(stacked, direction):
    row_count = stacked.shape[1]
    half_width = stacked.shape[2] // 2
    positions = jnp.arange(row_count, dtype=jnp.int32)
    angles = phase_angle(positions[:, None] * positions[None, :], row_count)
    with_cos = jnp.einsum("gm,imc->igc", jnp.cos(angles), stacked, precision=HIGHEST)
    with_sin = jnp.einsum("gm,imc->igc", direction * jnp.sin(angles), stacked, precision=HIGHEST)
    real_part = with_cos[..., :half_width] - with_sin[..., half_width:]
    imag_part = with_cos[..., half_width:] + with_sin[..., :half_width]
    return (real_part, imag_part)


def last_section(stacked, out_rows, freq_order, padded):
    freq_count = freq_order.shape[0]
    half_width = stacked.shape[2] // 2
    angles = phase_angle(out_rows[:, None] * freq_order[None, :], freq_count)
    cos_table = jnp.cos(angles) / padded
    sin_table = jnp.sin(angles) / padded
    real_in = stacked[..., :half_width]
    imag_in = stacked[..., half_width:]
    leading, trailing, factor = (real_in, imag_in, -1.0)
    return jnp.einsum("pf,frc->prc", cos_table, leading, precision=HIGHEST) + factor * jnp.einsum(
        "pf,frc->prc", sin_table, trailing, precision=HIGHEST
    )


def by_frequencies(tokens_in, grad_out, decay_rate, w_in, b_in, w_mid, w_out):
    devices = lax.axis_size("ctx")
    own_index = lax.axis_index("ctx")
    tok_rows = tokens_in.shape[0]
    slab_rows = tok_rows // devices
    length = tok_rows * devices
    padded = 2 * length
    freq_order = frequency_rows(devices)
    lag_rows = source_rows(devices)
    token_cols = jnp.arange(devices, dtype=jnp.int32)
    local_slab = own_index * slab_rows + jnp.arange(slab_rows, dtype=jnp.int32)
    pair_index = jnp.arange(2, dtype=jnp.int32)
    local_freq = jnp.where(
        pair_index == 0, own_index, jnp.where(own_index == 0, devices, 2 * devices - own_index)
    )
    circular = (own_index + pair_index * devices)[:, None] * tok_rows + jnp.arange(
        tok_rows, dtype=jnp.int32
    )[None, :]
    lag_values = jnp.where(circular < length, circular, circular - padded)
    scaled = lag_values.astype(jnp.float32) / length
    weights_env = envelope(lag_values, decay_rate, length)

    def position_net(w_first, w_bias, w_middle, w_last):
        return position_mlp(scaled, w_first, w_bias, w_middle, w_last)

    position, pull_back = jax.vjp(position_net, w_in, b_in, w_mid, w_out)
    kernel = (position * weights_env).astype(jnp.bfloat16)
    tokens_mid, grads_mid, kernel_mid = (
        lax.all_to_all(tokens_in[None], "ctx", split_axis=1, concat_axis=0, tiled=True),
        lax.all_to_all(grad_out[None], "ctx", split_axis=1, concat_axis=0, tiled=True),
        lax.all_to_all(kernel, "ctx", split_axis=1, concat_axis=0, tiled=True),
    )
    token_real, token_imag = first_section(
        tokens_mid.astype(jnp.float32), token_cols, freq_order, local_slab, padded
    )
    cotan_real, cotan_imag = first_section(
        grads_mid.astype(jnp.float32), token_cols, freq_order, local_slab, padded
    )
    kern_real, kern_imag = first_section(
        kernel_mid.astype(jnp.float32), lag_rows, freq_order, local_slab, padded
    )
    kernel_stack = jnp.concatenate([kern_real, kern_imag], axis=2)
    token_stack = jnp.concatenate([token_real, token_imag], axis=2)
    cotan_stack = jnp.concatenate([cotan_real, cotan_imag], axis=2)
    token_spec, cotan_spec, kernel_spec = (
        lax.all_to_all(token_stack, "ctx", split_axis=0, concat_axis=1, tiled=True),
        lax.all_to_all(cotan_stack, "ctx", split_axis=0, concat_axis=1, tiled=True),
        lax.all_to_all(kernel_stack, "ctx", split_axis=0, concat_axis=1, tiled=True),
    )
    spec_token_real, spec_token_imag = along_rows(token_spec, -1.0)
    spec_cotan_real, spec_cotan_imag = along_rows(cotan_spec, -1.0)
    spec_kern_real, spec_kern_imag = along_rows(kernel_spec, -1.0)
    input_real = spec_kern_real * spec_cotan_real + spec_kern_imag * spec_cotan_imag
    input_imag = spec_kern_real * spec_cotan_imag - spec_kern_imag * spec_cotan_real
    lagged_real = spec_cotan_real * spec_token_real + spec_cotan_imag * spec_token_imag
    lagged_imag = spec_cotan_imag * spec_token_real - spec_cotan_real * spec_token_imag
    positions = jnp.arange(tok_rows, dtype=jnp.int32)
    back_angle = phase_angle(local_freq[:, None] * positions[None, :], padded)[:, :, None]
    back_cos = jnp.cos(back_angle)
    back_sin = jnp.sin(back_angle)

    def inverse_rows(real_part, imag_part):
        stacked = jnp.concatenate([real_part, imag_part], axis=2)
        out_real, out_imag = along_rows(stacked, 1.0)
        turned_real, turned_imag = rotate(out_real, out_imag, back_cos, back_sin)
        return jnp.concatenate([turned_real, turned_imag], axis=2)

    spread_input, spread_lagged = (
        lax.all_to_all(
            inverse_rows(input_real, input_imag), "ctx", split_axis=1, concat_axis=0, tiled=True
        ),
        lax.all_to_all(
            inverse_rows(lagged_real, lagged_imag), "ctx", split_axis=1, concat_axis=0, tiled=True
        ),
    )
    input_rows = last_section(spread_input, token_cols, freq_order, padded)
    lagged_rows = last_section(spread_lagged, lag_rows, freq_order, padded)
    input_back, lag_back = (
        lax.all_to_all(input_rows, "ctx", split_axis=0, concat_axis=1, tiled=True),
        lax.all_to_all(lagged_rows, "ctx", split_axis=0, concat_axis=1, tiled=True),
    )
    input_grad = input_back[0]
    gradients = pull_back(lag_back * weights_env)
    summed = lax.psum((gradients[0], gradients[1], gradients[2], gradients[3]), "ctx")
    loss_scale = 1.0 / math.sqrt(length)
    return (
        input_grad.astype(jnp.bfloat16),
        summed[0] * loss_scale,
        summed[1] * loss_scale,
        summed[2] * loss_scale,
        summed[3] * loss_scale,
    )


def on_device(tokens_in, grad_out, decay_rate, w_in, b_in, w_mid, w_out):
    devices = lax.axis_size("ctx")
    fits = (
        tokens_in.shape == (128, 64 * devices)
        and devices % 2 == 0
        and devices * 128 % (128 * HALF) == 0
        and w_mid.shape == (64, 64)
    )
    form = by_channels if fits else by_frequencies
    return form(tokens_in, grad_out, decay_rate, w_in, b_in, w_mid, w_out)


def solution(mesh):
    in_specs = (P(("groups", "ctx"), None), P(("groups", "ctx"), None), P(), P(), P(), P(), P())
    out_specs = (
        P(("groups", "ctx"), None),
        P("groups"),
        P("groups"),
        P("groups", None),
        P("groups", None),
    )
    return jax.shard_map(
        on_device, mesh=mesh, in_specs=in_specs, out_specs=out_specs, check_vma=False
    )
```

```python
import functools
import math

import jax
import jax.numpy as jnp
import numpy as np
from jax import lax
from jax.experimental import pallas as pl
from jax.experimental.pallas import tpu as pltpu
from jax.sharding import PartitionSpec as P

RADIX = 16
HALF = RADIX // 2
CHUNK = 32
UNROLL_CHUNK = 8
UNROLL_BIN = 9
UNROLL_ROWS = 8
PACK_PARTS = 4
FIRST_LIMIT = 56
SECOND_LIMIT = 50
F32 = jnp.float32
BF16 = jnp.bfloat16


def split_pair(value):
    high = value.astype(BF16)
    return high, (value - high.astype(F32)).astype(BF16)


def dot(left, right):
    return jnp.dot(left, right, preferred_element_type=F32)


def pair_lanes(value):
    return jnp.concatenate(split_pair(value), axis=1)


def square(matrix):
    high, low = split_pair(matrix)
    return jnp.concatenate(
        [
            jnp.concatenate([high, low], axis=1),
            jnp.concatenate([high, jnp.zeros_like(low)], axis=1),
        ],
        axis=0,
    )


def dot_pair(rows, squared):
    product = dot(rows, squared)
    return product[:, 0:128] + product[:, 128:256]


def tall_three(value):
    high, low = split_pair(value)
    return jnp.concatenate([high, high, low], axis=0)


def dft_tables(padded):
    inner = padded // RADIX
    grid = np.outer(np.arange(inner), np.arange(inner)) % inner
    angles = 2.0 * np.pi * grid / inner
    matrix = np.concatenate([np.cos(angles), np.sin(angles)], axis=0)
    high = matrix.astype(jnp.bfloat16)
    low = (matrix - high.astype(np.float64)).astype(jnp.bfloat16)
    matrix = np.concatenate([high, low, high], axis=1)
    turn = 2.0 * np.pi * np.outer(np.arange(inner), np.arange(RADIX)) / padded
    twiddle = np.zeros((inner, 128), np.float32)
    twiddle[:, :RADIX] = np.cos(turn)
    twiddle[:, RADIX : 2 * RADIX] = np.sin(turn)
    return jnp.asarray(matrix), jnp.asarray(twiddle)


def cos_of(index):
    return math.cos(2.0 * math.pi * index / RADIX)


def sin_of(index):
    return math.sin(2.0 * math.pi * index / RADIX)


def spread(x):
    plus = [x[q] + x[q + 4] for q in range(4)]
    minus = [x[q] - x[q + 4] for q in range(4)]
    root = math.sqrt(0.5)
    out = [None] * 9
    even, odd = plus[0] + plus[2], plus[1] + plus[3]
    out[0] = (even + odd, None)
    out[8] = (even - odd, None)
    out[4] = (plus[0] - plus[2], plus[3] - plus[1])
    across, along = root * (minus[1] - minus[3]), root * (minus[1] + minus[3])
    out[2] = (minus[0] + across, -minus[2] - along)
    out[6] = (minus[0] - across, minus[2] - along)
    differ = {q: x[q] - x[8 - q] for q in (1, 2, 3)}
    same = {q: x[q] + x[8 - q] for q in (1, 2, 3)}
    for j in (1, 3):
        real_even = x[0] + cos_of(2 * j) * differ[2]
        real_odd = cos_of(j) * differ[1] + cos_of(3 * j) * differ[3]
        imag_even = sin_of(4 * j) * x[4] + sin_of(2 * j) * same[2]
        imag_odd = sin_of(j) * same[1] + sin_of(3 * j) * same[3]
        out[j] = (real_even + real_odd, -(imag_odd + imag_even))
        out[8 - j] = (real_even - real_odd, imag_even - imag_odd)
    return out


def gather_back(real, imag):
    even, odd = [None] * 8, [None] * 8
    total, differ = real[0] + real[8], real[0] - real[8]
    real_sum, real_dif = real[2] + real[6], real[2] - real[6]
    imag_sum, imag_dif = imag[2] + imag[6], imag[2] - imag[6]
    root = math.sqrt(0.5)
    even[0] = total + real_sum + real[4]
    even[4] = total - real_sum + real[4]
    even[2] = total - imag_dif - real[4]
    even[6] = total + imag_dif - real[4]
    first, second = root * (real_dif - imag_sum), root * (real_dif + imag_sum)
    even[1] = differ + first - imag[4]
    even[5] = differ - first - imag[4]
    even[3] = differ - second + imag[4]
    even[7] = differ + second + imag[4]
    one_sum, one_dif = real[1] + real[7], real[1] - real[7]
    three_sum, three_dif = real[3] + real[5], real[3] - real[5]
    ione_sum, ione_dif = imag[1] + imag[7], imag[1] - imag[7]
    ithree_sum, ithree_dif = imag[3] + imag[5], imag[3] - imag[5]
    odd[0] = one_sum + three_sum
    odd[4] = ithree_dif - ione_dif
    for q in (1, 2, 3):
        if q % 2 == 0:
            cosines = cos_of(q) * one_sum + cos_of(3 * q) * three_sum
            sines = sin_of(q) * ione_dif + sin_of(3 * q) * ithree_dif
        else:
            cosines = cos_of(q) * one_dif + cos_of(3 * q) * three_dif
            sines = sin_of(q) * ione_sum + sin_of(3 * q) * ithree_sum
        odd[q] = cosines - sines
        odd[8 - q] = -cosines - sines
    return even, odd


def residues_to_scratch(load, twiddle, stage, inner):
    def chunk(step, carry):
        start = pl.multiple_of(step * CHUNK, CHUNK)
        turn = twiddle[pl.ds(start, CHUNK), :]
        for j, (real, imag) in enumerate(spread([load(q * inner + start) for q in range(HALF)])):
            if j > 0:
                cosine, sine = turn[:, j : j + 1], turn[:, RADIX + j : RADIX + j + 1]
                if imag is None:
                    real, imag = real * cosine, -real * sine
                else:
                    real, imag = real * cosine + imag * sine, imag * cosine - real * sine
            else:
                imag = jnp.zeros_like(real)
            for part, value in enumerate((real, imag)):
                high, low = split_pair(value)
                lanes = slice(128 * part, 128 * part + 128)
                stage[j, pl.ds(start, CHUNK), lanes] = high
                stage[j, pl.ds(inner + start, CHUNK), lanes] = high
                stage[j, pl.ds(2 * inner + start, CHUNK), lanes] = low
        return carry

    lax.fori_loop(0, inner // CHUNK, chunk, 0, unroll=UNROLL_CHUNK)


def inner_dft(stacked, matrix, inner, direction):
    reals, imags = [], []
    for row in range(0, inner, 128):
        cosines = dot(matrix[row : row + 128, :], stacked)
        sines = dot(matrix[inner + row : inner + row + 128, :], stacked)
        cos_real, cos_imag = cosines[:, :128], cosines[:, 128:]
        sin_real, sin_imag = sines[:, :128], sines[:, 128:]
        reals.append(cos_real + sin_imag if direction > 0 else cos_real - sin_imag)
        imags.append(cos_imag - sin_real if direction > 0 else cos_imag + sin_real)
    return jnp.concatenate(reals, axis=0), jnp.concatenate(imags, axis=0)


def low_lanes(rows):
    return lax.broadcasted_iota(jnp.int32, (rows, 128), 1) < 64


def swap(value):
    return pltpu.roll(value, 64, 1)


def copies_of(sources, buffers, semaphores):
    return [
        pltpu.make_async_copy(source, buffer, semaphores.at[index])
        for index, (source, buffer) in enumerate(zip(sources, buffers))
    ]


def fetch(sources, buffers, semaphores):
    copies = copies_of(sources, buffers, semaphores)
    for copy in copies:
        copy.start()
    return copies


def pack_kernel(tokens_hbm, cotan_hbm, out_hbm, tokens, cotan, out, load_semaphores, store_semaphores):
    loads, stores = [], []
    rows_each = tokens.shape[0] // PACK_PARTS
    for part in range(PACK_PARTS):
        rows = pl.ds(part * rows_each, rows_each)
        loads.append(
            fetch(
                (tokens_hbm.at[rows, :], cotan_hbm.at[rows, :]),
                (tokens.at[rows, :], cotan.at[rows, :]),
                load_semaphores.at[part],
            )
        )
    for part in range(PACK_PARTS):
        rows = pl.ds(part * rows_each, rows_each)
        for copy in loads[part]:
            copy.wait()
        for block in range(out.shape[0]):
            lanes = slice(64 * block, 64 * block + 64)
            out[block, rows, :] = jnp.concatenate([tokens[rows, lanes], cotan[rows, lanes]], axis=1)
        store = pltpu.make_async_copy(
            out.at[:, rows, :], out_hbm.at[:, rows, :], store_semaphores.at[part]
        )
        store.start()
        stores.append(store)
    for store in stores:
        store.wait()


def diagonal(matrix):
    empty = jnp.zeros_like(matrix)
    return jnp.concatenate(
        [jnp.concatenate([matrix, empty], axis=1), jnp.concatenate([empty, matrix], axis=1)], axis=0
    )


def twice(row):
    return jnp.concatenate([row, row], axis=1)


def exp_minus_one(value):
    series = jnp.ones_like(value)
    for order in range(9, 1, -1):
        series = 1.0 + series * value * (1.0 / order)
    return jnp.where(jnp.abs(value) < 0.35, value * series, jnp.exp(value) - 1.0)


def kernel_spectrum_kernel(
    length, rates, w_first, w_bias, w_mid, w_last, matrix, twiddle, wide_hbm, narrow_hbm,
    spectrum, slope_two, slope_one, consts, one, two, mid_back, last_back, semaphores, taps, stage,
):
    inner = 2 * length // RADIX
    low_half = low_lanes(inner)
    own = lax.axis_index("ctx")
    lanes = pl.ds(pl.multiple_of(own // 2 * 128, 128), 128)
    odd = own % 2 == 1
    last = w_last[:, lanes]
    last = diagonal(jnp.where(odd, swap(last), last)[:, 0:64])
    rate = rates[:, lanes]
    rate = twice(jnp.where(odd, swap(rate), rate)[:, 0:64])
    double = 2.0 * rate
    ratio = exp_minus_one(-double * (length - 1)) / exp_minus_one(-double)
    geometric = 1.0 + 2.0 * jnp.exp(-double) * ratio
    scale = lax.rsqrt(geometric)
    mid = diagonal(w_mid[...])
    mid_back[...] = square(mid.T)
    last_back[...] = square(last.T)
    mid, last = square(mid), square(last)
    first, bias = twice(w_first[...]), twice(w_bias[...])
    consts[...] = jnp.concatenate([rate, scale, first, bias, jnp.zeros((4, 128), F32)], axis=0)

    def block(step, carry):
        start = pl.multiple_of(step * inner, inner)
        rows = pl.ds(start, inner)
        place = start + lax.broadcasted_iota(jnp.int32, (inner, 128), 0)
        lag = jnp.where(low_half, place, place - length)
        scaled = lag.astype(F32) / length
        pre_one = scaled * first + bias
        gate_one = 1.0 / (1.0 + jnp.exp(-pre_one))
        hidden_one = pre_one * gate_one
        slope_one[rows, :] = gate_one * (1.0 + pre_one * (1.0 - gate_one))
        pre_two = dot_pair(pair_lanes(hidden_one), mid)
        gate_two = 1.0 / (1.0 + jnp.exp(-pre_two))
        hidden_two = pre_two * gate_two
        slope_two[rows, :] = gate_two * (1.0 + pre_two * (1.0 - gate_two))
        position = dot_pair(pair_lanes(hidden_two), last)
        live = jnp.where(lag == -length, 0.0, 1.0)
        env = live * scale * jnp.exp(-jnp.abs(lag).astype(F32) * rate)
        taps[rows, :] = (position * env).astype(BF16).astype(F32)
        one[0:128, rows], one[128:256, rows] = split_pair(hidden_one.T)
        two[0:128, rows], two[128:256, rows] = split_pair(hidden_two.T)
        return carry

    lax.fori_loop(0, HALF, block, 0, unroll=UNROLL_ROWS)
    places = passed_places(length, wide_hbm, narrow_hbm)
    held = (slope_two, slope_one, consts, one, two, mid_back, last_back)
    copies = fetch(held, places[1:], semaphores)
    residues_to_scratch(lambda start: taps[pl.ds(start, CHUNK), :], twiddle, stage, inner)

    def transform(j, carry):
        real, imag = inner_dft(stage[j], matrix, inner, 1)
        sign = 1.0 - 2.0 * lax.rem(jnp.asarray(j, jnp.int32), 2).astype(F32)
        spectrum[pl.ds((2 * j + 0) * inner, inner), :] = real + sign * swap(real)
        spectrum[pl.ds((2 * j + 1) * inner, inner), :] = imag + sign * swap(imag)
        return carry

    lax.fori_loop(0, HALF + 1, transform, 0, unroll=UNROLL_BIN)
    last_copy = pltpu.make_async_copy(spectrum, places[0], semaphores.at[len(copies)])
    last_copy.start()
    for copy in copies + [last_copy]:
        copy.wait()


def gradient_kernel(
    length, signal, wide_hbm, narrow_hbm, matrix, twiddle, out,
    spectrum, slope_two, slope_one, consts, one, two, mid_back, last_back, semaphores, stage, back_ref,
    slopes, pre, decay,
):
    padded = 2 * length
    inner = padded // RADIX
    low_half = low_lanes(inner)
    held = (spectrum, slope_two, slope_one, consts, one, two, mid_back, last_back)
    copies = copies_of(passed_places(length, wide_hbm, narrow_hbm), held, semaphores)
    first_needed, needed_later = (copies[0], copies[3]), copies[1:3] + copies[4:]
    for copy in first_needed:
        copy.start()
    residues_to_scratch(
        lambda start: signal[pl.ds(start, CHUNK), :].astype(F32), twiddle, stage, inner
    )
    for copy in needed_later:
        copy.start()

    def analyse(j, carry):
        real, imag = inner_dft(stage[j], matrix, inner, 1)
        back_ref[j, :, 0:128] = real
        back_ref[j, :, 128:256] = imag
        return carry

    lax.fori_loop(0, HALF + 1, analyse, 0, unroll=UNROLL_BIN)
    for copy in first_needed:
        copy.wait()

    def transform(j, carry):
        real, imag = back_ref[j, :, 0:128], back_ref[j, :, 128:256]
        real_swap, imag_swap = swap(real), swap(imag)
        cotan_real = jnp.where(low_half, real_swap, real)
        cotan_imag = jnp.where(low_half, imag_swap, imag)
        other_real = jnp.where(low_half, spectrum[pl.ds((2 * j + 0) * inner, inner), :], real_swap)
        other_imag = jnp.where(low_half, spectrum[pl.ds((2 * j + 1) * inner, inner), :], imag_swap)
        product = jnp.concatenate(
            [
                cotan_real * other_real + cotan_imag * other_imag,
                cotan_imag * other_real - cotan_real * other_imag,
            ],
            axis=1,
        )
        real, imag = inner_dft(tall_three(product), matrix, inner, -1)
        back_ref[j, :, 0:128] = real
        back_ref[j, :, 128:256] = imag
        return carry

    lax.fori_loop(0, HALF + 1, transform, 0, unroll=UNROLL_BIN)
    rate, scale, first, bias = (consts[index : index + 1, :] for index in range(4))
    place = lax.broadcasted_iota(jnp.int32, (inner, 128), 0)
    near = jnp.where(low_half, place, inner - 1 - place).astype(F32)
    decay[...] = jnp.exp(-near * rate)
    low_row = low_lanes(1)

    def unspread(step, carry):
        start = pl.multiple_of(step * CHUNK, CHUNK)
        rows = pl.ds(start, CHUNK)
        turn = twiddle[rows, :]
        real_list, imag_list = [], []
        for j in range(HALF + 1):
            weight = (1.0 if j in (0, HALF) else 2.0) / padded
            real, imag = back_ref[j, rows, 0:128], back_ref[j, rows, 128:256]
            if j == 0:
                real_list.append(real * weight)
                imag_list.append(None)
                continue
            cosine = turn[:, j : j + 1] * weight
            sine = turn[:, RADIX + j : RADIX + j + 1] * weight
            real_list.append(real * cosine - imag * sine)
            imag_list.append(real * sine + imag * cosine)
        even, odd = gather_back(real_list, imag_list)
        for q in range(HALF):
            joined, apart = even[q] + odd[q], even[q] - odd[q]
            back_ref[q, rows, 0:128] = joined
            at = pl.ds(q * inner + start, CHUNK)
            lag_grad = jnp.where(low_lanes(CHUNK), swap(joined), apart)
            far = jnp.where(low_row, q * inner, length - q * inner - inner + 1).astype(F32)
            weighted = lag_grad * (scale * jnp.exp(-far * rate)) * decay[rows, :]
            if q == 0:
                row = start + lax.broadcasted_iota(jnp.int32, (CHUNK, 128), 0)
                weighted = jnp.where((row == 0) & ~low_lanes(CHUNK), 0.0, weighted)
            slopes[at, :] = pair_lanes(weighted)
        return carry

    lax.fori_loop(0, inner // CHUNK, unspread, 0, unroll=UNROLL_CHUNK)
    for copy in needed_later:
        copy.wait()
    local_rows = 128
    half_rows = local_rows // 2

    def block(q, carry):
        start = pl.multiple_of(q * inner, inner)
        rows = pl.ds(start, inner)
        for part in range(inner // local_rows):
            base = part * local_rows
            upper = back_ref[q, base : base + half_rows, 0:128]
            lower = back_ref[q, base + half_rows : base + local_rows, 0:128]
            out[q * (inner // local_rows) + part, 0:half_rows, :] = jnp.where(
                low_half[:half_rows], upper, swap(lower)
            ).astype(BF16)
        return carry

    pre[...] = pair_lanes(dot_pair(slopes[...], last_back[...]) * slope_two[...])
    lax.fori_loop(0, HALF, block, 0, unroll=UNROLL_ROWS)
    last_product = dot(two[...], slopes[...])

    def first_layer(q, carry):
        first_sum, bias_sum = carry
        start = pl.multiple_of(q * inner, inner)
        rows = pl.ds(start, inner)
        base = jnp.where(low_row, start, start - length)
        scaled = (place + base).astype(F32) * (1.0 / length)
        pre_one = dot_pair(pre[rows, :], mid_back[...]) * slope_one[rows, :]
        first_sum = first_sum + jnp.sum((pre_one * scaled).reshape(inner // 8, 8, 128), axis=0)
        bias_sum = bias_sum + jnp.sum(pre_one.reshape(inner // 8, 8, 128), axis=0)
        return first_sum, bias_sum

    none = jnp.zeros((8, 128), F32)
    first_sum, bias_sum = lax.fori_loop(0, HALF, first_layer, (none, none), unroll=UNROLL_ROWS)
    last_sum, mid_sum = (
        product[0:128, 0:128] + (product[0:128, 128:256] + product[128:256, 0:128])
        for product in (last_product, dot(one[...], pre[...]))
    )
    low_32 = low_lanes(32)
    grad_last = last_sum[0:64] + swap(last_sum[64:128])
    last_rows = jnp.where(low_32, grad_last[0:32], swap(grad_last[32:64]))
    grad_mid = mid_sum[0:64] + swap(mid_sum[64:128])
    mid_rows = jnp.where(low_32, grad_mid[0:32], swap(grad_mid[32:64]))
    first = jnp.sum(first_sum, axis=0, keepdims=True)
    bias = jnp.sum(bias_sum, axis=0, keepdims=True)
    first = first + swap(first)
    bias = bias + swap(bias)
    joined = jnp.where(low_lanes(1), first, bias)
    joined_high = joined.astype(BF16).astype(F32)
    row_index = lax.broadcasted_iota(jnp.int32, (8, 128), 0)
    joined_rows = jnp.where(
        row_index == 0, joined_high, jnp.where(row_index == 1, joined - joined_high, 0.0)
    )
    for device in range(out.shape[0]):
        half = slice(16 * (device % 2), 16 * (device % 2) + 16)
        tail = [last_rows[half], mid_rows[half], joined_rows]
        out[device, half_rows:, :] = jnp.concatenate(tail, axis=0).astype(BF16)


def sums_kernel(received, half, joined_out):
    half_rows = received.shape[1] - 40
    mid = jnp.zeros((16, 128), F32)
    joined = jnp.zeros((8, 128), F32)
    for source in range(received.shape[0]):
        lanes = slice(64 * source, 64 * source + 64)
        last = received[source, half_rows : half_rows + 16, :]
        half[0:16, lanes] = last[:, 0:64]
        half[16:32, lanes] = last[:, 64:128]
        mid = mid + received[source, half_rows + 16 : half_rows + 32, :].astype(F32)
        joined = joined + received[source, half_rows + 32 : half_rows + 40, :].astype(F32)
    mid = jnp.concatenate([mid, swap(mid)], axis=0)
    high = mid.astype(BF16).astype(F32)
    columns = 64 * received.shape[0]
    rest = swap(mid - high)
    half[:, columns : columns + 128] = jnp.where(low_lanes(32), high, rest).astype(BF16)
    joined_out[...] = joined


def tokens_kernel(received, grad_tokens):
    half_rows = grad_tokens.shape[0] // 2
    for source in range(received.shape[0]):
        lanes = slice(64 * source, 64 * source + 64)
        tile = received[source, 0:half_rows, :]
        grad_tokens[0:half_rows, lanes] = tile[:, 0:64]
        grad_tokens[half_rows:, lanes] = tile[:, 64:128]


def weights_kernel(loss_scale, joined, mine, other, grad_first, grad_bias, grad_mid, grad_last):
    odd = lax.rem(lax.axis_index("ctx"), 2)
    columns = grad_last.shape[1]
    for source, parity in ((mine, odd), (other, 1 - odd)):
        last = source[:, 0:columns].astype(F32) * loss_scale
        grad_last[pl.ds(pl.multiple_of(16 * parity, 16), 16), :] = last[0:16]
        grad_last[pl.ds(pl.multiple_of(32 + 16 * parity, 16), 16), :] = last[16:32]
        mid = source[:, columns : columns + 128].astype(F32) * loss_scale
        mid = (mid + swap(mid))[:, 0:64]
        grad_mid[pl.ds(pl.multiple_of(16 * parity, 16), 16), :] = mid[0:16]
        grad_mid[pl.ds(pl.multiple_of(32 + 16 * parity, 16), 16), :] = mid[16:32]
    first = (joined[0:1] + joined[1:2]) * loss_scale
    grad_first[...] = first[:, 0:64]
    grad_bias[...] = first[:, 64:128]


def call(kernel, out_shape, scratch=(), flops=0, limit=24, **specs):
    return pl.pallas_call(
        kernel,
        out_shape=out_shape,
        **specs,
        scratch_shapes=list(scratch),
        compiler_params=pltpu.CompilerParams(vmem_limit_bytes=limit << 20),
        cost_estimate=pl.CostEstimate(flops=flops, bytes_accessed=1 << 20, transcendentals=0),
    )


def shape(dims, dtype):
    return jax.ShapeDtypeStruct(dims, dtype)


ON_HBM = pl.BlockSpec(memory_space=pltpu.HBM)
ON_VMEM = pl.BlockSpec(memory_space=pltpu.VMEM)


def passed_places(length, wide, narrow):
    bins = 2 * (HALF + 1) * (2 * length // RADIX)
    parts = [wide.at[pl.ds(0, bins), :]]
    parts += [wide.at[pl.ds(bins + index * length, length), :] for index in range(2)]
    parts += [wide.at[pl.ds(bins + 2 * length, 8), :]]
    parts += [narrow.at[pl.ds(256 * index, 256), :] for index in range(2)]
    return parts + [narrow.at[pl.ds(512, 256), pl.ds(256 * index, 256)] for index in range(2)]


def passed_shapes(length):
    bins = 2 * (HALF + 1) * (2 * length // RADIX)
    return [shape((bins + 2 * length + 8, 128), F32), shape((512 + 256, length), BF16)]


def held_arrays(length):
    bins = 2 * (HALF + 1) * (2 * length // RADIX)
    held = [pltpu.VMEM((rows, 128), F32) for rows in (bins, length, length, 8)]
    held += [pltpu.VMEM((256, length), BF16)] * 2 + [pltpu.VMEM((256, 256), BF16)] * 2
    return held + [pltpu.SemaphoreType.DMA((len(held),))]


def spectrum_call(length, *operands):
    inner = 2 * length // RADIX
    return call(
        functools.partial(kernel_spectrum_kernel, length),
        passed_shapes(length),
        scratch=held_arrays(length)
        + [pltpu.VMEM((length, 128), F32), pltpu.VMEM((HALF + 1, 3 * inner, 256), BF16)],
        flops=4 << 30,
        limit=FIRST_LIMIT,
        out_specs=[ON_HBM] * 2,
    )(*operands)


def gradient_call(length, *operands):
    inner = 2 * length // RADIX
    local_rows = 128
    return call(
        functools.partial(gradient_kernel, length),
        shape((length // local_rows, local_rows // 2 + 40, 128), BF16),
        scratch=held_arrays(length)
        + [
            pltpu.VMEM((HALF + 1, 3 * inner, 256), BF16),
            pltpu.VMEM((HALF + 1, inner, 256), F32),
        ]
        + [pltpu.VMEM((length, 256), BF16)] * 2
        + [pltpu.VMEM((inner, 128), F32)],
        flops=8 << 30,
        limit=SECOND_LIMIT,
        in_specs=[ON_VMEM] + [ON_HBM] * 2 + [ON_VMEM] * 2,
    )(*operands)


def by_channels(tokens_in, grad_out, decay_rate, w_in, b_in, w_mid, w_out):
    devices = lax.axis_size("ctx")
    local_rows = tokens_in.shape[0]
    length = local_rows * devices
    matrix, twiddle = dft_tables(2 * length)
    packed = call(
        pack_kernel,
        shape((devices, local_rows, 128), BF16),
        scratch=[pltpu.VMEM(tokens_in.shape, BF16)] * 2
        + [
            pltpu.VMEM((devices, local_rows, 128), BF16),
            pltpu.SemaphoreType.DMA((PACK_PARTS, 2)),
            pltpu.SemaphoreType.DMA((PACK_PARTS,)),
        ],
        limit=58,
        in_specs=[ON_HBM] * 2,
        out_specs=ON_HBM,
    )(tokens_in, grad_out)
    signal = lax.all_to_all(packed, "ctx", split_axis=0, concat_axis=0, tiled=True)
    forward = spectrum_call(
        length, decay_rate.reshape(1, -1), w_in.reshape(1, -1), b_in.reshape(1, -1), w_mid, w_out,
        matrix, twiddle,
    )
    sent = gradient_call(length, signal.reshape(length, 128), *forward, matrix, twiddle)
    received = lax.all_to_all(sent, "ctx", split_axis=0, concat_axis=0, tiled=True)
    half, joined = call(
        sums_kernel, [shape((32, 64 * devices + 128), BF16), shape((8, 128), F32)]
    )(received)
    other = lax.ppermute(half, "ctx", [(index, index ^ 1) for index in range(devices)])
    input_grad = call(tokens_kernel, shape(tokens_in.shape, BF16), flops=1 << 26)(received)
    grad_first, grad_bias, grad_mid, grad_last = call(
        functools.partial(weights_kernel, 1.0 / math.sqrt(length)),
        [shape((1, 64), F32), shape((1, 64), F32), shape((64, 64), F32), shape(w_out.shape, F32)],
    )(joined, half, other)
    return input_grad, grad_first.reshape(64), grad_bias.reshape(64), grad_mid, grad_last


HIGHEST = lax.Precision.HIGHEST
TWO_PI = 2.0 * math.pi


def phase_angle(product, period):
    return TWO_PI / period * (product % period).astype(jnp.float32)


def frequency_rows(devices):
    row_index = jnp.arange(2 * devices, dtype=jnp.int32)
    row_block = row_index // 2
    second = row_index % 2
    paired = jnp.where(row_block == 0, devices, 2 * devices - row_block)
    return jnp.where(second == 0, row_block, paired)


def source_rows(devices):
    row_index = jnp.arange(2 * devices, dtype=jnp.int32)
    return row_index // 2 + row_index % 2 * devices


def envelope(lag_values, decay_rate, length):
    double = 2.0 * decay_rate
    geometric = 1.0 + 2.0 * jnp.exp(-double) * jnp.expm1(-double * (length - 1)) / jnp.expm1(
        -double
    )
    distance = jnp.abs(lag_values).astype(jnp.float32)[..., None]
    live_mask = (lag_values != -length).astype(jnp.float32)[..., None]
    return live_mask * lax.rsqrt(geometric) * jnp.exp(-distance * decay_rate)


def position_mlp(scaled, w_first, w_bias, w_middle, w_last):
    hidden_one = jax.nn.silu(scaled[..., None] * w_first + w_bias)
    hidden_two = jax.nn.silu(jnp.dot(hidden_one, w_middle, precision=HIGHEST))
    return jnp.dot(hidden_two, w_last, precision=HIGHEST)


def rotate(real_a, imag_a, real_b, imag_b):
    return (real_a * real_b - imag_a * imag_b, real_a * imag_b + imag_a * real_b)


def first_section(signal, columns, freq_order, local_slab, padded):
    freq_count = freq_order.shape[0]
    angles = phase_angle(freq_order[:, None] * columns[None, :], freq_count)
    real_part = jnp.einsum("fp,prc->frc", jnp.cos(angles), signal, precision=HIGHEST)
    imag_part = jnp.einsum("fp,prc->frc", -jnp.sin(angles), signal, precision=HIGHEST)
    twiddle = phase_angle(freq_order[:, None] * local_slab[None, :], padded)[:, :, None]
    return rotate(real_part, imag_part, jnp.cos(twiddle), -jnp.sin(twiddle))


def along_rows(stacked, direction):
    row_count = stacked.shape[1]
    half_width = stacked.shape[2] // 2
    positions = jnp.arange(row_count, dtype=jnp.int32)
    angles = phase_angle(positions[:, None] * positions[None, :], row_count)
    with_cos = jnp.einsum("gm,imc->igc", jnp.cos(angles), stacked, precision=HIGHEST)
    with_sin = jnp.einsum("gm,imc->igc", direction * jnp.sin(angles), stacked, precision=HIGHEST)
    real_part = with_cos[..., :half_width] - with_sin[..., half_width:]
    imag_part = with_cos[..., half_width:] + with_sin[..., :half_width]
    return (real_part, imag_part)


def last_section(stacked, out_rows, freq_order, padded):
    freq_count = freq_order.shape[0]
    half_width = stacked.shape[2] // 2
    angles = phase_angle(out_rows[:, None] * freq_order[None, :], freq_count)
    cos_table = jnp.cos(angles) / padded
    sin_table = jnp.sin(angles) / padded
    real_in = stacked[..., :half_width]
    imag_in = stacked[..., half_width:]
    leading, trailing, factor = (real_in, imag_in, -1.0)
    return jnp.einsum("pf,frc->prc", cos_table, leading, precision=HIGHEST) + factor * jnp.einsum(
        "pf,frc->prc", sin_table, trailing, precision=HIGHEST
    )


def by_frequencies(tokens_in, grad_out, decay_rate, w_in, b_in, w_mid, w_out):
    devices = lax.axis_size("ctx")
    own_index = lax.axis_index("ctx")
    tok_rows = tokens_in.shape[0]
    slab_rows = tok_rows // devices
    length = tok_rows * devices
    padded = 2 * length
    freq_order = frequency_rows(devices)
    lag_rows = source_rows(devices)
    token_cols = jnp.arange(devices, dtype=jnp.int32)
    local_slab = own_index * slab_rows + jnp.arange(slab_rows, dtype=jnp.int32)
    pair_index = jnp.arange(2, dtype=jnp.int32)
    local_freq = jnp.where(
        pair_index == 0, own_index, jnp.where(own_index == 0, devices, 2 * devices - own_index)
    )
    circular = (own_index + pair_index * devices)[:, None] * tok_rows + jnp.arange(
        tok_rows, dtype=jnp.int32
    )[None, :]
    lag_values = jnp.where(circular < length, circular, circular - padded)
    scaled = lag_values.astype(jnp.float32) / length
    weights_env = envelope(lag_values, decay_rate, length)

    def position_net(w_first, w_bias, w_middle, w_last):
        return position_mlp(scaled, w_first, w_bias, w_middle, w_last)

    position, pull_back = jax.vjp(position_net, w_in, b_in, w_mid, w_out)
    kernel = (position * weights_env).astype(jnp.bfloat16)
    tokens_mid, grads_mid, kernel_mid = (
        lax.all_to_all(tokens_in[None], "ctx", split_axis=1, concat_axis=0, tiled=True),
        lax.all_to_all(grad_out[None], "ctx", split_axis=1, concat_axis=0, tiled=True),
        lax.all_to_all(kernel, "ctx", split_axis=1, concat_axis=0, tiled=True),
    )
    token_real, token_imag = first_section(
        tokens_mid.astype(jnp.float32), token_cols, freq_order, local_slab, padded
    )
    cotan_real, cotan_imag = first_section(
        grads_mid.astype(jnp.float32), token_cols, freq_order, local_slab, padded
    )
    kern_real, kern_imag = first_section(
        kernel_mid.astype(jnp.float32), lag_rows, freq_order, local_slab, padded
    )
    kernel_stack = jnp.concatenate([kern_real, kern_imag], axis=2)
    token_stack = jnp.concatenate([token_real, token_imag], axis=2)
    cotan_stack = jnp.concatenate([cotan_real, cotan_imag], axis=2)
    token_spec, cotan_spec, kernel_spec = (
        lax.all_to_all(token_stack, "ctx", split_axis=0, concat_axis=1, tiled=True),
        lax.all_to_all(cotan_stack, "ctx", split_axis=0, concat_axis=1, tiled=True),
        lax.all_to_all(kernel_stack, "ctx", split_axis=0, concat_axis=1, tiled=True),
    )
    spec_token_real, spec_token_imag = along_rows(token_spec, -1.0)
    spec_cotan_real, spec_cotan_imag = along_rows(cotan_spec, -1.0)
    spec_kern_real, spec_kern_imag = along_rows(kernel_spec, -1.0)
    input_real = spec_kern_real * spec_cotan_real + spec_kern_imag * spec_cotan_imag
    input_imag = spec_kern_real * spec_cotan_imag - spec_kern_imag * spec_cotan_real
    lagged_real = spec_cotan_real * spec_token_real + spec_cotan_imag * spec_token_imag
    lagged_imag = spec_cotan_imag * spec_token_real - spec_cotan_real * spec_token_imag
    positions = jnp.arange(tok_rows, dtype=jnp.int32)
    back_angle = phase_angle(local_freq[:, None] * positions[None, :], padded)[:, :, None]
    back_cos = jnp.cos(back_angle)
    back_sin = jnp.sin(back_angle)

    def inverse_rows(real_part, imag_part):
        stacked = jnp.concatenate([real_part, imag_part], axis=2)
        out_real, out_imag = along_rows(stacked, 1.0)
        turned_real, turned_imag = rotate(out_real, out_imag, back_cos, back_sin)
        return jnp.concatenate([turned_real, turned_imag], axis=2)

    spread_input, spread_lagged = (
        lax.all_to_all(
            inverse_rows(input_real, input_imag), "ctx", split_axis=1, concat_axis=0, tiled=True
        ),
        lax.all_to_all(
            inverse_rows(lagged_real, lagged_imag), "ctx", split_axis=1, concat_axis=0, tiled=True
        ),
    )
    input_rows = last_section(spread_input, token_cols, freq_order, padded)
    lagged_rows = last_section(spread_lagged, lag_rows, freq_order, padded)
    input_back, lag_back = (
        lax.all_to_all(input_rows, "ctx", split_axis=0, concat_axis=1, tiled=True),
        lax.all_to_all(lagged_rows, "ctx", split_axis=0, concat_axis=1, tiled=True),
    )
    input_grad = input_back[0]
    gradients = pull_back(lag_back * weights_env)
    summed = lax.psum((gradients[0], gradients[1], gradients[2], gradients[3]), "ctx")
    loss_scale = 1.0 / math.sqrt(length)
    return (
        input_grad.astype(jnp.bfloat16),
        summed[0] * loss_scale,
        summed[1] * loss_scale,
        summed[2] * loss_scale,
        summed[3] * loss_scale,
    )


def on_device(tokens_in, grad_out, decay_rate, w_in, b_in, w_mid, w_out):
    devices = lax.axis_size("ctx")
    fits = (
        tokens_in.shape == (128, 64 * devices)
        and devices % 2 == 0
        and devices * 128 % (128 * HALF) == 0
        and w_mid.shape == (64, 64)
    )
    form = by_channels if fits else by_frequencies
    return form(tokens_in, grad_out, decay_rate, w_in, b_in, w_mid, w_out)


def solution(mesh):
    in_specs = (P(("groups", "ctx"), None), P(("groups", "ctx"), None), P(), P(), P(), P(), P())
    out_specs = (
        P(("groups", "ctx"), None),
        P("groups"),
        P("groups"),
        P("groups", None),
        P("groups", None),
    )
    return jax.shard_map(
        on_device, mesh=mesh, in_specs=in_specs, out_specs=out_specs, check_vma=False
    )
```

```python
import functools
import math

import jax
import jax.numpy as jnp
import numpy as np
from jax import lax
from jax.experimental import pallas as pl
from jax.experimental.pallas import tpu as pltpu
from jax.sharding import PartitionSpec as P

RADIX = 16
HALF = RADIX // 2
CHUNK = 64
UNROLL_CHUNK = 4
UNROLL_BIN = 9
UNROLL_ROWS = 8
PACK_PARTS = 4
FIRST_LIMIT = 56
SECOND_LIMIT = 50
F32 = jnp.float32
BF16 = jnp.bfloat16


def split_pair(value):
    high = value.astype(BF16)
    return high, (value - high.astype(F32)).astype(BF16)


def dot(left, right):
    return jnp.dot(left, right, preferred_element_type=F32)


def pair_lanes(value):
    return jnp.concatenate(split_pair(value), axis=1)


def square(matrix):
    high, low = split_pair(matrix)
    return jnp.concatenate(
        [
            jnp.concatenate([high, low], axis=1),
            jnp.concatenate([high, jnp.zeros_like(low)], axis=1),
        ],
        axis=0,
    )


def dot_pair(rows, squared):
    product = dot(rows, squared)
    return product[:, 0:128] + product[:, 128:256]


def tall_three(value):
    high, low = split_pair(value)
    return jnp.concatenate([high, high, low], axis=0)


def dft_tables(padded):
    inner = padded // RADIX
    grid = np.outer(np.arange(inner), np.arange(inner)) % inner
    angles = 2.0 * np.pi * grid / inner
    matrix = np.concatenate([np.cos(angles), np.sin(angles)], axis=0)
    high = matrix.astype(jnp.bfloat16)
    low = (matrix - high.astype(np.float64)).astype(jnp.bfloat16)
    matrix = np.concatenate([high, low, high], axis=1)
    turn = 2.0 * np.pi * np.outer(np.arange(inner), np.arange(RADIX)) / padded
    twiddle = np.zeros((inner, 128), np.float32)
    twiddle[:, :RADIX] = np.cos(turn)
    twiddle[:, RADIX : 2 * RADIX] = np.sin(turn)
    return jnp.asarray(matrix), jnp.asarray(twiddle)


def cos_of(index):
    return math.cos(2.0 * math.pi * index / RADIX)


def sin_of(index):
    return math.sin(2.0 * math.pi * index / RADIX)


def spread(x):
    plus = [x[q] + x[q + 4] for q in range(4)]
    minus = [x[q] - x[q + 4] for q in range(4)]
    root = math.sqrt(0.5)
    out = [None] * 9
    even, odd = plus[0] + plus[2], plus[1] + plus[3]
    out[0] = (even + odd, None)
    out[8] = (even - odd, None)
    out[4] = (plus[0] - plus[2], plus[3] - plus[1])
    across, along = root * (minus[1] - minus[3]), root * (minus[1] + minus[3])
    out[2] = (minus[0] + across, -minus[2] - along)
    out[6] = (minus[0] - across, minus[2] - along)
    differ = {q: x[q] - x[8 - q] for q in (1, 2, 3)}
    same = {q: x[q] + x[8 - q] for q in (1, 2, 3)}
    for j in (1, 3):
        real_even = x[0] + cos_of(2 * j) * differ[2]
        real_odd = cos_of(j) * differ[1] + cos_of(3 * j) * differ[3]
        imag_even = sin_of(4 * j) * x[4] + sin_of(2 * j) * same[2]
        imag_odd = sin_of(j) * same[1] + sin_of(3 * j) * same[3]
        out[j] = (real_even + real_odd, -(imag_odd + imag_even))
        out[8 - j] = (real_even - real_odd, imag_even - imag_odd)
    return out


def gather_back(real, imag):
    even, odd = [None] * 8, [None] * 8
    total, differ = real[0] + real[8], real[0] - real[8]
    real_sum, real_dif = real[2] + real[6], real[2] - real[6]
    imag_sum, imag_dif = imag[2] + imag[6], imag[2] - imag[6]
    root = math.sqrt(0.5)
    even[0] = total + real_sum + real[4]
    even[4] = total - real_sum + real[4]
    even[2] = total - imag_dif - real[4]
    even[6] = total + imag_dif - real[4]
    first, second = root * (real_dif - imag_sum), root * (real_dif + imag_sum)
    even[1] = differ + first - imag[4]
    even[5] = differ - first - imag[4]
    even[3] = differ - second + imag[4]
    even[7] = differ + second + imag[4]
    one_sum, one_dif = real[1] + real[7], real[1] - real[7]
    three_sum, three_dif = real[3] + real[5], real[3] - real[5]
    ione_sum, ione_dif = imag[1] + imag[7], imag[1] - imag[7]
    ithree_sum, ithree_dif = imag[3] + imag[5], imag[3] - imag[5]
    odd[0] = one_sum + three_sum
    odd[4] = ithree_dif - ione_dif
    for q in (1, 2, 3):
        if q % 2 == 0:
            cosines = cos_of(q) * one_sum + cos_of(3 * q) * three_sum
            sines = sin_of(q) * ione_dif + sin_of(3 * q) * ithree_dif
        else:
            cosines = cos_of(q) * one_dif + cos_of(3 * q) * three_dif
            sines = sin_of(q) * ione_sum + sin_of(3 * q) * ithree_sum
        odd[q] = cosines - sines
        odd[8 - q] = -cosines - sines
    return even, odd


def residues_to_scratch(load, twiddle, stage, inner):
    def chunk(step, carry):
        start = pl.multiple_of(step * CHUNK, CHUNK)
        turn = twiddle[pl.ds(start, CHUNK), :]
        for j, (real, imag) in enumerate(spread([load(q * inner + start) for q in range(HALF)])):
            if j > 0:
                cosine, sine = turn[:, j : j + 1], turn[:, RADIX + j : RADIX + j + 1]
                if imag is None:
                    real, imag = real * cosine, -real * sine
                else:
                    real, imag = real * cosine + imag * sine, imag * cosine - real * sine
            else:
                imag = jnp.zeros_like(real)
            for part, value in enumerate((real, imag)):
                high, low = split_pair(value)
                lanes = slice(128 * part, 128 * part + 128)
                stage[j, pl.ds(start, CHUNK), lanes] = high
                stage[j, pl.ds(inner + start, CHUNK), lanes] = high
                stage[j, pl.ds(2 * inner + start, CHUNK), lanes] = low
        return carry

    lax.fori_loop(0, inner // CHUNK, chunk, 0, unroll=UNROLL_CHUNK)


def inner_dft(stacked, matrix, inner, direction):
    reals, imags = [], []
    for row in range(0, inner, 128):
        cosines = dot(matrix[row : row + 128, :], stacked)
        sines = dot(matrix[inner + row : inner + row + 128, :], stacked)
        cos_real, cos_imag = cosines[:, :128], cosines[:, 128:]
        sin_real, sin_imag = sines[:, :128], sines[:, 128:]
        reals.append(cos_real + sin_imag if direction > 0 else cos_real - sin_imag)
        imags.append(cos_imag - sin_real if direction > 0 else cos_imag + sin_real)
    return jnp.concatenate(reals, axis=0), jnp.concatenate(imags, axis=0)


def low_lanes(rows):
    return lax.broadcasted_iota(jnp.int32, (rows, 128), 1) < 64


def swap(value):
    return pltpu.roll(value, 64, 1)


def copies_of(sources, buffers, semaphores):
    return [
        pltpu.make_async_copy(source, buffer, semaphores.at[index])
        for index, (source, buffer) in enumerate(zip(sources, buffers))
    ]


def fetch(sources, buffers, semaphores):
    copies = copies_of(sources, buffers, semaphores)
    for copy in copies:
        copy.start()
    return copies


def pack_kernel(tokens_hbm, cotan_hbm, out_hbm, tokens, cotan, out, load_semaphores, store_semaphores):
    loads, stores = [], []
    rows_each = tokens.shape[0] // PACK_PARTS
    for part in range(PACK_PARTS):
        rows = pl.ds(part * rows_each, rows_each)
        loads.append(
            fetch(
                (tokens_hbm.at[rows, :], cotan_hbm.at[rows, :]),
                (tokens.at[rows, :], cotan.at[rows, :]),
                load_semaphores.at[part],
            )
        )
    for part in range(PACK_PARTS):
        rows = pl.ds(part * rows_each, rows_each)
        for copy in loads[part]:
            copy.wait()
        for block in range(out.shape[0]):
            lanes = slice(64 * block, 64 * block + 64)
            out[block, rows, :] = jnp.concatenate([tokens[rows, lanes], cotan[rows, lanes]], axis=1)
        store = pltpu.make_async_copy(
            out.at[:, rows, :], out_hbm.at[:, rows, :], store_semaphores.at[part]
        )
        store.start()
        stores.append(store)
    for store in stores:
        store.wait()


def diagonal(matrix):
    empty = jnp.zeros_like(matrix)
    return jnp.concatenate(
        [jnp.concatenate([matrix, empty], axis=1), jnp.concatenate([empty, matrix], axis=1)], axis=0
    )


def twice(row):
    return jnp.concatenate([row, row], axis=1)


def exp_minus_one(value):
    series = jnp.ones_like(value)
    for order in range(9, 1, -1):
        series = 1.0 + series * value * (1.0 / order)
    return jnp.where(jnp.abs(value) < 0.35, value * series, jnp.exp(value) - 1.0)


def kernel_spectrum_kernel(
    length, rates, w_first, w_bias, w_mid, w_last, matrix, twiddle, wide_hbm, narrow_hbm,
    spectrum, slope_two, slope_one, consts, one, two, mid_back, last_back, semaphores, taps, stage,
):
    inner = 2 * length // RADIX
    low_half = low_lanes(inner)
    own = lax.axis_index("ctx")
    lanes = pl.ds(pl.multiple_of(own // 2 * 128, 128), 128)
    odd = own % 2 == 1
    last = w_last[:, lanes]
    last = diagonal(jnp.where(odd, swap(last), last)[:, 0:64])
    rate = rates[:, lanes]
    rate = twice(jnp.where(odd, swap(rate), rate)[:, 0:64])
    double = 2.0 * rate
    ratio = exp_minus_one(-double * (length - 1)) / exp_minus_one(-double)
    geometric = 1.0 + 2.0 * jnp.exp(-double) * ratio
    scale = lax.rsqrt(geometric)
    mid = diagonal(w_mid[...])
    mid_back[...] = square(mid.T)
    last_back[...] = square(last.T)
    mid, last = square(mid), square(last)
    first, bias = twice(w_first[...]), twice(w_bias[...])
    consts[...] = jnp.concatenate([rate, scale, first, bias, jnp.zeros((4, 128), F32)], axis=0)

    def block(step, carry):
        start = pl.multiple_of(step * inner, inner)
        rows = pl.ds(start, inner)
        place = start + lax.broadcasted_iota(jnp.int32, (inner, 128), 0)
        lag = jnp.where(low_half, place, place - length)
        scaled = lag.astype(F32) / length
        pre_one = scaled * first + bias
        gate_one = 1.0 / (1.0 + jnp.exp(-pre_one))
        hidden_one = pre_one * gate_one
        slope_one[rows, :] = gate_one * (1.0 + pre_one * (1.0 - gate_one))
        pre_two = dot_pair(pair_lanes(hidden_one), mid)
        gate_two = 1.0 / (1.0 + jnp.exp(-pre_two))
        hidden_two = pre_two * gate_two
        slope_two[rows, :] = gate_two * (1.0 + pre_two * (1.0 - gate_two))
        position = dot_pair(pair_lanes(hidden_two), last)
        live = jnp.where(lag == -length, 0.0, 1.0)
        env = live * scale * jnp.exp(-jnp.abs(lag).astype(F32) * rate)
        taps[rows, :] = (position * env).astype(BF16).astype(F32)
        one[0:128, rows], one[128:256, rows] = split_pair(hidden_one.T)
        two[0:128, rows], two[128:256, rows] = split_pair(hidden_two.T)
        return carry

    lax.fori_loop(0, HALF, block, 0, unroll=UNROLL_ROWS)
    places = passed_places(length, wide_hbm, narrow_hbm)
    held = (slope_two, slope_one, consts, one, two, mid_back, last_back)
    copies = fetch(held, places[1:], semaphores)
    residues_to_scratch(lambda start: taps[pl.ds(start, CHUNK), :], twiddle, stage, inner)

    def transform(j, carry):
        real, imag = inner_dft(stage[j], matrix, inner, 1)
        sign = 1.0 - 2.0 * lax.rem(jnp.asarray(j, jnp.int32), 2).astype(F32)
        spectrum[pl.ds((2 * j + 0) * inner, inner), :] = real + sign * swap(real)
        spectrum[pl.ds((2 * j + 1) * inner, inner), :] = imag + sign * swap(imag)
        return carry

    lax.fori_loop(0, HALF + 1, transform, 0, unroll=UNROLL_BIN)
    last_copy = pltpu.make_async_copy(spectrum, places[0], semaphores.at[len(copies)])
    last_copy.start()
    for copy in copies + [last_copy]:
        copy.wait()


def gradient_kernel(
    length, signal, wide_hbm, narrow_hbm, matrix, twiddle, out,
    spectrum, slope_two, slope_one, consts, one, two, mid_back, last_back, semaphores, stage, back_ref,
    slopes, pre, decay,
):
    padded = 2 * length
    inner = padded // RADIX
    low_half = low_lanes(inner)
    held = (spectrum, slope_two, slope_one, consts, one, two, mid_back, last_back)
    copies = copies_of(passed_places(length, wide_hbm, narrow_hbm), held, semaphores)
    first_needed, needed_later = (copies[0], copies[3]), copies[1:3] + copies[4:]
    for copy in first_needed:
        copy.start()
    residues_to_scratch(
        lambda start: signal[pl.ds(start, CHUNK), :].astype(F32), twiddle, stage, inner
    )
    for copy in needed_later:
        copy.start()

    def analyse(j, carry):
        real, imag = inner_dft(stage[j], matrix, inner, 1)
        back_ref[j, :, 0:128] = real
        back_ref[j, :, 128:256] = imag
        return carry

    lax.fori_loop(0, HALF + 1, analyse, 0, unroll=UNROLL_BIN)
    for copy in first_needed:
        copy.wait()

    def transform(j, carry):
        real, imag = back_ref[j, :, 0:128], back_ref[j, :, 128:256]
        real_swap, imag_swap = swap(real), swap(imag)
        cotan_real = jnp.where(low_half, real_swap, real)
        cotan_imag = jnp.where(low_half, imag_swap, imag)
        other_real = jnp.where(low_half, spectrum[pl.ds((2 * j + 0) * inner, inner), :], real_swap)
        other_imag = jnp.where(low_half, spectrum[pl.ds((2 * j + 1) * inner, inner), :], imag_swap)
        product = jnp.concatenate(
            [
                cotan_real * other_real + cotan_imag * other_imag,
                cotan_imag * other_real - cotan_real * other_imag,
            ],
            axis=1,
        )
        real, imag = inner_dft(tall_three(product), matrix, inner, -1)
        back_ref[j, :, 0:128] = real
        back_ref[j, :, 128:256] = imag
        return carry

    lax.fori_loop(0, HALF + 1, transform, 0, unroll=UNROLL_BIN)
    rate, scale, first, bias = (consts[index : index + 1, :] for index in range(4))
    place = lax.broadcasted_iota(jnp.int32, (inner, 128), 0)
    near = jnp.where(low_half, place, inner - 1 - place).astype(F32)
    decay[...] = jnp.exp(-near * rate)
    low_row = low_lanes(1)

    def unspread(step, carry):
        start = pl.multiple_of(step * CHUNK, CHUNK)
        rows = pl.ds(start, CHUNK)
        turn = twiddle[rows, :]
        real_list, imag_list = [], []
        for j in range(HALF + 1):
            weight = (1.0 if j in (0, HALF) else 2.0) / padded
            real, imag = back_ref[j, rows, 0:128], back_ref[j, rows, 128:256]
            if j == 0:
                real_list.append(real * weight)
                imag_list.append(None)
                continue
            cosine = turn[:, j : j + 1] * weight
            sine = turn[:, RADIX + j : RADIX + j + 1] * weight
            real_list.append(real * cosine - imag * sine)
            imag_list.append(real * sine + imag * cosine)
        even, odd = gather_back(real_list, imag_list)
        for q in range(HALF):
            joined, apart = even[q] + odd[q], even[q] - odd[q]
            back_ref[q, rows, 0:128] = joined
            at = pl.ds(q * inner + start, CHUNK)
            lag_grad = jnp.where(low_lanes(CHUNK), swap(joined), apart)
            far = jnp.where(low_row, q * inner, length - q * inner - inner + 1).astype(F32)
            weighted = lag_grad * (scale * jnp.exp(-far * rate)) * decay[rows, :]
            if q == 0:
                row = start + lax.broadcasted_iota(jnp.int32, (CHUNK, 128), 0)
                weighted = jnp.where((row == 0) & ~low_lanes(CHUNK), 0.0, weighted)
            slopes[at, :] = pair_lanes(weighted)
        return carry

    lax.fori_loop(0, inner // CHUNK, unspread, 0, unroll=UNROLL_CHUNK)
    for copy in needed_later:
        copy.wait()
    local_rows = 128
    half_rows = local_rows // 2

    def block(q, carry):
        start = pl.multiple_of(q * inner, inner)
        rows = pl.ds(start, inner)
        for part in range(inner // local_rows):
            base = part * local_rows
            upper = back_ref[q, base : base + half_rows, 0:128]
            lower = back_ref[q, base + half_rows : base + local_rows, 0:128]
            out[q * (inner // local_rows) + part, 0:half_rows, :] = jnp.where(
                low_half[:half_rows], upper, swap(lower)
            ).astype(BF16)
        return carry

    pre[...] = pair_lanes(dot_pair(slopes[...], last_back[...]) * slope_two[...])
    lax.fori_loop(0, HALF, block, 0, unroll=UNROLL_ROWS)
    last_product = dot(two[...], slopes[...])

    def first_layer(q, carry):
        first_sum, bias_sum = carry
        start = pl.multiple_of(q * inner, inner)
        rows = pl.ds(start, inner)
        base = jnp.where(low_row, start, start - length)
        scaled = (place + base).astype(F32) * (1.0 / length)
        pre_one = dot_pair(pre[rows, :], mid_back[...]) * slope_one[rows, :]
        first_sum = first_sum + jnp.sum((pre_one * scaled).reshape(inner // 8, 8, 128), axis=0)
        bias_sum = bias_sum + jnp.sum(pre_one.reshape(inner // 8, 8, 128), axis=0)
        return first_sum, bias_sum

    none = jnp.zeros((8, 128), F32)
    first_sum, bias_sum = lax.fori_loop(0, HALF, first_layer, (none, none), unroll=UNROLL_ROWS)
    last_sum, mid_sum = (
        product[0:128, 0:128] + (product[0:128, 128:256] + product[128:256, 0:128])
        for product in (last_product, dot(one[...], pre[...]))
    )
    low_32 = low_lanes(32)
    grad_last = last_sum[0:64] + swap(last_sum[64:128])
    last_rows = jnp.where(low_32, grad_last[0:32], swap(grad_last[32:64]))
    grad_mid = mid_sum[0:64] + swap(mid_sum[64:128])
    mid_rows = jnp.where(low_32, grad_mid[0:32], swap(grad_mid[32:64]))
    first = jnp.sum(first_sum, axis=0, keepdims=True)
    bias = jnp.sum(bias_sum, axis=0, keepdims=True)
    first = first + swap(first)
    bias = bias + swap(bias)
    joined = jnp.where(low_lanes(1), first, bias)
    joined_high = joined.astype(BF16).astype(F32)
    row_index = lax.broadcasted_iota(jnp.int32, (8, 128), 0)
    joined_rows = jnp.where(
        row_index == 0, joined_high, jnp.where(row_index == 1, joined - joined_high, 0.0)
    )
    for device in range(out.shape[0]):
        half = slice(16 * (device % 2), 16 * (device % 2) + 16)
        tail = [last_rows[half], mid_rows[half], joined_rows]
        out[device, half_rows:, :] = jnp.concatenate(tail, axis=0).astype(BF16)


def sums_kernel(received, half, joined_out):
    half_rows = received.shape[1] - 40
    mid = jnp.zeros((16, 128), F32)
    joined = jnp.zeros((8, 128), F32)
    for source in range(received.shape[0]):
        lanes = slice(64 * source, 64 * source + 64)
        last = received[source, half_rows : half_rows + 16, :]
        half[0:16, lanes] = last[:, 0:64]
        half[16:32, lanes] = last[:, 64:128]
        mid = mid + received[source, half_rows + 16 : half_rows + 32, :].astype(F32)
        joined = joined + received[source, half_rows + 32 : half_rows + 40, :].astype(F32)
    mid = jnp.concatenate([mid, swap(mid)], axis=0)
    high = mid.astype(BF16).astype(F32)
    columns = 64 * received.shape[0]
    rest = swap(mid - high)
    half[:, columns : columns + 128] = jnp.where(low_lanes(32), high, rest).astype(BF16)
    joined_out[...] = joined


def tokens_kernel(received, grad_tokens):
    half_rows = grad_tokens.shape[0] // 2
    for source in range(received.shape[0]):
        lanes = slice(64 * source, 64 * source + 64)
        tile = received[source, 0:half_rows, :]
        grad_tokens[0:half_rows, lanes] = tile[:, 0:64]
        grad_tokens[half_rows:, lanes] = tile[:, 64:128]


def weights_kernel(loss_scale, joined, mine, other, grad_first, grad_bias, grad_mid, grad_last):
    odd = lax.rem(lax.axis_index("ctx"), 2)
    columns = grad_last.shape[1]
    for source, parity in ((mine, odd), (other, 1 - odd)):
        last = source[:, 0:columns].astype(F32) * loss_scale
        grad_last[pl.ds(pl.multiple_of(16 * parity, 16), 16), :] = last[0:16]
        grad_last[pl.ds(pl.multiple_of(32 + 16 * parity, 16), 16), :] = last[16:32]
        mid = source[:, columns : columns + 128].astype(F32) * loss_scale
        mid = (mid + swap(mid))[:, 0:64]
        grad_mid[pl.ds(pl.multiple_of(16 * parity, 16), 16), :] = mid[0:16]
        grad_mid[pl.ds(pl.multiple_of(32 + 16 * parity, 16), 16), :] = mid[16:32]
    first = (joined[0:1] + joined[1:2]) * loss_scale
    grad_first[...] = first[:, 0:64]
    grad_bias[...] = first[:, 64:128]


def call(kernel, out_shape, scratch=(), flops=0, limit=24, **specs):
    return pl.pallas_call(
        kernel,
        out_shape=out_shape,
        **specs,
        scratch_shapes=list(scratch),
        compiler_params=pltpu.CompilerParams(vmem_limit_bytes=limit << 20),
        cost_estimate=pl.CostEstimate(flops=flops, bytes_accessed=1 << 20, transcendentals=0),
    )


def shape(dims, dtype):
    return jax.ShapeDtypeStruct(dims, dtype)


ON_HBM = pl.BlockSpec(memory_space=pltpu.HBM)
ON_VMEM = pl.BlockSpec(memory_space=pltpu.VMEM)


def passed_places(length, wide, narrow):
    bins = 2 * (HALF + 1) * (2 * length // RADIX)
    parts = [wide.at[pl.ds(0, bins), :]]
    parts += [wide.at[pl.ds(bins + index * length, length), :] for index in range(2)]
    parts += [wide.at[pl.ds(bins + 2 * length, 8), :]]
    parts += [narrow.at[pl.ds(256 * index, 256), :] for index in range(2)]
    return parts + [narrow.at[pl.ds(512, 256), pl.ds(256 * index, 256)] for index in range(2)]


def passed_shapes(length):
    bins = 2 * (HALF + 1) * (2 * length // RADIX)
    return [shape((bins + 2 * length + 8, 128), F32), shape((512 + 256, length), BF16)]


def held_arrays(length):
    bins = 2 * (HALF + 1) * (2 * length // RADIX)
    held = [pltpu.VMEM((rows, 128), F32) for rows in (bins, length, length, 8)]
    held += [pltpu.VMEM((256, length), BF16)] * 2 + [pltpu.VMEM((256, 256), BF16)] * 2
    return held + [pltpu.SemaphoreType.DMA((len(held),))]


def spectrum_call(length, *operands):
    inner = 2 * length // RADIX
    return call(
        functools.partial(kernel_spectrum_kernel, length),
        passed_shapes(length),
        scratch=held_arrays(length)
        + [pltpu.VMEM((length, 128), F32), pltpu.VMEM((HALF + 1, 3 * inner, 256), BF16)],
        flops=4 << 30,
        limit=FIRST_LIMIT,
        out_specs=[ON_HBM] * 2,
    )(*operands)


def gradient_call(length, *operands):
    inner = 2 * length // RADIX
    local_rows = 128
    return call(
        functools.partial(gradient_kernel, length),
        shape((length // local_rows, local_rows // 2 + 40, 128), BF16),
        scratch=held_arrays(length)
        + [
            pltpu.VMEM((HALF + 1, 3 * inner, 256), BF16),
            pltpu.VMEM((HALF + 1, inner, 256), F32),
        ]
        + [pltpu.VMEM((length, 256), BF16)] * 2
        + [pltpu.VMEM((inner, 128), F32)],
        flops=8 << 30,
        limit=SECOND_LIMIT,
        in_specs=[ON_VMEM] + [ON_HBM] * 2 + [ON_VMEM] * 2,
    )(*operands)


def by_channels(tokens_in, grad_out, decay_rate, w_in, b_in, w_mid, w_out):
    devices = lax.axis_size("ctx")
    local_rows = tokens_in.shape[0]
    length = local_rows * devices
    matrix, twiddle = dft_tables(2 * length)
    packed = call(
        pack_kernel,
        shape((devices, local_rows, 128), BF16),
        scratch=[pltpu.VMEM(tokens_in.shape, BF16)] * 2
        + [
            pltpu.VMEM((devices, local_rows, 128), BF16),
            pltpu.SemaphoreType.DMA((PACK_PARTS, 2)),
            pltpu.SemaphoreType.DMA((PACK_PARTS,)),
        ],
        limit=58,
        in_specs=[ON_HBM] * 2,
        out_specs=ON_HBM,
    )(tokens_in, grad_out)
    signal = lax.all_to_all(packed, "ctx", split_axis=0, concat_axis=0, tiled=True)
    forward = spectrum_call(
        length, decay_rate.reshape(1, -1), w_in.reshape(1, -1), b_in.reshape(1, -1), w_mid, w_out,
        matrix, twiddle,
    )
    sent = gradient_call(length, signal.reshape(length, 128), *forward, matrix, twiddle)
    received = lax.all_to_all(sent, "ctx", split_axis=0, concat_axis=0, tiled=True)
    half, joined = call(
        sums_kernel, [shape((32, 64 * devices + 128), BF16), shape((8, 128), F32)]
    )(received)
    other = lax.ppermute(half, "ctx", [(index, index ^ 1) for index in range(devices)])
    input_grad = call(tokens_kernel, shape(tokens_in.shape, BF16), flops=1 << 26)(received)
    grad_first, grad_bias, grad_mid, grad_last = call(
        functools.partial(weights_kernel, 1.0 / math.sqrt(length)),
        [shape((1, 64), F32), shape((1, 64), F32), shape((64, 64), F32), shape(w_out.shape, F32)],
    )(joined, half, other)
    return input_grad, grad_first.reshape(64), grad_bias.reshape(64), grad_mid, grad_last


HIGHEST = lax.Precision.HIGHEST
TWO_PI = 2.0 * math.pi


def phase_angle(product, period):
    return TWO_PI / period * (product % period).astype(jnp.float32)


def frequency_rows(devices):
    row_index = jnp.arange(2 * devices, dtype=jnp.int32)
    row_block = row_index // 2
    second = row_index % 2
    paired = jnp.where(row_block == 0, devices, 2 * devices - row_block)
    return jnp.where(second == 0, row_block, paired)


def source_rows(devices):
    row_index = jnp.arange(2 * devices, dtype=jnp.int32)
    return row_index // 2 + row_index % 2 * devices


def envelope(lag_values, decay_rate, length):
    double = 2.0 * decay_rate
    geometric = 1.0 + 2.0 * jnp.exp(-double) * jnp.expm1(-double * (length - 1)) / jnp.expm1(
        -double
    )
    distance = jnp.abs(lag_values).astype(jnp.float32)[..., None]
    live_mask = (lag_values != -length).astype(jnp.float32)[..., None]
    return live_mask * lax.rsqrt(geometric) * jnp.exp(-distance * decay_rate)


def position_mlp(scaled, w_first, w_bias, w_middle, w_last):
    hidden_one = jax.nn.silu(scaled[..., None] * w_first + w_bias)
    hidden_two = jax.nn.silu(jnp.dot(hidden_one, w_middle, precision=HIGHEST))
    return jnp.dot(hidden_two, w_last, precision=HIGHEST)


def rotate(real_a, imag_a, real_b, imag_b):
    return (real_a * real_b - imag_a * imag_b, real_a * imag_b + imag_a * real_b)


def first_section(signal, columns, freq_order, local_slab, padded):
    freq_count = freq_order.shape[0]
    angles = phase_angle(freq_order[:, None] * columns[None, :], freq_count)
    real_part = jnp.einsum("fp,prc->frc", jnp.cos(angles), signal, precision=HIGHEST)
    imag_part = jnp.einsum("fp,prc->frc", -jnp.sin(angles), signal, precision=HIGHEST)
    twiddle = phase_angle(freq_order[:, None] * local_slab[None, :], padded)[:, :, None]
    return rotate(real_part, imag_part, jnp.cos(twiddle), -jnp.sin(twiddle))


def along_rows(stacked, direction):
    row_count = stacked.shape[1]
    half_width = stacked.shape[2] // 2
    positions = jnp.arange(row_count, dtype=jnp.int32)
    angles = phase_angle(positions[:, None] * positions[None, :], row_count)
    with_cos = jnp.einsum("gm,imc->igc", jnp.cos(angles), stacked, precision=HIGHEST)
    with_sin = jnp.einsum("gm,imc->igc", direction * jnp.sin(angles), stacked, precision=HIGHEST)
    real_part = with_cos[..., :half_width] - with_sin[..., half_width:]
    imag_part = with_cos[..., half_width:] + with_sin[..., :half_width]
    return (real_part, imag_part)


def last_section(stacked, out_rows, freq_order, padded):
    freq_count = freq_order.shape[0]
    half_width = stacked.shape[2] // 2
    angles = phase_angle(out_rows[:, None] * freq_order[None, :], freq_count)
    cos_table = jnp.cos(angles) / padded
    sin_table = jnp.sin(angles) / padded
    real_in = stacked[..., :half_width]
    imag_in = stacked[..., half_width:]
    leading, trailing, factor = (real_in, imag_in, -1.0)
    return jnp.einsum("pf,frc->prc", cos_table, leading, precision=HIGHEST) + factor * jnp.einsum(
        "pf,frc->prc", sin_table, trailing, precision=HIGHEST
    )


def by_frequencies(tokens_in, grad_out, decay_rate, w_in, b_in, w_mid, w_out):
    devices = lax.axis_size("ctx")
    own_index = lax.axis_index("ctx")
    tok_rows = tokens_in.shape[0]
    slab_rows = tok_rows // devices
    length = tok_rows * devices
    padded = 2 * length
    freq_order = frequency_rows(devices)
    lag_rows = source_rows(devices)
    token_cols = jnp.arange(devices, dtype=jnp.int32)
    local_slab = own_index * slab_rows + jnp.arange(slab_rows, dtype=jnp.int32)
    pair_index = jnp.arange(2, dtype=jnp.int32)
    local_freq = jnp.where(
        pair_index == 0, own_index, jnp.where(own_index == 0, devices, 2 * devices - own_index)
    )
    circular = (own_index + pair_index * devices)[:, None] * tok_rows + jnp.arange(
        tok_rows, dtype=jnp.int32
    )[None, :]
    lag_values = jnp.where(circular < length, circular, circular - padded)
    scaled = lag_values.astype(jnp.float32) / length
    weights_env = envelope(lag_values, decay_rate, length)

    def position_net(w_first, w_bias, w_middle, w_last):
        return position_mlp(scaled, w_first, w_bias, w_middle, w_last)

    position, pull_back = jax.vjp(position_net, w_in, b_in, w_mid, w_out)
    kernel = (position * weights_env).astype(jnp.bfloat16)
    tokens_mid, grads_mid, kernel_mid = (
        lax.all_to_all(tokens_in[None], "ctx", split_axis=1, concat_axis=0, tiled=True),
        lax.all_to_all(grad_out[None], "ctx", split_axis=1, concat_axis=0, tiled=True),
        lax.all_to_all(kernel, "ctx", split_axis=1, concat_axis=0, tiled=True),
    )
    token_real, token_imag = first_section(
        tokens_mid.astype(jnp.float32), token_cols, freq_order, local_slab, padded
    )
    cotan_real, cotan_imag = first_section(
        grads_mid.astype(jnp.float32), token_cols, freq_order, local_slab, padded
    )
    kern_real, kern_imag = first_section(
        kernel_mid.astype(jnp.float32), lag_rows, freq_order, local_slab, padded
    )
    kernel_stack = jnp.concatenate([kern_real, kern_imag], axis=2)
    token_stack = jnp.concatenate([token_real, token_imag], axis=2)
    cotan_stack = jnp.concatenate([cotan_real, cotan_imag], axis=2)
    token_spec, cotan_spec, kernel_spec = (
        lax.all_to_all(token_stack, "ctx", split_axis=0, concat_axis=1, tiled=True),
        lax.all_to_all(cotan_stack, "ctx", split_axis=0, concat_axis=1, tiled=True),
        lax.all_to_all(kernel_stack, "ctx", split_axis=0, concat_axis=1, tiled=True),
    )
    spec_token_real, spec_token_imag = along_rows(token_spec, -1.0)
    spec_cotan_real, spec_cotan_imag = along_rows(cotan_spec, -1.0)
    spec_kern_real, spec_kern_imag = along_rows(kernel_spec, -1.0)
    input_real = spec_kern_real * spec_cotan_real + spec_kern_imag * spec_cotan_imag
    input_imag = spec_kern_real * spec_cotan_imag - spec_kern_imag * spec_cotan_real
    lagged_real = spec_cotan_real * spec_token_real + spec_cotan_imag * spec_token_imag
    lagged_imag = spec_cotan_imag * spec_token_real - spec_cotan_real * spec_token_imag
    positions = jnp.arange(tok_rows, dtype=jnp.int32)
    back_angle = phase_angle(local_freq[:, None] * positions[None, :], padded)[:, :, None]
    back_cos = jnp.cos(back_angle)
    back_sin = jnp.sin(back_angle)

    def inverse_rows(real_part, imag_part):
        stacked = jnp.concatenate([real_part, imag_part], axis=2)
        out_real, out_imag = along_rows(stacked, 1.0)
        turned_real, turned_imag = rotate(out_real, out_imag, back_cos, back_sin)
        return jnp.concatenate([turned_real, turned_imag], axis=2)

    spread_input, spread_lagged = (
        lax.all_to_all(
            inverse_rows(input_real, input_imag), "ctx", split_axis=1, concat_axis=0, tiled=True
        ),
        lax.all_to_all(
            inverse_rows(lagged_real, lagged_imag), "ctx", split_axis=1, concat_axis=0, tiled=True
        ),
    )
    input_rows = last_section(spread_input, token_cols, freq_order, padded)
    lagged_rows = last_section(spread_lagged, lag_rows, freq_order, padded)
    input_back, lag_back = (
        lax.all_to_all(input_rows, "ctx", split_axis=0, concat_axis=1, tiled=True),
        lax.all_to_all(lagged_rows, "ctx", split_axis=0, concat_axis=1, tiled=True),
    )
    input_grad = input_back[0]
    gradients = pull_back(lag_back * weights_env)
    summed = lax.psum((gradients[0], gradients[1], gradients[2], gradients[3]), "ctx")
    loss_scale = 1.0 / math.sqrt(length)
    return (
        input_grad.astype(jnp.bfloat16),
        summed[0] * loss_scale,
        summed[1] * loss_scale,
        summed[2] * loss_scale,
        summed[3] * loss_scale,
    )


def on_device(tokens_in, grad_out, decay_rate, w_in, b_in, w_mid, w_out):
    devices = lax.axis_size("ctx")
    fits = (
        tokens_in.shape == (128, 64 * devices)
        and devices % 2 == 0
        and devices * 128 % (128 * HALF) == 0
        and w_mid.shape == (64, 64)
    )
    form = by_channels if fits else by_frequencies
    return form(tokens_in, grad_out, decay_rate, w_in, b_in, w_mid, w_out)


def solution(mesh):
    in_specs = (P(("groups", "ctx"), None), P(("groups", "ctx"), None), P(), P(), P(), P(), P())
    out_specs = (
        P(("groups", "ctx"), None),
        P("groups"),
        P("groups"),
        P("groups", None),
        P("groups", None),
    )
    return jax.shard_map(
        on_device, mesh=mesh, in_specs=in_specs, out_specs=out_specs, check_vma=False
    )
```

```python
import functools
import math

import jax
import jax.numpy as jnp
import numpy as np
from jax import lax
from jax.experimental import pallas as pl
from jax.experimental.pallas import tpu as pltpu
from jax.sharding import PartitionSpec as P

RADIX = 16
HALF = RADIX // 2
CHUNK = 64
UNROLL_CHUNK = 4
UNROLL_BIN = 9
UNROLL_ROWS = 8
PACK_PARTS = 2
FIRST_LIMIT = 56
SECOND_LIMIT = 50
F32 = jnp.float32
BF16 = jnp.bfloat16


def split_pair(value):
    high = value.astype(BF16)
    return high, (value - high.astype(F32)).astype(BF16)


def dot(left, right):
    return jnp.dot(left, right, preferred_element_type=F32)


def pair_lanes(value):
    return jnp.concatenate(split_pair(value), axis=1)


def square(matrix):
    high, low = split_pair(matrix)
    return jnp.concatenate(
        [
            jnp.concatenate([high, low], axis=1),
            jnp.concatenate([high, jnp.zeros_like(low)], axis=1),
        ],
        axis=0,
    )


def dot_pair(rows, squared):
    product = dot(rows, squared)
    return product[:, 0:128] + product[:, 128:256]


def tall_three(value):
    high, low = split_pair(value)
    return jnp.concatenate([high, high, low], axis=0)


def dft_tables(padded):
    inner = padded // RADIX
    grid = np.outer(np.arange(inner), np.arange(inner)) % inner
    angles = 2.0 * np.pi * grid / inner
    matrix = np.concatenate([np.cos(angles), np.sin(angles)], axis=0)
    high = matrix.astype(jnp.bfloat16)
    low = (matrix - high.astype(np.float64)).astype(jnp.bfloat16)
    matrix = np.concatenate([high, low, high], axis=1)
    turn = 2.0 * np.pi * np.outer(np.arange(inner), np.arange(RADIX)) / padded
    twiddle = np.zeros((inner, 128), np.float32)
    twiddle[:, :RADIX] = np.cos(turn)
    twiddle[:, RADIX : 2 * RADIX] = np.sin(turn)
    return jnp.asarray(matrix), jnp.asarray(twiddle)


def cos_of(index):
    return math.cos(2.0 * math.pi * index / RADIX)


def sin_of(index):
    return math.sin(2.0 * math.pi * index / RADIX)


def spread(x):
    plus = [x[q] + x[q + 4] for q in range(4)]
    minus = [x[q] - x[q + 4] for q in range(4)]
    root = math.sqrt(0.5)
    out = [None] * 9
    even, odd = plus[0] + plus[2], plus[1] + plus[3]
    out[0] = (even + odd, None)
    out[8] = (even - odd, None)
    out[4] = (plus[0] - plus[2], plus[3] - plus[1])
    across, along = root * (minus[1] - minus[3]), root * (minus[1] + minus[3])
    out[2] = (minus[0] + across, -minus[2] - along)
    out[6] = (minus[0] - across, minus[2] - along)
    differ = {q: x[q] - x[8 - q] for q in (1, 2, 3)}
    same = {q: x[q] + x[8 - q] for q in (1, 2, 3)}
    for j in (1, 3):
        real_even = x[0] + cos_of(2 * j) * differ[2]
        real_odd = cos_of(j) * differ[1] + cos_of(3 * j) * differ[3]
        imag_even = sin_of(4 * j) * x[4] + sin_of(2 * j) * same[2]
        imag_odd = sin_of(j) * same[1] + sin_of(3 * j) * same[3]
        out[j] = (real_even + real_odd, -(imag_odd + imag_even))
        out[8 - j] = (real_even - real_odd, imag_even - imag_odd)
    return out


def gather_back(real, imag):
    even, odd = [None] * 8, [None] * 8
    total, differ = real[0] + real[8], real[0] - real[8]
    real_sum, real_dif = real[2] + real[6], real[2] - real[6]
    imag_sum, imag_dif = imag[2] + imag[6], imag[2] - imag[6]
    root = math.sqrt(0.5)
    even[0] = total + real_sum + real[4]
    even[4] = total - real_sum + real[4]
    even[2] = total - imag_dif - real[4]
    even[6] = total + imag_dif - real[4]
    first, second = root * (real_dif - imag_sum), root * (real_dif + imag_sum)
    even[1] = differ + first - imag[4]
    even[5] = differ - first - imag[4]
    even[3] = differ - second + imag[4]
    even[7] = differ + second + imag[4]
    one_sum, one_dif = real[1] + real[7], real[1] - real[7]
    three_sum, three_dif = real[3] + real[5], real[3] - real[5]
    ione_sum, ione_dif = imag[1] + imag[7], imag[1] - imag[7]
    ithree_sum, ithree_dif = imag[3] + imag[5], imag[3] - imag[5]
    odd[0] = one_sum + three_sum
    odd[4] = ithree_dif - ione_dif
    for q in (1, 2, 3):
        if q % 2 == 0:
            cosines = cos_of(q) * one_sum + cos_of(3 * q) * three_sum
            sines = sin_of(q) * ione_dif + sin_of(3 * q) * ithree_dif
        else:
            cosines = cos_of(q) * one_dif + cos_of(3 * q) * three_dif
            sines = sin_of(q) * ione_sum + sin_of(3 * q) * ithree_sum
        odd[q] = cosines - sines
        odd[8 - q] = -cosines - sines
    return even, odd


def residues_to_scratch(load, twiddle, stage, inner):
    def chunk(step, carry):
        start = pl.multiple_of(step * CHUNK, CHUNK)
        turn = twiddle[pl.ds(start, CHUNK), :]
        for j, (real, imag) in enumerate(spread([load(q * inner + start) for q in range(HALF)])):
            if j > 0:
                cosine, sine = turn[:, j : j + 1], turn[:, RADIX + j : RADIX + j + 1]
                if imag is None:
                    real, imag = real * cosine, -real * sine
                else:
                    real, imag = real * cosine + imag * sine, imag * cosine - real * sine
            else:
                imag = jnp.zeros_like(real)
            for part, value in enumerate((real, imag)):
                high, low = split_pair(value)
                lanes = slice(128 * part, 128 * part + 128)
                stage[j, pl.ds(start, CHUNK), lanes] = high
                stage[j, pl.ds(inner + start, CHUNK), lanes] = high
                stage[j, pl.ds(2 * inner + start, CHUNK), lanes] = low
        return carry

    lax.fori_loop(0, inner // CHUNK, chunk, 0, unroll=UNROLL_CHUNK)


def inner_dft(stacked, matrix, inner, direction):
    reals, imags = [], []
    for row in range(0, inner, 128):
        cosines = dot(matrix[row : row + 128, :], stacked)
        sines = dot(matrix[inner + row : inner + row + 128, :], stacked)
        cos_real, cos_imag = cosines[:, :128], cosines[:, 128:]
        sin_real, sin_imag = sines[:, :128], sines[:, 128:]
        reals.append(cos_real + sin_imag if direction > 0 else cos_real - sin_imag)
        imags.append(cos_imag - sin_real if direction > 0 else cos_imag + sin_real)
    return jnp.concatenate(reals, axis=0), jnp.concatenate(imags, axis=0)


def low_lanes(rows):
    return lax.broadcasted_iota(jnp.int32, (rows, 128), 1) < 64


def swap(value):
    return pltpu.roll(value, 64, 1)


def copies_of(sources, buffers, semaphores):
    return [
        pltpu.make_async_copy(source, buffer, semaphores.at[index])
        for index, (source, buffer) in enumerate(zip(sources, buffers))
    ]


def fetch(sources, buffers, semaphores):
    copies = copies_of(sources, buffers, semaphores)
    for copy in copies:
        copy.start()
    return copies


def pack_kernel(tokens_hbm, cotan_hbm, out_hbm, tokens, cotan, out, load_semaphores, store_semaphores):
    loads, stores = [], []
    rows_each = tokens.shape[0] // PACK_PARTS
    for part in range(PACK_PARTS):
        rows = pl.ds(part * rows_each, rows_each)
        loads.append(
            fetch(
                (tokens_hbm.at[rows, :], cotan_hbm.at[rows, :]),
                (tokens.at[rows, :], cotan.at[rows, :]),
                load_semaphores.at[part],
            )
        )
    for part in range(PACK_PARTS):
        rows = pl.ds(part * rows_each, rows_each)
        for copy in loads[part]:
            copy.wait()
        for block in range(out.shape[0]):
            lanes = slice(64 * block, 64 * block + 64)
            out[block, rows, :] = jnp.concatenate([tokens[rows, lanes], cotan[rows, lanes]], axis=1)
        store = pltpu.make_async_copy(
            out.at[:, rows, :], out_hbm.at[:, rows, :], store_semaphores.at[part]
        )
        store.start()
        stores.append(store)
    for store in stores:
        store.wait()


def diagonal(matrix):
    empty = jnp.zeros_like(matrix)
    return jnp.concatenate(
        [jnp.concatenate([matrix, empty], axis=1), jnp.concatenate([empty, matrix], axis=1)], axis=0
    )


def twice(row):
    return jnp.concatenate([row, row], axis=1)


def exp_minus_one(value):
    series = jnp.ones_like(value)
    for order in range(9, 1, -1):
        series = 1.0 + series * value * (1.0 / order)
    return jnp.where(jnp.abs(value) < 0.35, value * series, jnp.exp(value) - 1.0)


def kernel_spectrum_kernel(
    length, rates, w_first, w_bias, w_mid, w_last, matrix, twiddle, wide_hbm, narrow_hbm,
    spectrum, slope_two, slope_one, consts, one, two, mid_back, last_back, semaphores, taps, stage,
):
    inner = 2 * length // RADIX
    low_half = low_lanes(inner)
    own = lax.axis_index("ctx")
    lanes = pl.ds(pl.multiple_of(own // 2 * 128, 128), 128)
    odd = own % 2 == 1
    last = w_last[:, lanes]
    last = diagonal(jnp.where(odd, swap(last), last)[:, 0:64])
    rate = rates[:, lanes]
    rate = twice(jnp.where(odd, swap(rate), rate)[:, 0:64])
    double = 2.0 * rate
    ratio = exp_minus_one(-double * (length - 1)) / exp_minus_one(-double)
    geometric = 1.0 + 2.0 * jnp.exp(-double) * ratio
    scale = lax.rsqrt(geometric)
    mid = diagonal(w_mid[...])
    mid_back[...] = square(mid.T)
    last_back[...] = square(last.T)
    mid, last = square(mid), square(last)
    first, bias = twice(w_first[...]), twice(w_bias[...])
    consts[...] = jnp.concatenate([rate, scale, first, bias, jnp.zeros((4, 128), F32)], axis=0)

    def block(step, carry):
        start = pl.multiple_of(step * inner, inner)
        rows = pl.ds(start, inner)
        place = start + lax.broadcasted_iota(jnp.int32, (inner, 128), 0)
        lag = jnp.where(low_half, place, place - length)
        scaled = lag.astype(F32) / length
        pre_one = scaled * first + bias
        gate_one = 1.0 / (1.0 + jnp.exp(-pre_one))
        hidden_one = pre_one * gate_one
        slope_one[rows, :] = gate_one * (1.0 + pre_one * (1.0 - gate_one))
        pre_two = dot_pair(pair_lanes(hidden_one), mid)
        gate_two = 1.0 / (1.0 + jnp.exp(-pre_two))
        hidden_two = pre_two * gate_two
        slope_two[rows, :] = gate_two * (1.0 + pre_two * (1.0 - gate_two))
        position = dot_pair(pair_lanes(hidden_two), last)
        live = jnp.where(lag == -length, 0.0, 1.0)
        env = live * scale * jnp.exp(-jnp.abs(lag).astype(F32) * rate)
        taps[rows, :] = (position * env).astype(BF16).astype(F32)
        one[0:128, rows], one[128:256, rows] = split_pair(hidden_one.T)
        two[0:128, rows], two[128:256, rows] = split_pair(hidden_two.T)
        return carry

    lax.fori_loop(0, HALF, block, 0, unroll=UNROLL_ROWS)
    places = passed_places(length, wide_hbm, narrow_hbm)
    held = (slope_two, slope_one, consts, one, two, mid_back, last_back)
    copies = fetch(held, places[1:], semaphores)
    residues_to_scratch(lambda start: taps[pl.ds(start, CHUNK), :], twiddle, stage, inner)

    def transform(j, carry):
        real, imag = inner_dft(stage[j], matrix, inner, 1)
        sign = 1.0 - 2.0 * lax.rem(jnp.asarray(j, jnp.int32), 2).astype(F32)
        spectrum[pl.ds((2 * j + 0) * inner, inner), :] = real + sign * swap(real)
        spectrum[pl.ds((2 * j + 1) * inner, inner), :] = imag + sign * swap(imag)
        return carry

    lax.fori_loop(0, HALF + 1, transform, 0, unroll=UNROLL_BIN)
    last_copy = pltpu.make_async_copy(spectrum, places[0], semaphores.at[len(copies)])
    last_copy.start()
    for copy in copies + [last_copy]:
        copy.wait()


def gradient_kernel(
    length, signal, wide_hbm, narrow_hbm, matrix, twiddle, out,
    spectrum, slope_two, slope_one, consts, one, two, mid_back, last_back, semaphores, stage, back_ref,
    slopes, pre, decay,
):
    padded = 2 * length
    inner = padded // RADIX
    low_half = low_lanes(inner)
    held = (spectrum, slope_two, slope_one, consts, one, two, mid_back, last_back)
    copies = copies_of(passed_places(length, wide_hbm, narrow_hbm), held, semaphores)
    first_needed, needed_later = (copies[0], copies[3]), copies[1:3] + copies[4:]
    for copy in first_needed:
        copy.start()
    residues_to_scratch(
        lambda start: signal[pl.ds(start, CHUNK), :].astype(F32), twiddle, stage, inner
    )
    for copy in needed_later:
        copy.start()

    def analyse(j, carry):
        real, imag = inner_dft(stage[j], matrix, inner, 1)
        back_ref[j, :, 0:128] = real
        back_ref[j, :, 128:256] = imag
        return carry

    lax.fori_loop(0, HALF + 1, analyse, 0, unroll=UNROLL_BIN)
    for copy in first_needed:
        copy.wait()

    def transform(j, carry):
        real, imag = back_ref[j, :, 0:128], back_ref[j, :, 128:256]
        real_swap, imag_swap = swap(real), swap(imag)
        cotan_real = jnp.where(low_half, real_swap, real)
        cotan_imag = jnp.where(low_half, imag_swap, imag)
        other_real = jnp.where(low_half, spectrum[pl.ds((2 * j + 0) * inner, inner), :], real_swap)
        other_imag = jnp.where(low_half, spectrum[pl.ds((2 * j + 1) * inner, inner), :], imag_swap)
        product = jnp.concatenate(
            [
                cotan_real * other_real + cotan_imag * other_imag,
                cotan_imag * other_real - cotan_real * other_imag,
            ],
            axis=1,
        )
        real, imag = inner_dft(tall_three(product), matrix, inner, -1)
        back_ref[j, :, 0:128] = real
        back_ref[j, :, 128:256] = imag
        return carry

    lax.fori_loop(0, HALF + 1, transform, 0, unroll=UNROLL_BIN)
    rate, scale, first, bias = (consts[index : index + 1, :] for index in range(4))
    place = lax.broadcasted_iota(jnp.int32, (inner, 128), 0)
    near = jnp.where(low_half, place, inner - 1 - place).astype(F32)
    decay[...] = jnp.exp(-near * rate)
    low_row = low_lanes(1)

    def unspread(step, carry):
        start = pl.multiple_of(step * CHUNK, CHUNK)
        rows = pl.ds(start, CHUNK)
        turn = twiddle[rows, :]
        real_list, imag_list = [], []
        for j in range(HALF + 1):
            weight = (1.0 if j in (0, HALF) else 2.0) / padded
            real, imag = back_ref[j, rows, 0:128], back_ref[j, rows, 128:256]
            if j == 0:
                real_list.append(real * weight)
                imag_list.append(None)
                continue
            cosine = turn[:, j : j + 1] * weight
            sine = turn[:, RADIX + j : RADIX + j + 1] * weight
            real_list.append(real * cosine - imag * sine)
            imag_list.append(real * sine + imag * cosine)
        even, odd = gather_back(real_list, imag_list)
        for q in range(HALF):
            joined, apart = even[q] + odd[q], even[q] - odd[q]
            back_ref[q, rows, 0:128] = joined
            at = pl.ds(q * inner + start, CHUNK)
            lag_grad = jnp.where(low_lanes(CHUNK), swap(joined), apart)
            far = jnp.where(low_row, q * inner, length - q * inner - inner + 1).astype(F32)
            weighted = lag_grad * (scale * jnp.exp(-far * rate)) * decay[rows, :]
            if q == 0:
                row = start + lax.broadcasted_iota(jnp.int32, (CHUNK, 128), 0)
                weighted = jnp.where((row == 0) & ~low_lanes(CHUNK), 0.0, weighted)
            slopes[at, :] = pair_lanes(weighted)
        return carry

    lax.fori_loop(0, inner // CHUNK, unspread, 0, unroll=UNROLL_CHUNK)
    for copy in needed_later:
        copy.wait()
    local_rows = 128
    half_rows = local_rows // 2

    def block(q, carry):
        start = pl.multiple_of(q * inner, inner)
        rows = pl.ds(start, inner)
        for part in range(inner // local_rows):
            base = part * local_rows
            upper = back_ref[q, base : base + half_rows, 0:128]
            lower = back_ref[q, base + half_rows : base + local_rows, 0:128]
            out[q * (inner // local_rows) + part, 0:half_rows, :] = jnp.where(
                low_half[:half_rows], upper, swap(lower)
            ).astype(BF16)
        return carry

    pre[...] = pair_lanes(dot_pair(slopes[...], last_back[...]) * slope_two[...])
    lax.fori_loop(0, HALF, block, 0, unroll=UNROLL_ROWS)
    last_product = dot(two[...], slopes[...])

    def first_layer(q, carry):
        first_sum, bias_sum = carry
        start = pl.multiple_of(q * inner, inner)
        rows = pl.ds(start, inner)
        base = jnp.where(low_row, start, start - length)
        scaled = (place + base).astype(F32) * (1.0 / length)
        pre_one = dot_pair(pre[rows, :], mid_back[...]) * slope_one[rows, :]
        first_sum = first_sum + jnp.sum((pre_one * scaled).reshape(inner // 8, 8, 128), axis=0)
        bias_sum = bias_sum + jnp.sum(pre_one.reshape(inner // 8, 8, 128), axis=0)
        return first_sum, bias_sum

    none = jnp.zeros((8, 128), F32)
    first_sum, bias_sum = lax.fori_loop(0, HALF, first_layer, (none, none), unroll=UNROLL_ROWS)
    last_sum, mid_sum = (
        product[0:128, 0:128] + (product[0:128, 128:256] + product[128:256, 0:128])
        for product in (last_product, dot(one[...], pre[...]))
    )
    low_32 = low_lanes(32)
    grad_last = last_sum[0:64] + swap(last_sum[64:128])
    last_rows = jnp.where(low_32, grad_last[0:32], swap(grad_last[32:64]))
    grad_mid = mid_sum[0:64] + swap(mid_sum[64:128])
    mid_rows = jnp.where(low_32, grad_mid[0:32], swap(grad_mid[32:64]))
    first = jnp.sum(first_sum, axis=0, keepdims=True)
    bias = jnp.sum(bias_sum, axis=0, keepdims=True)
    first = first + swap(first)
    bias = bias + swap(bias)
    joined = jnp.where(low_lanes(1), first, bias)
    joined_high = joined.astype(BF16).astype(F32)
    row_index = lax.broadcasted_iota(jnp.int32, (8, 128), 0)
    joined_rows = jnp.where(
        row_index == 0, joined_high, jnp.where(row_index == 1, joined - joined_high, 0.0)
    )
    for device in range(out.shape[0]):
        half = slice(16 * (device % 2), 16 * (device % 2) + 16)
        tail = [last_rows[half], mid_rows[half], joined_rows]
        out[device, half_rows:, :] = jnp.concatenate(tail, axis=0).astype(BF16)


def sums_kernel(received, half, joined_out):
    half_rows = received.shape[1] - 40
    mid = jnp.zeros((16, 128), F32)
    joined = jnp.zeros((8, 128), F32)
    for source in range(received.shape[0]):
        lanes = slice(64 * source, 64 * source + 64)
        last = received[source, half_rows : half_rows + 16, :]
        half[0:16, lanes] = last[:, 0:64]
        half[16:32, lanes] = last[:, 64:128]
        mid = mid + received[source, half_rows + 16 : half_rows + 32, :].astype(F32)
        joined = joined + received[source, half_rows + 32 : half_rows + 40, :].astype(F32)
    mid = jnp.concatenate([mid, swap(mid)], axis=0)
    high = mid.astype(BF16).astype(F32)
    columns = 64 * received.shape[0]
    rest = swap(mid - high)
    half[:, columns : columns + 128] = jnp.where(low_lanes(32), high, rest).astype(BF16)
    joined_out[...] = joined


def tokens_kernel(received, grad_tokens):
    half_rows = grad_tokens.shape[0] // 2
    for source in range(received.shape[0]):
        lanes = slice(64 * source, 64 * source + 64)
        tile = received[source, 0:half_rows, :]
        grad_tokens[0:half_rows, lanes] = tile[:, 0:64]
        grad_tokens[half_rows:, lanes] = tile[:, 64:128]


def weights_kernel(loss_scale, joined, mine, other, grad_first, grad_bias, grad_mid, grad_last):
    odd = lax.rem(lax.axis_index("ctx"), 2)
    columns = grad_last.shape[1]
    for source, parity in ((mine, odd), (other, 1 - odd)):
        last = source[:, 0:columns].astype(F32) * loss_scale
        grad_last[pl.ds(pl.multiple_of(16 * parity, 16), 16), :] = last[0:16]
        grad_last[pl.ds(pl.multiple_of(32 + 16 * parity, 16), 16), :] = last[16:32]
        mid = source[:, columns : columns + 128].astype(F32) * loss_scale
        mid = (mid + swap(mid))[:, 0:64]
        grad_mid[pl.ds(pl.multiple_of(16 * parity, 16), 16), :] = mid[0:16]
        grad_mid[pl.ds(pl.multiple_of(32 + 16 * parity, 16), 16), :] = mid[16:32]
    first = (joined[0:1] + joined[1:2]) * loss_scale
    grad_first[...] = first[:, 0:64]
    grad_bias[...] = first[:, 64:128]


def call(kernel, out_shape, scratch=(), flops=0, limit=24, **specs):
    return pl.pallas_call(
        kernel,
        out_shape=out_shape,
        **specs,
        scratch_shapes=list(scratch),
        compiler_params=pltpu.CompilerParams(vmem_limit_bytes=limit << 20),
        cost_estimate=pl.CostEstimate(flops=flops, bytes_accessed=1 << 20, transcendentals=0),
    )


def shape(dims, dtype):
    return jax.ShapeDtypeStruct(dims, dtype)


ON_HBM = pl.BlockSpec(memory_space=pltpu.HBM)
ON_VMEM = pl.BlockSpec(memory_space=pltpu.VMEM)


def passed_places(length, wide, narrow):
    bins = 2 * (HALF + 1) * (2 * length // RADIX)
    parts = [wide.at[pl.ds(0, bins), :]]
    parts += [wide.at[pl.ds(bins + index * length, length), :] for index in range(2)]
    parts += [wide.at[pl.ds(bins + 2 * length, 8), :]]
    parts += [narrow.at[pl.ds(256 * index, 256), :] for index in range(2)]
    return parts + [narrow.at[pl.ds(512, 256), pl.ds(256 * index, 256)] for index in range(2)]


def passed_shapes(length):
    bins = 2 * (HALF + 1) * (2 * length // RADIX)
    return [shape((bins + 2 * length + 8, 128), F32), shape((512 + 256, length), BF16)]


def held_arrays(length):
    bins = 2 * (HALF + 1) * (2 * length // RADIX)
    held = [pltpu.VMEM((rows, 128), F32) for rows in (bins, length, length, 8)]
    held += [pltpu.VMEM((256, length), BF16)] * 2 + [pltpu.VMEM((256, 256), BF16)] * 2
    return held + [pltpu.SemaphoreType.DMA((len(held),))]


def spectrum_call(length, *operands):
    inner = 2 * length // RADIX
    return call(
        functools.partial(kernel_spectrum_kernel, length),
        passed_shapes(length),
        scratch=held_arrays(length)
        + [pltpu.VMEM((length, 128), F32), pltpu.VMEM((HALF + 1, 3 * inner, 256), BF16)],
        flops=4 << 30,
        limit=FIRST_LIMIT,
        out_specs=[ON_HBM] * 2,
    )(*operands)


def gradient_call(length, *operands):
    inner = 2 * length // RADIX
    local_rows = 128
    return call(
        functools.partial(gradient_kernel, length),
        shape((length // local_rows, local_rows // 2 + 40, 128), BF16),
        scratch=held_arrays(length)
        + [
            pltpu.VMEM((HALF + 1, 3 * inner, 256), BF16),
            pltpu.VMEM((HALF + 1, inner, 256), F32),
        ]
        + [pltpu.VMEM((length, 256), BF16)] * 2
        + [pltpu.VMEM((inner, 128), F32)],
        flops=8 << 30,
        limit=SECOND_LIMIT,
        in_specs=[ON_VMEM] + [ON_HBM] * 2 + [ON_VMEM] * 2,
    )(*operands)


def by_channels(tokens_in, grad_out, decay_rate, w_in, b_in, w_mid, w_out):
    devices = lax.axis_size("ctx")
    local_rows = tokens_in.shape[0]
    length = local_rows * devices
    matrix, twiddle = dft_tables(2 * length)
    packed = call(
        pack_kernel,
        shape((devices, local_rows, 128), BF16),
        scratch=[pltpu.VMEM(tokens_in.shape, BF16)] * 2
        + [
            pltpu.VMEM((devices, local_rows, 128), BF16),
            pltpu.SemaphoreType.DMA((PACK_PARTS, 2)),
            pltpu.SemaphoreType.DMA((PACK_PARTS,)),
        ],
        limit=58,
        in_specs=[ON_HBM] * 2,
        out_specs=ON_HBM,
    )(tokens_in, grad_out)
    signal = lax.all_to_all(packed, "ctx", split_axis=0, concat_axis=0, tiled=True)
    forward = spectrum_call(
        length, decay_rate.reshape(1, -1), w_in.reshape(1, -1), b_in.reshape(1, -1), w_mid, w_out,
        matrix, twiddle,
    )
    sent = gradient_call(length, signal.reshape(length, 128), *forward, matrix, twiddle)
    received = lax.all_to_all(sent, "ctx", split_axis=0, concat_axis=0, tiled=True)
    half, joined = call(
        sums_kernel, [shape((32, 64 * devices + 128), BF16), shape((8, 128), F32)]
    )(received)
    other = lax.ppermute(half, "ctx", [(index, index ^ 1) for index in range(devices)])
    input_grad = call(tokens_kernel, shape(tokens_in.shape, BF16), flops=1 << 26)(received)
    grad_first, grad_bias, grad_mid, grad_last = call(
        functools.partial(weights_kernel, 1.0 / math.sqrt(length)),
        [shape((1, 64), F32), shape((1, 64), F32), shape((64, 64), F32), shape(w_out.shape, F32)],
    )(joined, half, other)
    return input_grad, grad_first.reshape(64), grad_bias.reshape(64), grad_mid, grad_last


HIGHEST = lax.Precision.HIGHEST
TWO_PI = 2.0 * math.pi


def phase_angle(product, period):
    return TWO_PI / period * (product % period).astype(jnp.float32)


def frequency_rows(devices):
    row_index = jnp.arange(2 * devices, dtype=jnp.int32)
    row_block = row_index // 2
    second = row_index % 2
    paired = jnp.where(row_block == 0, devices, 2 * devices - row_block)
    return jnp.where(second == 0, row_block, paired)


def source_rows(devices):
    row_index = jnp.arange(2 * devices, dtype=jnp.int32)
    return row_index // 2 + row_index % 2 * devices


def envelope(lag_values, decay_rate, length):
    double = 2.0 * decay_rate
    geometric = 1.0 + 2.0 * jnp.exp(-double) * jnp.expm1(-double * (length - 1)) / jnp.expm1(
        -double
    )
    distance = jnp.abs(lag_values).astype(jnp.float32)[..., None]
    live_mask = (lag_values != -length).astype(jnp.float32)[..., None]
    return live_mask * lax.rsqrt(geometric) * jnp.exp(-distance * decay_rate)


def position_mlp(scaled, w_first, w_bias, w_middle, w_last):
    hidden_one = jax.nn.silu(scaled[..., None] * w_first + w_bias)
    hidden_two = jax.nn.silu(jnp.dot(hidden_one, w_middle, precision=HIGHEST))
    return jnp.dot(hidden_two, w_last, precision=HIGHEST)


def rotate(real_a, imag_a, real_b, imag_b):
    return (real_a * real_b - imag_a * imag_b, real_a * imag_b + imag_a * real_b)


def first_section(signal, columns, freq_order, local_slab, padded):
    freq_count = freq_order.shape[0]
    angles = phase_angle(freq_order[:, None] * columns[None, :], freq_count)
    real_part = jnp.einsum("fp,prc->frc", jnp.cos(angles), signal, precision=HIGHEST)
    imag_part = jnp.einsum("fp,prc->frc", -jnp.sin(angles), signal, precision=HIGHEST)
    twiddle = phase_angle(freq_order[:, None] * local_slab[None, :], padded)[:, :, None]
    return rotate(real_part, imag_part, jnp.cos(twiddle), -jnp.sin(twiddle))


def along_rows(stacked, direction):
    row_count = stacked.shape[1]
    half_width = stacked.shape[2] // 2
    positions = jnp.arange(row_count, dtype=jnp.int32)
    angles = phase_angle(positions[:, None] * positions[None, :], row_count)
    with_cos = jnp.einsum("gm,imc->igc", jnp.cos(angles), stacked, precision=HIGHEST)
    with_sin = jnp.einsum("gm,imc->igc", direction * jnp.sin(angles), stacked, precision=HIGHEST)
    real_part = with_cos[..., :half_width] - with_sin[..., half_width:]
    imag_part = with_cos[..., half_width:] + with_sin[..., :half_width]
    return (real_part, imag_part)


def last_section(stacked, out_rows, freq_order, padded):
    freq_count = freq_order.shape[0]
    half_width = stacked.shape[2] // 2
    angles = phase_angle(out_rows[:, None] * freq_order[None, :], freq_count)
    cos_table = jnp.cos(angles) / padded
    sin_table = jnp.sin(angles) / padded
    real_in = stacked[..., :half_width]
    imag_in = stacked[..., half_width:]
    leading, trailing, factor = (real_in, imag_in, -1.0)
    return jnp.einsum("pf,frc->prc", cos_table, leading, precision=HIGHEST) + factor * jnp.einsum(
        "pf,frc->prc", sin_table, trailing, precision=HIGHEST
    )


def by_frequencies(tokens_in, grad_out, decay_rate, w_in, b_in, w_mid, w_out):
    devices = lax.axis_size("ctx")
    own_index = lax.axis_index("ctx")
    tok_rows = tokens_in.shape[0]
    slab_rows = tok_rows // devices
    length = tok_rows * devices
    padded = 2 * length
    freq_order = frequency_rows(devices)
    lag_rows = source_rows(devices)
    token_cols = jnp.arange(devices, dtype=jnp.int32)
    local_slab = own_index * slab_rows + jnp.arange(slab_rows, dtype=jnp.int32)
    pair_index = jnp.arange(2, dtype=jnp.int32)
    local_freq = jnp.where(
        pair_index == 0, own_index, jnp.where(own_index == 0, devices, 2 * devices - own_index)
    )
    circular = (own_index + pair_index * devices)[:, None] * tok_rows + jnp.arange(
        tok_rows, dtype=jnp.int32
    )[None, :]
    lag_values = jnp.where(circular < length, circular, circular - padded)
    scaled = lag_values.astype(jnp.float32) / length
    weights_env = envelope(lag_values, decay_rate, length)

    def position_net(w_first, w_bias, w_middle, w_last):
        return position_mlp(scaled, w_first, w_bias, w_middle, w_last)

    position, pull_back = jax.vjp(position_net, w_in, b_in, w_mid, w_out)
    kernel = (position * weights_env).astype(jnp.bfloat16)
    tokens_mid, grads_mid, kernel_mid = (
        lax.all_to_all(tokens_in[None], "ctx", split_axis=1, concat_axis=0, tiled=True),
        lax.all_to_all(grad_out[None], "ctx", split_axis=1, concat_axis=0, tiled=True),
        lax.all_to_all(kernel, "ctx", split_axis=1, concat_axis=0, tiled=True),
    )
    token_real, token_imag = first_section(
        tokens_mid.astype(jnp.float32), token_cols, freq_order, local_slab, padded
    )
    cotan_real, cotan_imag = first_section(
        grads_mid.astype(jnp.float32), token_cols, freq_order, local_slab, padded
    )
    kern_real, kern_imag = first_section(
        kernel_mid.astype(jnp.float32), lag_rows, freq_order, local_slab, padded
    )
    kernel_stack = jnp.concatenate([kern_real, kern_imag], axis=2)
    token_stack = jnp.concatenate([token_real, token_imag], axis=2)
    cotan_stack = jnp.concatenate([cotan_real, cotan_imag], axis=2)
    token_spec, cotan_spec, kernel_spec = (
        lax.all_to_all(token_stack, "ctx", split_axis=0, concat_axis=1, tiled=True),
        lax.all_to_all(cotan_stack, "ctx", split_axis=0, concat_axis=1, tiled=True),
        lax.all_to_all(kernel_stack, "ctx", split_axis=0, concat_axis=1, tiled=True),
    )
    spec_token_real, spec_token_imag = along_rows(token_spec, -1.0)
    spec_cotan_real, spec_cotan_imag = along_rows(cotan_spec, -1.0)
    spec_kern_real, spec_kern_imag = along_rows(kernel_spec, -1.0)
    input_real = spec_kern_real * spec_cotan_real + spec_kern_imag * spec_cotan_imag
    input_imag = spec_kern_real * spec_cotan_imag - spec_kern_imag * spec_cotan_real
    lagged_real = spec_cotan_real * spec_token_real + spec_cotan_imag * spec_token_imag
    lagged_imag = spec_cotan_imag * spec_token_real - spec_cotan_real * spec_token_imag
    positions = jnp.arange(tok_rows, dtype=jnp.int32)
    back_angle = phase_angle(local_freq[:, None] * positions[None, :], padded)[:, :, None]
    back_cos = jnp.cos(back_angle)
    back_sin = jnp.sin(back_angle)

    def inverse_rows(real_part, imag_part):
        stacked = jnp.concatenate([real_part, imag_part], axis=2)
        out_real, out_imag = along_rows(stacked, 1.0)
        turned_real, turned_imag = rotate(out_real, out_imag, back_cos, back_sin)
        return jnp.concatenate([turned_real, turned_imag], axis=2)

    spread_input, spread_lagged = (
        lax.all_to_all(
            inverse_rows(input_real, input_imag), "ctx", split_axis=1, concat_axis=0, tiled=True
        ),
        lax.all_to_all(
            inverse_rows(lagged_real, lagged_imag), "ctx", split_axis=1, concat_axis=0, tiled=True
        ),
    )
    input_rows = last_section(spread_input, token_cols, freq_order, padded)
    lagged_rows = last_section(spread_lagged, lag_rows, freq_order, padded)
    input_back, lag_back = (
        lax.all_to_all(input_rows, "ctx", split_axis=0, concat_axis=1, tiled=True),
        lax.all_to_all(lagged_rows, "ctx", split_axis=0, concat_axis=1, tiled=True),
    )
    input_grad = input_back[0]
    gradients = pull_back(lag_back * weights_env)
    summed = lax.psum((gradients[0], gradients[1], gradients[2], gradients[3]), "ctx")
    loss_scale = 1.0 / math.sqrt(length)
    return (
        input_grad.astype(jnp.bfloat16),
        summed[0] * loss_scale,
        summed[1] * loss_scale,
        summed[2] * loss_scale,
        summed[3] * loss_scale,
    )


def on_device(tokens_in, grad_out, decay_rate, w_in, b_in, w_mid, w_out):
    devices = lax.axis_size("ctx")
    fits = (
        tokens_in.shape == (128, 64 * devices)
        and devices % 2 == 0
        and devices * 128 % (128 * HALF) == 0
        and w_mid.shape == (64, 64)
    )
    form = by_channels if fits else by_frequencies
    return form(tokens_in, grad_out, decay_rate, w_in, b_in, w_mid, w_out)


def solution(mesh):
    in_specs = (P(("groups", "ctx"), None), P(("groups", "ctx"), None), P(), P(), P(), P(), P())
    out_specs = (
        P(("groups", "ctx"), None),
        P("groups"),
        P("groups"),
        P("groups", None),
        P("groups", None),
    )
    return jax.shard_map(
        on_device, mesh=mesh, in_specs=in_specs, out_specs=out_specs, check_vma=False
    )
```
